128 devices in a mesh: frames: 2 (over core), prow: 8 (over z_lo, x), pcol: 8 (over y, z_hi).
Axes of the slice: x: 4, y: 4, z: 4 (z_hi: 2, z_lo: 2; z = z_hi * 2 + z_lo), core: 2. Of those that a mesh axis runs over, the one named last changes fastest.
Arguments:
- poses: bfloat16 [262144, 256], P(('frames', 'prow', 'pcol')), may hold values from -6 to 6
- codebook: bfloat16 [32, 256], replicated, may hold values from -4 to 4
- offsets: bfloat16 [32, 256], replicated, may hold values from -4 to 4
- confidence: float32 [262144], P(('frames', 'prow', 'pcol')), may hold values from 0.2 to 1
- code_ids: int32 [262144], P(('frames', 'prow', 'pcol')), may hold values from 0 to 31
- creature_ids: int32 [262144], P(('frames', 'prow', 'pcol')), may hold values from 0 to 31
- hess_raw: float32 [8, 8, 128, 8, 8, 128], P(None, 'prow', None, None, 'pcol'), may hold values from -1 to 1, as said below
- pattern: int32 [64, 64], replicated, may hold values from 0 to 1, as said below
- membership: int32 [2, 2], replicated, may hold values from 0 to 63, as said below
Outputs:
- factor_state: float32 [8, 8, 128, 8, 8, 128], P(None, 'prow', None, None, 'pcol')
- reduced_grad: float32 [8, 8, 128], P(None, 'prow')
The draws below stay inside these ranges and needn't reach their ends.
Inputs may be any that keep to these rules, and one draw needn't show every extreme that they name: As an 8192 x 8192 matrix hess_raw is symmetric. pattern is symmetric with ones on its diagonal. Within each row of membership all pattern entries are one, and for every block row i outside a supernode, pattern[i, p] is the same for all block columns p of that supernode. The 4 entries of membership are distinct block indices.
All inputs are finite; a program needn't handle non-finite values.
Results may differ from the reference program's by a relative error of at most 0.0003.
Values sent between devices are 32-bit elements; how exact they have to be, the bound alone decides.
A program may use at most 64 MiB of HBM per device.

```python
import math
import jax
import jax.numpy as jnp
from jax import lax

W = 256
NPAN = 8192
BS = 128
NCRE = 32
SN = 2
CODES = 32
NB = 64
STEPS = 4
FRAMES = 262144
N_PROW = 8
N_PCOL = 8


def draw_hess_raw(key, part):
    values = jax.random.uniform(key, (NPAN, NPAN), jnp.float32, -1.0, 1.0)
    row_ids = jnp.arange(NPAN)[:, None]
    col_ids = jnp.arange(NPAN)[None, :]
    symmetric = jnp.where(row_ids <= col_ids, values, values.T)
    return symmetric.reshape(NB // N_PROW, N_PROW, BS, NB // N_PCOL, N_PCOL, BS)


def chosen_members(key):
    base = jax.random.fold_in(key, 11)
    inner = jax.random.permutation(base, NB - 2)[:2 * SN - 2].astype(jnp.int32) + 1
    chosen = jnp.concatenate([jnp.array([0, NB - 1], jnp.int32), inner])
    mixing = jax.random.permutation(jax.random.fold_in(base, 7), 2 * SN)
    return chosen[mixing].reshape(2, SN).astype(jnp.int32)


def draw_pattern(key, part):
    members = chosen_members(key)
    coins = jax.random.randint(jax.random.fold_in(key, 12), (NB, NB), 0, 2)
    row_ids = jnp.arange(NB)[:, None]
    col_ids = jnp.arange(NB)[None, :]
    symmetric = jnp.where(row_ids < col_ids, coins, coins.T)
    leader = jnp.arange(NB, dtype=jnp.int32)
    leader = leader.at[members[0]].set(members[0, 0])
    leader = leader.at[members[1]].set(members[1, 0])
    shared = symmetric[leader][:, leader]
    shared = jnp.where(leader[:, None] == leader[None, :], 1, shared)
    return shared.astype(jnp.int32)


def draw_membership(key, part):
    return chosen_members(key)


def plant(values, own_key, smallest, top_value):
    spot = [jax.random.randint(jax.random.fold_in(own_key, axis), (), 0, length) for axis, length in enumerate(values.shape)]
    main_axis = values.shape.index(max(values.shape))
    next_to = spot[:main_axis] + [(spot[main_axis] + 1) % values.shape[main_axis]] + spot[main_axis + 1:]
    return values.at[tuple(spot)].set(smallest).at[tuple(next_to)].set(top_value)


def block_levels(own_key, dims, split, least, largest):
    factor_of = 1.0
    for dim, blocks in split:
        draws = jax.random.uniform(jax.random.fold_in(jax.random.fold_in(own_key, 6), dim), (blocks,), jnp.float32, least / len(split), largest / len(split))
        factor_of = factor_of * jnp.repeat(jnp.exp(draws), dims[dim] // blocks).reshape((-1,) + (1,) * (len(dims) - 1 - dim))
    return factor_of


def normal_values(stream_key, dims, width, reach, cuts=(), kind=jnp.bfloat16):
    result = width * jax.random.normal(stream_key, dims, jnp.float32)
    if cuts:
        result = result * block_levels(stream_key, dims, cuts, -0.22, 0.18)
    return jnp.clip(result, -reach, reach).astype(kind)


def setup_inputs(seed: int = 0) -> dict:
    keys = jax.random.split(jax.random.key(seed), 10)
    poses = normal_values(keys[0], (FRAMES, W), 1.0, 6.0, ((0, 128),))
    codebook = normal_values(keys[1], (CODES, W), 0.5, 4.0)
    offsets = normal_values(keys[2], (NCRE, W), 0.5, 4.0)
    confidence = jnp.clip(jnp.exp(math.log(1.0) - 1.609438 * jax.random.uniform(keys[3], (FRAMES,), jnp.float32) ** block_levels(keys[3], (FRAMES,), ((0, 128),), -0.2, 0.2)), 0.2, 1.0)
    code_ids = plant(jax.random.randint(keys[4], (FRAMES,), 0, CODES), jax.random.fold_in(keys[4], 1), 0, CODES - 1).astype(jnp.int32)
    creature_ids = plant(jax.random.randint(keys[5], (FRAMES,), 0, NCRE), jax.random.fold_in(keys[5], 1), 0, NCRE - 1).astype(jnp.int32)
    hess_raw = draw_hess_raw(jax.random.fold_in(keys[9], 71), 0)
    pattern = draw_pattern(jax.random.fold_in(keys[9], 71), 0)
    membership = draw_membership(jax.random.fold_in(keys[9], 71), 0)
    return dict(poses=poses, codebook=codebook, offsets=offsets, confidence=confidence, code_ids=code_ids, creature_ids=creature_ids, hess_raw=hess_raw, pattern=pattern, membership=membership)


precise = lax.Precision.HIGHEST

def solve_rows(factor_blk, column):
    blocksize = factor_blk.shape[0]
    block_count = column.shape[0]
    right_side = jnp.transpose(column, (2, 0, 1)).reshape(blocksize, block_count * blocksize)
    solution = jax.scipy.linalg.solve_triangular(factor_blk, right_side, lower=True)
    return jnp.transpose(solution.reshape(blocksize, block_count, blocksize), (1, 2, 0))

def reference(poses, codebook, offsets, confidence, code_ids, creature_ids, hess_raw, pattern, membership):
    code_table = (code_ids[None, :] == jnp.arange(CODES, dtype=jnp.int32)[:, None]).astype(jnp.float32)
    kind_table = (creature_ids[None, :] == jnp.arange(NCRE, dtype=jnp.int32)[:, None]).astype(jnp.float32)
    predicted = jnp.einsum('cf,cw->fw', code_table, codebook.astype(jnp.float32), precision=precise)
    predicted = predicted + jnp.einsum('cf,cw->fw', kind_table, offsets.astype(jnp.float32), precision=precise)
    residual = confidence[:, None] * (poses.astype(jnp.float32) - predicted)
    gradient = jnp.einsum('cf,fw->cw', code_table, residual, precision=precise) / math.sqrt(FRAMES / CODES)
    gradient = gradient.reshape(NB, BS)
    shift = 2.5 * math.sqrt(NPAN)
    mask_four = pattern.astype(jnp.float32)[:, None, :, None]
    blocks = hess_raw.reshape(NB, BS, NB, BS) * mask_four
    diagonal = jnp.arange(NPAN, dtype=jnp.int32)
    blocks = blocks.reshape(NPAN, NPAN).at[diagonal, diagonal].add(shift).reshape(NB, BS, NB, BS)
    order = membership.reshape(-1)
    indices = jnp.arange(NB, dtype=jnp.int32)

    def eliminate(position, state_pair):
        blocks, gradient = state_pair
        pivot = order[position]
        diag_blk = lax.dynamic_index_in_dim(lax.dynamic_index_in_dim(blocks, pivot, 0, False), pivot, 1, False)
        factor_blk = jnp.linalg.cholesky(diag_blk)
        solved = jax.scipy.linalg.solve_triangular(factor_blk, lax.dynamic_index_in_dim(gradient, pivot, 0, False), lower=True)
        column = lax.dynamic_index_in_dim(blocks, pivot, 2, False) * (indices != pivot).astype(jnp.float32)[:, None, None]
        panel_rows = solve_rows(factor_blk, column)
        blocks = blocks - mask_four * jnp.einsum('ixk,jyk->ixjy', panel_rows, panel_rows, precision=precise)
        gradient = gradient - jnp.einsum('ixk,k->ix', panel_rows, solved, precision=precise)
        gradient = lax.dynamic_update_index_in_dim(gradient, solved, pivot, 0)
        blocks = lax.dynamic_update_index_in_dim(blocks, jnp.zeros((BS, NB, BS), jnp.float32), pivot, 0)
        filled = lax.dynamic_update_index_in_dim(panel_rows, factor_blk, pivot, 0)
        blocks = lax.dynamic_update_index_in_dim(blocks, filled, pivot, 2)
        return (blocks, gradient)
    blocks, gradient = lax.fori_loop(0, STEPS, eliminate, (blocks, gradient))
    factor_state = blocks.reshape(NB // N_PROW, N_PROW, BS, NB // N_PCOL, N_PCOL, BS)
    reduced_grad = gradient.reshape(NB // N_PROW, N_PROW, BS)
    return (factor_state, reduced_grad)
```

```python
import math

import jax
import jax.numpy as jnp
from jax import lax
from jax.experimental import pallas as pl
from jax.experimental.pallas import tpu as pltpu
from jax.sharding import PartitionSpec as P

NPAN = 8192
BS = 128
STEPS = 4
SHIFT = 2.5 * math.sqrt(NPAN)
PAIRS = [(k, m) for k in range(STEPS) for m in range(k + 1)]
NQ = len(PAIRS)
MESH = pl.DeviceIdType.MESH
precise = lax.Precision.HIGHEST
f32 = jnp.float32
bf16 = jnp.bfloat16
NT = (((1,), (1,)), ((), ()))


def loop(lo, hi, fn):
    def body(d, carry):
        fn(d)
        return carry

    lax.fori_loop(lo, hi, body, 0)


def exchange_kernel(
    mem, scand, ccand, pg,
    s_out, raw_r, raw_c, g_out,
    s1r, s1, s2r, par, mine, g1r, g1, g2r, g2, g3r,
    snd_s1, rcv_s1, snd_s2, rcv_s2, snd_s3, rcv_s3, snd_sx, rcv_sx,
    snd_a, rcv_a, snd_r, rcv_r, snd_t, rcv_t, snd_rx, rcv_rx, snd_cx, rcv_cx,
    snd_g1, rcv_g1, snd_g2, rcv_g2, snd_g3, rcv_g3, snd_g4, rcv_g4,
):
    f = lax.axis_index("frames")
    r = lax.axis_index("prow")
    c = lax.axis_index("pcol")

    def copy(src, dst, snd, rcv, f_to, r_to, c_to):
        return pltpu.make_async_remote_copy(
            src_ref=src, dst_ref=dst, send_sem=snd, recv_sem=rcv,
            device_id=(f_to, r_to, c_to), device_id_type=MESH,
        )

    def col_peer(d):
        return lax.rem(c + d, 8)

    def row_peer(d):
        return lax.rem(r + d, 8)

    def s1_copy(src, dst_slot, peer, sem):
        return copy(scand.at[src], s1r.at[dst_slot], snd_s1.at[peer], rcv_s1.at[sem], f, r, peer)

    def s1_send(d):
        peer = col_peer(d)
        s1_copy(peer + 8 * f, c, peer, c).start()

    loop(1, 8, s1_send)
    s1r[c] = scand[c + 8 * f]

    def g1_send(d):
        peer = col_peer(d)
        copy(pg.at[peer], g1r.at[c], snd_g1.at[peer], rcv_g1.at[c], f, r, peer).start()

    loop(1, 8, g1_send)
    g1r[c] = pg[c]

    def a_send(d):
        peer = col_peer(d)
        copy(ccand.at[peer, f], par.at[c], snd_a.at[peer], rcv_a.at[c], f, r, peer).start()

    loop(1, 8, a_send)
    par[c] = ccand[c, f]

    def s1_wait(d):
        peer = col_peer(d)
        s1_copy(peer + 8 * f, peer, peer, peer).wait()

    loop(1, 8, s1_wait)
    for q, (k, m) in enumerate(PAIRS):
        s1[q] = s1r[lax.rem(mem[m], 8), q]

    def s2_send(d):
        peer = row_peer(d)
        copy(s1, s2r.at[r], snd_s2.at[peer], rcv_s2.at[r], f, peer, c).start()

    loop(1, 8, s2_send)
    s2r[r] = s1[...]

    def g1_wait(d):
        peer = col_peer(d)
        copy(pg.at[peer], g1r.at[peer], snd_g1.at[peer], rcv_g1.at[peer], f, r, peer).wait()

    loop(1, 8, g1_wait)
    g1[...] = jnp.sum(g1r[...], axis=0)

    def g2_send(d):
        peer = row_peer(d)
        copy(g1, g2r.at[r], snd_g2.at[peer], rcv_g2.at[r], f, peer, c).start()

    loop(1, 8, g2_send)
    g2r[r] = g1[...]

    def s2_wait(d):
        peer = row_peer(d)
        copy(s1, s2r.at[peer], snd_s2.at[peer], rcv_s2.at[peer], f, peer, c).wait()

    loop(1, 8, s2_wait)
    here = c + 8 * f
    for q, (k, m) in enumerate(PAIRS):
        s_out[here, q] = s2r[lax.rem(mem[k], 8), q]

    def s3_send(d):
        peer = col_peer(d)
        copy(s_out.at[here], s_out.at[here], snd_s3.at[peer], rcv_s3.at[c], f, r, peer).start()

    loop(1, 8, s3_send)

    def sx_copy(slot, sem):
        return copy(s_out.at[slot], s_out.at[slot], snd_sx.at[sem], rcv_sx.at[sem], 1 - f, r, c)

    sx_copy(here, c).start()

    def s3_wait(d):
        peer = col_peer(d)
        slot = peer + 8 * f
        copy(s_out.at[slot], s_out.at[slot], snd_s3.at[peer], rcv_s3.at[peer], f, r, peer).wait_recv()
        sx_copy(slot, peer).start()

    loop(1, 8, s3_wait)

    def g2_wait(d):
        peer = row_peer(d)
        copy(g1, g2r.at[peer], snd_g2.at[peer], rcv_g2.at[peer], f, peer, c).wait()

    loop(1, 8, g2_wait)
    g2[...] = jnp.sum(g2r[...], axis=0)
    g3 = copy(g2, g3r, snd_g3, rcv_g3, 1 - f, r, c)
    g3.start()

    def a_wait(d):
        peer = col_peer(d)
        copy(ccand.at[peer, f], par.at[peer], snd_a.at[peer], rcv_a.at[peer], f, r, peer).wait()

    loop(1, 8, a_wait)
    for k in range(STEPS):
        mine[k] = par[lax.rem(mem[k], 8), k]

    def r_send(d):
        peer = col_peer(d)
        copy(mine, raw_r.at[c, f], snd_r.at[peer], rcv_r.at[c], f, r, peer).start()

    loop(1, 8, r_send)
    raw_r[c, f] = mine[...]

    def t_send(d):
        peer = row_peer(d)

        @pl.when(jnp.logical_or(peer != r, c != r))
        def _():
            copy(mine, raw_c.at[c, f], snd_t.at[peer], rcv_t.at[c], f, peer, r).start()

    loop(0, 8, t_send)

    @pl.when(r == c)
    def _():
        raw_c[c, f] = mine[...]

    g3.wait()
    g_out[c] = g2[...] + g3r[...]

    def g4_send(d):
        peer = col_peer(d)
        copy(g_out.at[c], g_out.at[c], snd_g4.at[peer], rcv_g4.at[c], f, r, peer).start()

    loop(1, 8, g4_send)

    def rx_copy(slot):
        return copy(raw_r.at[slot, f], raw_r.at[slot, f], snd_rx.at[slot], rcv_rx.at[slot], 1 - f, r, c)

    def cx_copy(slot):
        return copy(raw_c.at[slot, f], raw_c.at[slot, f], snd_cx.at[slot], rcv_cx.at[slot], 1 - f, r, c)

    rx_copy(c).start()

    def r_wait(d):
        peer = col_peer(d)
        copy(mine, raw_r.at[peer, f], snd_r.at[peer], rcv_r.at[peer], f, r, peer).wait_recv()
        rx_copy(peer).start()

    loop(1, 8, r_wait)

    def t_wait(b):
        @pl.when(jnp.logical_or(b != c, r != c))
        def _():
            copy(mine, raw_c.at[b, f], snd_t.at[b], rcv_t.at[b], f, c, b).wait_recv()

        cx_copy(b).start()

    loop(0, 8, t_wait)

    def g4_wait(d):
        peer = col_peer(d)
        copy(g_out.at[peer], g_out.at[peer], snd_g4.at[peer], rcv_g4.at[peer], f, r, peer).wait_recv()

    loop(1, 8, g4_wait)

    def x_wait(slot):
        other = 1 - f
        copy(s_out.at[slot + 8 * other], s_out.at[slot + 8 * other], snd_sx.at[slot], rcv_sx.at[slot], other, r, c).wait_recv()
        copy(raw_r.at[slot, other], raw_r.at[slot, other], snd_rx.at[slot], rcv_rx.at[slot], other, r, c).wait_recv()
        copy(raw_c.at[slot, other], raw_c.at[slot, other], snd_cx.at[slot], rcv_cx.at[slot], other, r, c).wait_recv()
        sx_copy(slot + 8 * f, slot).wait_send()
        rx_copy(slot).wait_send()
        cx_copy(slot).wait_send()

    loop(0, 8, x_wait)

    def tail(d):
        peer = col_peer(d)
        copy(s_out.at[here], s_out.at[here], snd_s3.at[peer], rcv_s3.at[c], f, r, peer).wait_send()
        copy(mine, raw_r.at[c, f], snd_r.at[peer], rcv_r.at[c], f, r, peer).wait_send()
        copy(g_out.at[c], g_out.at[c], snd_g4.at[peer], rcv_g4.at[c], f, r, peer).wait_send()

    loop(1, 8, tail)

    def t_tail(d):
        peer = row_peer(d)

        @pl.when(jnp.logical_or(peer != r, c != r))
        def _():
            copy(mine, raw_c.at[c, f], snd_t.at[peer], rcv_t.at[c], f, peer, r).wait_send()

    loop(0, 8, t_tail)


def exchange(mem, scand, ccand, pg):
    vm = pl.BlockSpec(memory_space=pltpu.VMEM)
    sem = pltpu.SemaphoreType.DMA
    return pl.pallas_call(
        exchange_kernel,
        out_shape=(
            jax.ShapeDtypeStruct((16, NQ, 8, BS), f32),
            jax.ShapeDtypeStruct((8, 2, STEPS, 64, BS), f32),
            jax.ShapeDtypeStruct((8, 2, STEPS, 64, BS), f32),
            jax.ShapeDtypeStruct((8, 8, BS), f32),
        ),
        in_specs=[pl.BlockSpec(memory_space=pltpu.SMEM), vm, vm, vm],
        out_specs=(vm, vm, vm, vm),
        scratch_shapes=[
            pltpu.VMEM((8, NQ, 8, BS), f32),
            pltpu.VMEM((NQ, 8, BS), f32),
            pltpu.VMEM((8, NQ, 8, BS), f32),
            pltpu.VMEM((8, STEPS, 64, BS), f32),
            pltpu.VMEM((STEPS, 64, BS), f32),
            pltpu.VMEM((8, 8, BS), f32),
            pltpu.VMEM((8, BS), f32),
            pltpu.VMEM((8, 8, BS), f32),
            pltpu.VMEM((8, BS), f32),
            pltpu.VMEM((8, BS), f32),
        ]
        + [sem((8,))] * 22
        + [sem, sem, sem((8,)), sem((8,))],
        compiler_params=pltpu.CompilerParams(has_side_effects=True, vmem_limit_bytes=40 << 20),
        name="exchange",
    )(mem, scand, ccand, pg)


def spread(row):
    return jnp.broadcast_to(row, (8, BS))


def factor_block(block):
    groups = BS // 8
    row_ids = lax.broadcasted_iota(jnp.int32, (8, BS), 0)
    lane_ids = lax.broadcasted_iota(jnp.int32, (8, BS), 1)
    upper = [block[8 * g : 8 * g + 8, :] for g in range(groups)]
    inv = [jnp.where(lane_ids == row_ids + 8 * g, 1.0, 0.0).astype(f32) for g in range(groups)]
    for g in range(groups):
        k = 8 * g
        v, w = upper[g], inv[g]
        cols = [jnp.broadcast_to(v[:, k + j : k + j + 1], (8, BS)) for j in range(8)]
        rows_v, rows_w, coef = [], [], []
        for j in range(8):
            pivot = spread(cols[j][j : j + 1, :])
            recip = 1.0 / pivot
            rv = spread(v[j : j + 1, :]) * recip
            rw = spread(w[j : j + 1, :]) * recip
            rows_v.append(rv)
            rows_w.append(rw)
            below = jnp.where(row_ids > j, cols[j], 0.0)
            coef.append([None] * 8)
            for t in range(j + 1, 8):
                coef[j][t] = spread(cols[t][j : j + 1, :]) * recip
                cols[t] = cols[t] - below * coef[j][t]
            v = v - below * rv
            w = w - below * rw
        upper[g], inv[g] = v, w
        for h in range(g + 1, groups):
            v, w = upper[h], inv[h]
            cols = [jnp.broadcast_to(v[:, k + j : k + j + 1], (8, BS)) for j in range(8)]
            for j in range(8):
                for t in range(j + 1, 8):
                    cols[t] = cols[t] - cols[j] * coef[j][t]
                v = v - cols[j] * rows_v[j]
                w = w - cols[j] * rows_w[j]
            upper[h], inv[h] = v, w
    full = jnp.concatenate(upper, axis=0)
    inverse = jnp.concatenate(inv, axis=0)
    rr = lax.broadcasted_iota(jnp.int32, (BS, BS), 0)
    cc = lax.broadcasted_iota(jnp.int32, (BS, BS), 1)
    pivots = jnp.sum(jnp.where(rr == cc, full, 0.0), axis=1, keepdims=True)
    scale = 1.0 / jnp.sqrt(pivots)
    return jnp.where(cc >= rr, full * scale, 0.0), inverse * scale


def dot_nt(a, b):
    return lax.dot_general(a, b, NT, precision=precise, preferred_element_type=f32)


def dot_nn(a, b):
    return lax.dot_general(a, b, (((1,), (0,)), ((), ())), precision=precise, preferred_element_type=f32)


def factor_kernel(mem, pat, s_ref, low_ref, inv_ref):
    rr = lax.broadcasted_iota(jnp.int32, (BS, BS), 0)
    cc = lax.broadcasted_iota(jnp.int32, (BS, BS), 1)
    low_ref[...] = jnp.zeros_like(low_ref)
    inv_ref[...] = jnp.zeros_like(inv_ref)

    def raw(k, m):
        q = PAIRS.index((k, m))
        keep = pat[mem[k], mem[m]].astype(f32)
        value = s_ref[:, q].reshape(BS, BS) * keep
        return value, keep

    for k in range(STEPS):
        lows = []
        for m in range(k):
            value, keep = raw(k, m)
            for t in range(m):
                value = value - keep * dot_nt(lows[t], low_ref[m, :, BS * t : BS * t + BS])
            lows.append(dot_nt(value, inv_ref[BS * m : BS * m + BS, BS * m : BS * m + BS]))
            low_ref[k, :, BS * m : BS * m + BS] = lows[m]
        value, _ = raw(k, k)
        value = value + jnp.where(rr == cc, SHIFT, 0.0)
        for t in range(k):
            value = value - dot_nt(lows[t], lows[t])
        upper, inverse = factor_block(value)
        low_ref[k, :, BS * k : BS * k + BS] = upper.T
        inv_ref[BS * k : BS * k + BS, BS * k : BS * k + BS] = inverse
        if k:
            row = jnp.concatenate(lows, axis=1)
            above = inv_ref[0 : BS * k, 0 : BS * k]
            inv_ref[BS * k : BS * k + BS, 0 : BS * k] = -dot_nn(inverse, dot_nn(row, above))


def factor(mem, pat, s):
    vm = pl.BlockSpec(memory_space=pltpu.VMEM)
    sm = pl.BlockSpec(memory_space=pltpu.SMEM)
    return pl.pallas_call(
        factor_kernel,
        out_shape=(
            jax.ShapeDtypeStruct((STEPS, BS, STEPS * BS), f32),
            jax.ShapeDtypeStruct((STEPS * BS, STEPS * BS), f32),
        ),
        in_specs=[sm, sm, vm],
        out_specs=(vm, vm),
        compiler_params=pltpu.CompilerParams(vmem_limit_bytes=40 << 20),
        name="factor",
    )(mem, pat, s)


def split(x):
    hi = x.astype(bf16)
    return hi, (x - hi.astype(f32)).astype(bf16)


def dot3(a, b):
    (ah, al), (bh, bl) = a, b
    d = lambda x, y: lax.dot_general(x, y, NT, preferred_element_type=f32)
    return d(ah, bh) + (d(ah, bl) + d(al, bh))


def update_kernel(
    where, mem, pat, low_ref, inv_ref, raw_r, raw_c, g_ref, hess, out, grad_out,
    blocks, xr, xr_hi, xr_lo, xc_hi, xc_lo, wh, wl, in_sem, out_sem,
):
    r, c = where[0], where[1]
    half = SNW = 2 * BS

    def load(b):
        return pltpu.make_async_copy(hess.at[:, :, b, :, :], blocks.at[b], in_sem.at[b])

    for b in range(8):
        load(b).start()

    h, l = split(inv_ref[...])
    wh[...] = h
    wl[...] = l
    w11 = (wh[0:SNW, 0:SNW], wl[0:SNW, 0:SNW])
    w21 = (wh[SNW:, 0:SNW], wl[SNW:, 0:SNW])
    w22 = (wh[SNW:, SNW:], wl[SNW:, SNW:])

    def keeps(i):
        pivot = i == mem[0]
        for k in range(1, STEPS):
            pivot = jnp.logical_or(pivot, i == mem[k])
        z = jnp.where(pivot, 0.0, 1.0).astype(f32)
        return z * pat[i, mem[0]].astype(f32), z * pat[i, mem[2]].astype(f32), z

    def panel(raw, base, store):
        for a in range(8):
            m1, m2, _ = keeps(8 * a + base)
            one = jnp.concatenate([raw[a, :, k].reshape(BS, BS) for k in (0, 1)], axis=1) * m1
            two = jnp.concatenate([raw[a, :, k].reshape(BS, BS) for k in (2, 3)], axis=1)
            one = split(one)
            x1 = dot3(one, w11)
            x2 = m2 * (dot3(one, w21) + dot3(split(two), w22))
            store(a, x1, x2)

    def store_r(a, x1, x2):
        rows = slice(BS * a, BS * a + BS)
        for lo, x in ((0, x1), (SNW, x2)):
            xr[rows, lo : lo + SNW] = x
            h, l = split(x)
            xr_hi[rows, lo : lo + SNW] = h
            xr_lo[rows, lo : lo + SNW] = l

    def store_c(a, x1, x2):
        rows = slice(BS * a, BS * a + BS)
        for lo, x in ((0, x1), (SNW, x2)):
            h, l = split(x)
            xc_hi[rows, lo : lo + SNW] = h
            xc_lo[rows, lo : lo + SNW] = l

    panel(raw_r, r, store_r)
    panel(raw_c, c, store_c)

    gp = jnp.concatenate(
        [g_ref[mem[k] // 8, pl.ds(lax.rem(mem[k], 8), 1), :] for k in range(STEPS)], axis=1
    )
    gp = jnp.broadcast_to(gp, (16, STEPS * BS))
    y = dot3(split(gp), (wh[...], wl[...]))
    dec = dot3(split(y), (xr_hi[...], xr_lo[...]))
    for a in range(8):
        i = 8 * a + r
        val = g_ref[a, pl.ds(r, 1), :] - dec[0:1, BS * a : BS * a + BS]
        for k in range(STEPS):
            val = jnp.where(i == mem[k], y[0:1, BS * k : BS * k + BS], val)
        grad_out[a : a + 1, :] = val

    rr = lax.broadcasted_iota(jnp.int32, (BS, BS), 0)
    cc = lax.broadcasted_iota(jnp.int32, (BS, BS), 1)
    shift = jnp.where(rr == cc, SHIFT, 0.0)
    xr_pair = (xr_hi[...], xr_lo[...])
    for bp in range(4):
        cols = slice(SNW * bp, SNW * bp + SNW)
        upd = dot3(xr_pair, (xc_hi[cols, :], xc_lo[cols, :]))
        for half in range(2):
            b = 2 * bp + half
            j = 8 * b + c
            load(b).wait()
            for a in range(8):
                i = 8 * a + r
                _, _, z = keeps(i)
                keep = z * pat[i, j].astype(f32)
                on = jnp.where(i == j, 1.0, 0.0).astype(f32) * z
                sub = upd[BS * a : BS * a + BS, BS * half : BS * half + BS]
                old = blocks[b, a].reshape(BS, BS)
                blocks[b, a] = (keep * (old - sub) + on * shift).reshape(BS, 1, BS)
            for k in range(STEPS):
                @pl.when(j == mem[k])
                def _():
                    for a in range(8):
                        blocks[b, a] = xr[BS * a : BS * a + BS, BS * k : BS * k + BS].reshape(BS, 1, BS)

                    @pl.when(lax.rem(mem[k], 8) == r)
                    def _():
                        blocks[b, mem[k] // 8] = low_ref[k, :, BS * k : BS * k + BS].reshape(BS, 1, BS)
            pltpu.make_async_copy(blocks.at[b], out.at[:, :, b, :, :], out_sem.at[b]).start()
    for b in range(8):
        pltpu.make_async_copy(blocks.at[b], out.at[:, :, b, :, :], out_sem.at[b]).wait()


def update(where, mem, pat, low, inv, raw_r, raw_c, g, hess):
    vm = pl.BlockSpec(memory_space=pltpu.VMEM)
    sm = pl.BlockSpec(memory_space=pltpu.SMEM)
    anywhere = pl.BlockSpec(memory_space=pl.ANY)
    wide = STEPS * BS
    return pl.pallas_call(
        update_kernel,
        out_shape=(
            jax.ShapeDtypeStruct(hess.shape, f32),
            jax.ShapeDtypeStruct((8, BS), f32),
        ),
        in_specs=[sm, sm, sm, vm, vm, vm, vm, vm, anywhere],
        out_specs=(anywhere, vm),
        scratch_shapes=[
            pltpu.VMEM((8, 8, BS, 1, BS), f32),
            pltpu.VMEM((1024, wide), f32),
            pltpu.VMEM((1024, wide), bf16),
            pltpu.VMEM((1024, wide), bf16),
            pltpu.VMEM((1024, wide), bf16),
            pltpu.VMEM((1024, wide), bf16),
            pltpu.VMEM((wide, wide), bf16),
            pltpu.VMEM((wide, wide), bf16),
            pltpu.SemaphoreType.DMA((8,)),
            pltpu.SemaphoreType.DMA((8,)),
        ],
        compiler_params=pltpu.CompilerParams(vmem_limit_bytes=48 << 20),
        name="update",
    )(where, mem, pat, low, inv, raw_r, raw_c, g, hess)


def shards(
    poses, codebook, offsets, confidence, code_ids, creature_ids, hess_raw, pattern, membership
):
    frame_total = poses.shape[0] * 128
    code_count = codebook.shape[0]
    kind_count = offsets.shape[0]
    mem = membership.reshape(-1)
    code_table = (code_ids[None, :] == jnp.arange(code_count, dtype=jnp.int32)[:, None]).astype(f32)
    kind_table = (creature_ids[None, :] == jnp.arange(kind_count, dtype=jnp.int32)[:, None]).astype(f32)
    predicted = jnp.einsum("cf,cw->fw", code_table, codebook.astype(f32), precision=precise)
    predicted = predicted + jnp.einsum("cf,cw->fw", kind_table, offsets.astype(f32), precision=precise)
    residual = confidence[:, None] * (poses.astype(f32) - predicted)
    pg = jnp.einsum("cf,fw->cw", code_table, residual, precision=precise) / math.sqrt(frame_total / code_count)
    pg = pg.reshape(8, 8, BS)

    hess = hess_raw.reshape(8, BS, 8, BS)
    slot = mem // 8
    ccand = jnp.stack([lax.dynamic_index_in_dim(hess, slot[k], 2, False) for k in range(STEPS)], axis=1)
    ccand = ccand.reshape(8, STEPS, 2, 64, BS).transpose(0, 2, 1, 3, 4)
    scand = jnp.stack(
        [
            lax.dynamic_slice(hess, (slot[k], 0, slot[m], 0), (1, BS, 1, BS)).reshape(16, 8, BS)
            for k, m in PAIRS
        ],
        axis=1,
    )
    s, raw_r, raw_c, g = exchange(mem, scand, ccand, pg)
    low, inv = factor(mem, pattern, s)
    where = jnp.stack([lax.axis_index("prow"), lax.axis_index("pcol")]).astype(jnp.int32)
    state, grad = update(
        where, mem, pattern, low, inv, raw_r, raw_c, g, hess_raw.reshape(8, BS, 8, 1, BS)
    )
    return state.reshape(hess_raw.shape), grad.reshape(8, 1, BS)


def solution(mesh):
    return jax.shard_map(
        shards,
        mesh=mesh,
        in_specs=(
            P(("frames", "prow", "pcol"), None),
            P(),
            P(),
            P(("frames", "prow", "pcol")),
            P(("frames", "prow", "pcol")),
            P(("frames", "prow", "pcol")),
            P(None, "prow", None, None, "pcol", None),
            P(),
            P(),
        ),
        out_specs=(P(None, "prow", None, None, "pcol", None), P(None, "prow", None)),
        check_vma=False,
    )
```

```python
import math

import jax
import jax.numpy as jnp
from jax import lax
from jax.experimental import pallas as pl
from jax.experimental.pallas import tpu as pltpu
from jax.sharding import PartitionSpec as P

NPAN = 8192
BS = 128
STEPS = 4
FRAMES = 262144
CODES = 32
SHIFT = 2.5 * math.sqrt(NPAN)
PAIRS = [(k, m) for k in range(STEPS) for m in range(k + 1)]
NQ = len(PAIRS)
CHUNKS = ((0, 3), (3, 7))
WIDE = STEPS * BS
MESH = pl.DeviceIdType.MESH
precise = lax.Precision.HIGHEST
f32 = jnp.float32
bf16 = jnp.bfloat16
NT = (((1,), (1,)), ((), ()))
NN = (((1,), (0,)), ((), ()))


def loop(lo, hi, fn):
    def body(d, carry):
        fn(d)
        return carry

    lax.fori_loop(lo, hi, body, 0)


def split(x):
    hi = x.astype(bf16)
    return hi, (x - hi.astype(f32)).astype(bf16)


def dot3(a, b):
    (ah, al), (bh, bl) = a, b
    d = lambda x, y: lax.dot_general(x, y, NT, preferred_element_type=f32)
    return d(ah, bh) + (d(ah, bl) + d(al, bh))


def member(mem, k):
    return mem[k // 2, k % 2]


VM = pl.BlockSpec(memory_space=pltpu.VMEM)
SM = pl.BlockSpec(memory_space=pltpu.SMEM)
ANY = pl.BlockSpec(memory_space=pl.ANY)


def prepare_kernel(mem, hess, poses, codebook, offsets, conf, codes, kinds, scand, ccand, pg, sem):
    f = lax.axis_index("frames")
    slot = [member(mem, k) // 8 for k in range(STEPS)]
    copies = [
        pltpu.make_async_copy(hess.at[slot[k], :, slot[m], 0, :], scand.at[q], sem.at[q])
        for q, (k, m) in enumerate(PAIRS)
    ]
    for copy in copies:
        copy.start()
    by_col = [
        pltpu.make_async_copy(hess.at[:, :, slot[k], 0, :], ccand.at[:, k], sem.at[NQ + k])
        for k in range(2)
    ]
    by_row = [
        pltpu.make_async_copy(hess.at[slot[2 + k], :, b, 0, :], ccand.at[b, k], sem.at[NQ + 2 + 8 * k + b])
        for k in range(2)
        for b in range(8)
    ]

    @pl.when(f == 0)
    def _():
        for copy in by_col:
            copy.start()

    @pl.when(f == 1)
    def _():
        for copy in by_row:
            copy.start()

    ids = lax.broadcasted_iota(jnp.int32, (CODES, BS), 0)
    weights, marks = [], []
    for s in range(16):
        weights.append(jnp.where(codes[s : s + 1, :] == ids, conf[s : s + 1, :], 0.0))
        marks.append(jnp.where(kinds[s : s + 1, :] == ids, 1.0, 0.0).astype(bf16))
    weight = jnp.concatenate(weights, axis=1)
    mark = jnp.concatenate(marks, axis=1)
    parts = []
    for _ in range(3):
        parts.append(weight.astype(bf16))
        weight = weight - parts[-1].astype(f32)
    stack = jnp.concatenate(parts, axis=0)

    def total(x):
        return x[0:CODES] + (x[CODES : 2 * CODES] + x[2 * CODES : 3 * CODES])

    moment = total(lax.dot_general(stack, poses[...], NN, preferred_element_type=f32))
    pair = total(lax.dot_general(stack, mark, NT, preferred_element_type=f32))
    count = jnp.sum(pair, axis=1, keepdims=True)
    moment = moment - count * codebook[...].astype(f32)
    moment = moment - lax.dot_general(
        pair, offsets[...].astype(f32), NN, precision=precise, preferred_element_type=f32
    )
    moment = moment / math.sqrt(FRAMES / CODES)
    for half in range(2):
        pg[pl.ds(half, CODES, stride=2), :] = moment[:, BS * half : BS * half + BS]

    for copy in copies:
        copy.wait()

    @pl.when(f == 0)
    def _():
        for copy in by_col:
            copy.wait()

    @pl.when(f == 1)
    def _():
        for copy in by_row:
            copy.wait()


def prepare(mem, hess, poses, codebook, offsets, conf, codes, kinds):
    return pl.pallas_call(
        prepare_kernel,
        out_shape=(
            jax.ShapeDtypeStruct((NQ, BS, BS), f32),
            jax.ShapeDtypeStruct((8, 2, BS, BS), f32),
            jax.ShapeDtypeStruct((64, BS), f32),
        ),
        in_specs=[SM, ANY, VM, VM, VM, VM, VM, VM],
        out_specs=(VM, VM, VM),
        scratch_shapes=[pltpu.SemaphoreType.DMA((NQ + 18,))],
        compiler_params=pltpu.CompilerParams(vmem_limit_bytes=24 << 20),
        name="prepare",
    )(mem, hess, poses, codebook, offsets, conf, codes, kinds)


def spread(row):
    return jnp.broadcast_to(row, (8, BS))


def factor_block(block):
    groups = BS // 8
    row_ids = lax.broadcasted_iota(jnp.int32, (8, BS), 0)
    lane_ids = lax.broadcasted_iota(jnp.int32, (8, BS), 1)
    upper = [block[8 * g : 8 * g + 8, :] for g in range(groups)]
    inv = [jnp.where(lane_ids == row_ids + 8 * g, 1.0, 0.0).astype(f32) for g in range(groups)]
    for g in range(groups):
        k = 8 * g
        v, w = upper[g], inv[g]
        cols = [jnp.broadcast_to(v[:, k + j : k + j + 1], (8, BS)) for j in range(8)]
        rows_v, rows_w, coef = [], [], []
        for j in range(8):
            pivot = spread(cols[j][j : j + 1, :])
            recip = 1.0 / pivot
            rv = spread(v[j : j + 1, :]) * recip
            rw = spread(w[j : j + 1, :]) * recip
            rows_v.append(rv)
            rows_w.append(rw)
            below = jnp.where(row_ids > j, cols[j], 0.0)
            coef.append([None] * 8)
            for t in range(j + 1, 8):
                coef[j][t] = spread(cols[t][j : j + 1, :]) * recip
                cols[t] = cols[t] - below * coef[j][t]
            v = v - below * rv
            w = w - below * rw
        upper[g], inv[g] = v, w
        for h in range(g + 1, groups):
            v, w = upper[h], inv[h]
            cols = [jnp.broadcast_to(v[:, k + j : k + j + 1], (8, BS)) for j in range(8)]
            for j in range(8):
                for t in range(j + 1, 8):
                    cols[t] = cols[t] - cols[j] * coef[j][t]
                v = v - cols[j] * rows_v[j]
                w = w - cols[j] * rows_w[j]
            upper[h], inv[h] = v, w
    full = jnp.concatenate(upper, axis=0)
    inverse = jnp.concatenate(inv, axis=0)
    rr = lax.broadcasted_iota(jnp.int32, (BS, BS), 0)
    cc = lax.broadcasted_iota(jnp.int32, (BS, BS), 1)
    pivots = jnp.sum(jnp.where(rr == cc, full, 0.0), axis=1, keepdims=True)
    scale = 1.0 / jnp.sqrt(pivots)
    return jnp.where(cc >= rr, full * scale, 0.0), inverse * scale


def dot_nt(a, b):
    return lax.dot_general(a, b, NT, precision=precise, preferred_element_type=f32)


def dot_nn(a, b):
    return lax.dot_general(a, b, (((1,), (0,)), ((), ())), precision=precise, preferred_element_type=f32)


def exchange_kernel(
    mem, pat, scand, ccand, pg,
    x_hi, x_lo, diag, y_out, g_out,
    s_all, low, inv, cur, fac_u, fac_i, raw, wh, wl,
    s1r_a, s1r_b, s1, s2r_a, s2r_b, par, mine, g1r, g1, g2r, g2, g3r,
    snd_s1, rcv_s1, snd_s2, rcv_s2, snd_s3, rcv_s3, snd_sx, rcv_sx,
    snd_a, rcv_a, snd_r, rcv_r, snd_t, rcv_t, snd_x, rcv_x,
    snd_g1, rcv_g1, snd_g2, rcv_g2, snd_g4, rcv_g4, snd_g3, rcv_g3,
):
    s1r, s2r = (s1r_a, s1r_b), (s2r_a, s2r_b)
    f = lax.axis_index("frames")
    r = lax.axis_index("prow")
    c = lax.axis_index("pcol")
    p = r + f * (c - r)
    q = c + f * (r - c)

    def place(p_to, q_to):
        return (f, p_to + f * (q_to - p_to), q_to + f * (p_to - q_to))

    sibling = (1 - f, r, c)

    def copy(src, dst, snd, rcv, to):
        return pltpu.make_async_remote_copy(
            src_ref=src, dst_ref=dst, send_sem=snd, recv_sem=rcv, device_id=to, device_id_type=MESH
        )

    def q_peer(d):
        return lax.rem(q + d, 8)

    def p_peer(d):
        return lax.rem(p + d, 8)

    def c_peer(d):
        return lax.rem(c + d, 8)

    def r_peer(d):
        return lax.rem(r + d, 8)

    barrier = pltpu.get_barrier_semaphore()

    def greet(to):
        pl.semaphore_signal(barrier, inc=1, device_id=to, device_id_type=MESH)

    greet(sibling)

    def greet_line(d):
        greet(place(p, q_peer(d)))
        greet(place(p_peer(d), q))

    loop(1, 8, greet_line)

    def greet_turn(d):
        @pl.when(jnp.logical_or(d != p, p != q))
        def _():
            greet(place(d, p))

        @pl.when(jnp.logical_or(d != q, p != q))
        def _():
            greet(place(q, d))

    loop(0, 8, greet_turn)
    same = jnp.where(p == q, 1, 0)
    pl.semaphore_wait(barrier, 31 - 2 * same)

    def rows_of(slice_id):
        return pl.ds(pl.multiple_of(8 * slice_id, 8), 8)

    def s1_copy(h, peer, at):
        lo, n = CHUNKS[h]
        return copy(
            scand.at[pl.ds(lo, n), rows_of(peer + 8 * f), :], s1r[h].at[at],
            snd_s1.at[h, peer], rcv_s1.at[h, at], place(p, peer),
        )

    def s2_copy(h, peer, at):
        lo, n = CHUNKS[h]
        return copy(
            s1.at[pl.ds(lo, n)], s2r[h].at[at],
            snd_s2.at[h, peer], rcv_s2.at[h, at], place(peer, q),
        )

    def s3_copy(h, peer, at):
        lo, n = CHUNKS[h]
        part = s_all.at[pl.ds(lo, n), rows_of(at + 8 * f), :]
        return copy(part, part, snd_s3.at[h, peer], rcv_s3.at[h, at], place(p, peer))

    def sx_copy(h, at, core):
        lo, n = CHUNKS[h]
        part = s_all.at[pl.ds(lo, n), rows_of(at + 8 * core), :]
        return copy(part, part, snd_sx.at[h, at], rcv_sx.at[h, at], sibling)

    def g1_copy(peer, at):
        return copy(pg.at[peer], g1r.at[at], snd_g1.at[peer], rcv_g1.at[at], (f, r, peer))

    def g2_copy(peer, at):
        return copy(g1, g2r.at[at], snd_g2.at[peer], rcv_g2.at[at], (f, peer, c))

    def g4_copy(peer, at):
        return copy(g_out.at[at], g_out.at[at], snd_g4.at[peer], rcv_g4.at[at], (f, r, peer))

    def a_copy(peer, at):
        return copy(ccand.at[peer], par.at[at], snd_a.at[peer], rcv_a.at[at], place(p, peer))

    def r_copy(peer, at):
        return copy(mine, raw.at[f, f, at], snd_r.at[peer], rcv_r.at[at], place(p, peer))

    def t_copy(peer, at):
        return copy(mine, raw.at[1 - f, f, at], snd_t.at[peer], rcv_t.at[at], place(peer, p))

    def x_copy(which, at, core):
        part = raw.at[which, core, at]
        return copy(part, part, snd_x.at[which, at], rcv_x.at[which, at], sibling)

    for h in range(2):
        loop(1, 8, lambda d: s1_copy(h, q_peer(d), q).start())
    loop(1, 8, lambda d: g1_copy(c_peer(d), c).start())
    for h, (lo, n) in enumerate(CHUNKS):
        s1r[h][q] = scand[lo : lo + n, rows_of(q + 8 * f), :]
    g1r[c] = pg[c]
    par[q] = ccand[q]

    for h in range(2):
        lo, n = CHUNKS[h]
        loop(1, 8, lambda d: s1_copy(h, q_peer(d), q_peer(d)).wait())
        for e in range(lo, lo + n):
            own_k = lax.rem(member(mem, PAIRS[e][0]), 8)
            own_m = lax.rem(member(mem, PAIRS[e][1]), 8)
            s1[e] = s1r[h][own_m + f * (own_k - own_m), e - lo]
        loop(1, 8, lambda d: s2_copy(h, p_peer(d), p).start())
        s2r[h][p] = s1[lo : lo + n]

    loop(1, 8, lambda d: g1_copy(c_peer(d), c_peer(d)).wait())
    g1[...] = jnp.sum(g1r[...], axis=0)
    loop(1, 8, lambda d: g2_copy(r_peer(d), r).start())
    g2r[r] = g1[...]


    for h in range(2):
        lo, n = CHUNKS[h]
        loop(1, 8, lambda d: s2_copy(h, p_peer(d), p_peer(d)).wait())
        for e in range(lo, lo + n):
            own_k = lax.rem(member(mem, PAIRS[e][0]), 8)
            own_m = lax.rem(member(mem, PAIRS[e][1]), 8)
            s_all[e, rows_of(q + 8 * f), :] = s2r[h][own_k + f * (own_m - own_k), e - lo]
        loop(1, 8, lambda d: s3_copy(h, q_peer(d), q).start())
        sx_copy(h, q, f).start()

    loop(1, 8, lambda d: a_copy(q_peer(d), q).start())

    loop(1, 8, lambda d: g2_copy(r_peer(d), r_peer(d)).wait())
    g2[...] = jnp.sum(g2r[...], axis=0)
    g3 = copy(g2, g3r, snd_g3, rcv_g3, sibling)
    g3.start()

    def pass_on(h):
        def one(d):
            s3_copy(h, q_peer(d), q_peer(d)).wait_recv()
            sx_copy(h, q_peer(d), f).start()

        loop(1, 8, one)

    def sx_ready(h):
        loop(0, 8, lambda at: sx_copy(h, at, 1 - f).wait_recv())

    pass_on(0)

    rr = lax.broadcasted_iota(jnp.int32, (BS, BS), 0)
    cc = lax.broadcasted_iota(jnp.int32, (BS, BS), 1)
    low[...] = jnp.zeros_like(low)
    inv[...] = jnp.zeros_like(inv)

    def before(k):
        if k == 0:
            sx_ready(0)
        if k == 2:
            sx_ready(1)
        for m in range(k):
            keep = pat[member(mem, k), member(mem, m)].astype(f32)
            value = s_all[PAIRS.index((k, m))] * keep
            if m:
                value = value - keep * dot_nt(low[k, :, 0 : BS * m], low[m, :, 0 : BS * m])
            low[k, :, BS * m : BS * m + BS] = dot_nt(value, inv[BS * m : BS * m + BS, BS * m : BS * m + BS])
        value = s_all[PAIRS.index((k, k))] * pat[member(mem, k), member(mem, k)].astype(f32)
        value = value + jnp.where(rr == cc, SHIFT, 0.0)
        if k:
            lows = low[k, :, 0 : BS * k]
            value = value - dot_nt(lows, lows)
        cur[...] = value

    def after(k):
        at = slice(BS * k, BS * k + BS)
        inv[at, at] = fac_i[...]
        if k:
            inv[at, 0 : BS * k] = -dot_nn(fac_i[...], dot_nn(low[k, :, 0 : BS * k], inv[0 : BS * k, 0 : BS * k]))
        lower = fac_u[...].T
        low[k, :, at] = lower
        diag[k] = lower
        if k == 0:
            pass_on(1)
        if k == 1:
            spread_panels()
        if k == 2:
            g3.wait()
            g_out[c] = g2[...] + g3r[...]
            loop(1, 8, lambda d: g4_copy(c_peer(d), c).start())

    def spread_panels():
        loop(1, 8, lambda d: a_copy(q_peer(d), q_peer(d)).wait())

        @pl.when(f == 0)
        def _():
            for k in range(2):
                mine[k] = par[lax.rem(mem[0, k], 8), k]

        @pl.when(f == 1)
        def _():
            for k in range(2):
                mine[k] = par[lax.rem(mem[1, k], 8), k].T

        loop(1, 8, lambda d: r_copy(q_peer(d), q).start())
        raw[f, f, q] = mine[...]

        def turn(d):
            @pl.when(jnp.logical_or(d != p, p != q))
            def _():
                t_copy(d, q).start()

        loop(0, 8, turn)

        @pl.when(p == q)
        def _():
            raw[1 - f, f, q] = mine[...]

        x_copy(f, q, f).start()

    def step(k):
        for kk in range(STEPS):
            @pl.when(k == kk)
            def _():
                before(kk)

        upper, inverse = factor_block(cur[...])
        fac_u[...] = upper
        fac_i[...] = inverse
        for kk in range(STEPS):
            @pl.when(k == kk)
            def _():
                after(kk)

    loop(0, STEPS, step)

    def r_arrives(d):
        r_copy(q_peer(d), q_peer(d)).wait_recv()
        x_copy(f, q_peer(d), f).start()

    loop(1, 8, r_arrives)

    def t_arrives(b):
        @pl.when(jnp.logical_or(b != q, p != q))
        def _():
            t_copy(b, b).wait_recv()

        x_copy(1 - f, b, f).start()

    loop(0, 8, t_arrives)

    h, l = split(inv[...])
    wh[...] = h
    wl[...] = l
    half = 2 * BS
    w11 = (wh[0:half, 0:half], wl[0:half, 0:half])
    w21 = (wh[half:, 0:half], wl[half:, 0:half])
    w22 = (wh[half:, half:], wl[half:, half:])

    loop(1, 8, lambda d: g4_copy(c_peer(d), c_peer(d)).wait_recv())
    gp = jnp.concatenate(
        [g_out[member(mem, k) // 8, pl.ds(lax.rem(member(mem, k), 8), 1), :] for k in range(STEPS)], axis=1
    )
    gp = jnp.broadcast_to(gp, (16, WIDE))
    y_out[...] = dot3(split(gp), (wh[...], wl[...]))[0:8]

    def panel(which, a):
        base = r + which * (c - r)
        i = 8 * a + base
        pivot = i == member(mem, 0)
        for k in range(1, STEPS):
            pivot = jnp.logical_or(pivot, i == member(mem, k))
        z = jnp.where(pivot, 0.0, 1.0).astype(f32)
        m1 = z * pat[i, member(mem, 0)].astype(f32)
        m2 = z * pat[i, member(mem, 2)].astype(f32)
        one = split(jnp.concatenate([raw[which, 0, a, 0], raw[which, 0, a, 1]], axis=1) * m1)
        two = split(jnp.concatenate([raw[which, 1, a, 0], raw[which, 1, a, 1]], axis=1))
        rows = pl.ds(pl.multiple_of(BS * a, BS), BS)
        for lo, x in ((0, dot3(one, w11)), (half, m2 * (dot3(one, w21) + dot3(two, w22)))):
            hi, rest = split(x)
            x_hi[which, rows, lo : lo + half] = hi
            x_lo[which, rows, lo : lo + half] = rest

    def panel_step(t):
        which = t // 8
        a = lax.rem(t, 8)
        x_copy(which, a, 1 - f).wait_recv()
        panel(which, a)

    loop(0, 16, panel_step)

    def tail(d):
        for h in range(2):
            s3_copy(h, q_peer(d), q).wait_send()
        r_copy(q_peer(d), q).wait_send()
        g4_copy(c_peer(d), c).wait_send()

    loop(1, 8, tail)

    def tail_turn(d):
        @pl.when(jnp.logical_or(d != p, p != q))
        def _():
            t_copy(d, q).wait_send()

        for h in range(2):
            sx_copy(h, d, f).wait_send()
        for which in range(2):
            x_copy(which, d, f).wait_send()

    loop(0, 8, tail_turn)


def exchange(mem, pat, scand, ccand, pg):
    vmem = pltpu.VMEM
    sem = pltpu.SemaphoreType.DMA
    return pl.pallas_call(
        exchange_kernel,
        out_shape=(
            jax.ShapeDtypeStruct((2, 1024, WIDE), bf16),
            jax.ShapeDtypeStruct((2, 1024, WIDE), bf16),
            jax.ShapeDtypeStruct((STEPS, BS, BS), f32),
            jax.ShapeDtypeStruct((8, WIDE), f32),
            jax.ShapeDtypeStruct((8, 8, BS), f32),
        ),
        in_specs=[SM, SM, VM, VM, VM],
        out_specs=(VM,) * 5,
        scratch_shapes=[
            vmem((NQ, BS, BS), f32),
            vmem((STEPS, BS, WIDE), f32),
            vmem((WIDE, WIDE), f32),
            vmem((BS, BS), f32),
            vmem((BS, BS), f32),
            vmem((BS, BS), f32),
            vmem((2, 2, 8, 2, BS, BS), f32),
            vmem((WIDE, WIDE), bf16),
            vmem((WIDE, WIDE), bf16),
            vmem((8, CHUNKS[0][1], 8, BS), f32),
            vmem((8, CHUNKS[1][1], 8, BS), f32),
            vmem((NQ, 8, BS), f32),
            vmem((8, CHUNKS[0][1], 8, BS), f32),
            vmem((8, CHUNKS[1][1], 8, BS), f32),
            vmem((8, 2, BS, BS), f32),
            vmem((2, BS, BS), f32),
            vmem((8, 8, BS), f32),
            vmem((8, BS), f32),
            vmem((8, 8, BS), f32),
            vmem((8, BS), f32),
            vmem((8, BS), f32),
        ]
        + [sem((2, 8))] * 8
        + [sem((8,))] * 6
        + [sem((2, 8))] * 2
        + [sem((8,))] * 6
        + [sem, sem],
        compiler_params=pltpu.CompilerParams(
            collective_id=0, has_side_effects=True, vmem_limit_bytes=40 << 20
        ),
        name="exchange",
    )(mem, pat, scand, ccand, pg)


def update_kernel(mem, pat, diag, x_hi, x_lo, y, g, hess, out, grad_out, rows, in_sem, out_sem):
    r = lax.axis_index("prow")
    c = lax.axis_index("pcol")

    def load(a):
        return pltpu.make_async_copy(hess.at[a], rows.at[a], in_sem.at[a])

    def save(a):
        return pltpu.make_async_copy(rows.at[a], out.at[a], out_sem.at[a])

    for a in range(8):
        load(a).start()

    def is_pivot(i):
        pivot = i == member(mem, 0)
        for k in range(1, STEPS):
            pivot = jnp.logical_or(pivot, i == member(mem, k))
        return pivot

    dec = dot3(split(jnp.concatenate([y[...], y[...]], axis=0)), (x_hi[0], x_lo[0]))
    for a in range(8):
        i = 8 * a + r
        val = g[a, pl.ds(r, 1), :] - dec[0:1, BS * a : BS * a + BS]
        for k in range(STEPS):
            val = jnp.where(i == member(mem, k), y[0:1, BS * k : BS * k + BS], val)
        grad_out[a : a + 1, :] = val

    rr = lax.broadcasted_iota(jnp.int32, (BS, BS), 0)
    cc = lax.broadcasted_iota(jnp.int32, (BS, BS), 1)
    shift = jnp.where(rr == cc, SHIFT, 0.0)
    cols = (x_hi[1], x_lo[1])

    def two_rows(t):
        at = pl.ds(pl.multiple_of(2 * BS * t, 2 * BS), 2 * BS)
        upd = dot3((x_hi[0, at, :], x_lo[0, at, :]), cols)
        for e in range(2):
            a = 2 * t + e
            i = 8 * a + r
            live = jnp.where(is_pivot(i), 0.0, 1.0).astype(f32)
            load(a).wait()
            for b in range(8):
                j = 8 * b + c
                keep = live * pat[i, j].astype(f32)
                on = jnp.where(i == j, 1.0, 0.0).astype(f32) * live
                sub = upd[BS * e : BS * e + BS, BS * b : BS * b + BS]
                there = pl.ds(b, BS, stride=8)
                rows[a, there, :] = keep * (rows[a, there, :] - sub) + on * shift
            for k in range(STEPS):
                pk = member(mem, k)

                @pl.when(lax.rem(pk, 8) == c)
                def _():
                    there = pl.ds(pk // 8, BS, stride=8)
                    mine = pl.ds(pl.multiple_of(BS * a, BS), BS)
                    part = slice(BS * k, BS * k + BS)

                    @pl.when(i != pk)
                    def _():
                        rows[a, there, :] = x_hi[0, mine, part].astype(f32) + x_lo[0, mine, part].astype(f32)

                    @pl.when(i == pk)
                    def _():
                        rows[a, there, :] = diag[k]
            save(a).start()

    loop(0, 4, two_rows)
    for a in range(8):
        save(a).wait()


def update(mem, pat, diag, x_hi, x_lo, y, g, hess):
    return pl.pallas_call(
        update_kernel,
        out_shape=(
            jax.ShapeDtypeStruct(hess.shape, f32),
            jax.ShapeDtypeStruct((8, BS), f32),
        ),
        in_specs=[SM, SM, VM, VM, VM, VM, VM, ANY],
        out_specs=(ANY, VM),
        scratch_shapes=[
            pltpu.VMEM((8, 1024, BS), f32),
            pltpu.SemaphoreType.DMA((8,)),
            pltpu.SemaphoreType.DMA((8,)),
        ],
        compiler_params=pltpu.CompilerParams(vmem_limit_bytes=32 << 20),
        name="update",
    )(mem, pat, diag, x_hi, x_lo, y, g, hess)


def shards(
    poses, codebook, offsets, confidence, code_ids, creature_ids, hess_raw, pattern, membership
):
    scand, ccand, pg = prepare(
        membership, hess_raw.reshape(8, BS, 8, 1, BS), poses, codebook, offsets,
        confidence.reshape(16, BS), code_ids.reshape(16, BS), creature_ids.reshape(16, BS),
    )
    x_hi, x_lo, diag, y, g = exchange(membership, pattern, scand, ccand, pg.reshape(8, 8, BS))
    state, grad = update(
        membership, pattern, diag, x_hi, x_lo, y, g, hess_raw.reshape(8, 1024, BS)
    )
    return state.reshape(hess_raw.shape), grad.reshape(8, 1, BS)


def solution(mesh):
    return jax.shard_map(
        shards,
        mesh=mesh,
        in_specs=(
            P(("frames", "prow", "pcol"), None),
            P(),
            P(),
            P(("frames", "prow", "pcol")),
            P(("frames", "prow", "pcol")),
            P(("frames", "prow", "pcol")),
            P(None, "prow", None, None, "pcol", None),
            P(),
            P(),
        ),
        out_specs=(P(None, "prow", None, None, "pcol", None), P(None, "prow", None)),
        check_vma=False,
    )
```

```python
import math

import jax
import jax.numpy as jnp
from jax import lax
from jax.experimental import pallas as pl
from jax.experimental.pallas import tpu as pltpu
from jax.sharding import PartitionSpec as P

NPAN = 8192
BS = 128
STEPS = 4
FRAMES = 262144
CODES = 32
SHIFT = 2.5 * math.sqrt(NPAN)
PAIRS = [(k, m) for k in range(STEPS) for m in range(k + 1)]
NQ = len(PAIRS)
CHUNKS = ((0, 3), (3, 7))
WIDE = STEPS * BS
MESH = pl.DeviceIdType.MESH
precise = lax.Precision.HIGHEST
f32 = jnp.float32
bf16 = jnp.bfloat16
NT = (((1,), (1,)), ((), ()))
NN = (((1,), (0,)), ((), ()))


def loop(lo, hi, fn):
    def body(d, carry):
        fn(d)
        return carry

    lax.fori_loop(lo, hi, body, 0)


def split(x):
    hi = x.astype(bf16)
    return hi, (x - hi.astype(f32)).astype(bf16)


def dot3(a, b):
    (ah, al), (bh, bl) = a, b
    d = lambda x, y: lax.dot_general(x, y, NT, preferred_element_type=f32)
    return d(ah, bh) + (d(ah, bl) + d(al, bh))


def member(mem, k):
    return mem[k // 2, k % 2]


VM = pl.BlockSpec(memory_space=pltpu.VMEM)
SM = pl.BlockSpec(memory_space=pltpu.SMEM)
ANY = pl.BlockSpec(memory_space=pl.ANY)


def prepare_kernel(
    mem, hess, poses_at, codebook_at, offsets_at, conf_at, codes_at, kinds_at, scand, ccand, pg,
    poses, codebook, offsets, conf, codes, kinds, sem, in_sem,
):
    fetches = [
        pltpu.make_async_copy(src, dst, in_sem.at[n])
        for n, (src, dst) in enumerate(
            [
                (codes_at, codes), (conf_at, conf), (kinds_at, kinds),
                (poses_at, poses), (codebook_at, codebook), (offsets_at, offsets),
            ]
        )
    ]
    for fetch in fetches:
        fetch.start()
    f = lax.axis_index("frames")
    slot = [member(mem, k) // 8 for k in range(STEPS)]
    copies = [
        pltpu.make_async_copy(hess.at[slot[k], :, slot[m], 0, :], scand.at[q], sem.at[q])
        for q, (k, m) in enumerate(PAIRS)
    ]
    for copy in copies:
        copy.start()
    by_col = [
        pltpu.make_async_copy(hess.at[:, :, slot[k], 0, :], ccand.at[:, k], sem.at[NQ + k])
        for k in range(2)
    ]
    by_row = [
        pltpu.make_async_copy(hess.at[slot[2 + k], :, b, 0, :], ccand.at[b, k], sem.at[NQ + 2 + 8 * k + b])
        for k in range(2)
        for b in range(8)
    ]

    @pl.when(f == 0)
    def _():
        for copy in by_col:
            copy.start()

    @pl.when(f == 1)
    def _():
        for copy in by_row:
            copy.start()

    for fetch in fetches:
        fetch.wait()
    ids = lax.broadcasted_iota(jnp.int32, (CODES, BS), 0)
    weights, marks = [], []
    for s in range(16):
        weights.append(jnp.where(codes[s : s + 1, :] == ids, conf[s : s + 1, :], 0.0))
        marks.append(jnp.where(kinds[s : s + 1, :] == ids, 1.0, 0.0).astype(bf16))
    weight = jnp.concatenate(weights, axis=1)
    mark = jnp.concatenate(marks, axis=1)
    parts = []
    for _ in range(3):
        parts.append(weight.astype(bf16))
        weight = weight - parts[-1].astype(f32)
    stack = jnp.concatenate(parts, axis=0)

    def total(x):
        return x[0:CODES] + (x[CODES : 2 * CODES] + x[2 * CODES : 3 * CODES])

    moment = total(lax.dot_general(stack, poses[...], NN, preferred_element_type=f32))
    pair = total(lax.dot_general(stack, mark, NT, preferred_element_type=f32))
    count = jnp.sum(pair, axis=1, keepdims=True)
    moment = moment - count * codebook[...].astype(f32)
    moment = moment - lax.dot_general(
        pair, offsets[...].astype(f32), NN, precision=precise, preferred_element_type=f32
    )
    moment = moment / math.sqrt(FRAMES / CODES)
    for half in range(2):
        pg[pl.ds(half, CODES, stride=2), :] = moment[:, BS * half : BS * half + BS]

    for copy in copies:
        copy.wait()

    @pl.when(f == 0)
    def _():
        for copy in by_col:
            copy.wait()

    @pl.when(f == 1)
    def _():
        for copy in by_row:
            copy.wait()


def prepare(mem, hess, poses, codebook, offsets, conf, codes, kinds):
    return pl.pallas_call(
        prepare_kernel,
        out_shape=(
            jax.ShapeDtypeStruct((NQ, BS, BS), f32),
            jax.ShapeDtypeStruct((8, 2, BS, BS), f32),
            jax.ShapeDtypeStruct((64, BS), f32),
        ),
        in_specs=[SM] + [ANY] * 7,
        out_specs=(VM, VM, VM),
        scratch_shapes=[pltpu.VMEM(x.shape, x.dtype) for x in (poses, codebook, offsets, conf, codes, kinds)]
        + [pltpu.SemaphoreType.DMA((NQ + 18,)), pltpu.SemaphoreType.DMA((6,))],
        compiler_params=pltpu.CompilerParams(vmem_limit_bytes=24 << 20),
        name="prepare",
    )(mem, hess, poses, codebook, offsets, conf, codes, kinds)


def spread(row):
    return jnp.broadcast_to(row, (8, BS))


def factor_block(block):
    groups = BS // 8
    row_ids = lax.broadcasted_iota(jnp.int32, (8, BS), 0)
    lane_ids = lax.broadcasted_iota(jnp.int32, (8, BS), 1)
    upper = [block[8 * g : 8 * g + 8, :] for g in range(groups)]
    inv = [jnp.where(lane_ids == row_ids + 8 * g, 1.0, 0.0).astype(f32) for g in range(groups)]
    for g in range(groups):
        k = 8 * g
        v, w = upper[g], inv[g]
        cols = [jnp.broadcast_to(v[:, k + j : k + j + 1], (8, BS)) for j in range(8)]
        rows_v, rows_w, coef = [], [], []
        for j in range(8):
            pivot = spread(cols[j][j : j + 1, :])
            recip = 1.0 / pivot
            rv = spread(v[j : j + 1, :]) * recip
            rw = spread(w[j : j + 1, :]) * recip
            rows_v.append(rv)
            rows_w.append(rw)
            below = jnp.where(row_ids > j, cols[j], 0.0)
            coef.append([None] * 8)
            for t in range(j + 1, 8):
                coef[j][t] = spread(cols[t][j : j + 1, :]) * recip
                cols[t] = cols[t] - below * coef[j][t]
            v = v - below * rv
            w = w - below * rw
        upper[g], inv[g] = v, w
        for h in range(g + 1, groups):
            v, w = upper[h], inv[h]
            cols = [jnp.broadcast_to(v[:, k + j : k + j + 1], (8, BS)) for j in range(8)]
            for j in range(8):
                for t in range(j + 1, 8):
                    cols[t] = cols[t] - cols[j] * coef[j][t]
                v = v - cols[j] * rows_v[j]
                w = w - cols[j] * rows_w[j]
            upper[h], inv[h] = v, w
    full = jnp.concatenate(upper, axis=0)
    inverse = jnp.concatenate(inv, axis=0)
    rr = lax.broadcasted_iota(jnp.int32, (BS, BS), 0)
    cc = lax.broadcasted_iota(jnp.int32, (BS, BS), 1)
    pivots = jnp.sum(jnp.where(rr == cc, full, 0.0), axis=1, keepdims=True)
    scale = 1.0 / jnp.sqrt(pivots)
    return jnp.where(cc >= rr, full * scale, 0.0), inverse * scale


def dot_nt(a, b):
    return lax.dot_general(a, b, NT, precision=precise, preferred_element_type=f32)


def dot_nn(a, b):
    return lax.dot_general(a, b, (((1,), (0,)), ((), ())), precision=precise, preferred_element_type=f32)


def exchange_kernel(
    mem, pat, scand, ccand, pg,
    x_hi, x_lo, diag, y_out, g_out,
    s_all, low, inv, cur, fac_u, fac_i, raw, wh, wl,
    s1r_a, s1r_b, s1, s2r_a, s2r_b, par, picked, other, both, mine, g1r, g1, g2r, g2, g3r,
    snd_s1, rcv_s1, snd_s2, rcv_s2, snd_s3, rcv_s3, snd_sx, rcv_sx,
    snd_x, rcv_x, snd_a, rcv_a, snd_r2, snd_t2, snd_t1, rcv_r, rcv_t,
    snd_g1, rcv_g1, snd_g2, rcv_g2, snd_g4, rcv_g4, snd_g3, rcv_g3, snd_b, rcv_b, snd_r1,
):
    s1r, s2r = (s1r_a, s1r_b), (s2r_a, s2r_b)
    f = lax.axis_index("frames")
    r = lax.axis_index("prow")
    c = lax.axis_index("pcol")
    p = r + f * (c - r)
    q = c + f * (r - c)

    def place(p_to, q_to):
        return (f, p_to + f * (q_to - p_to), q_to + f * (p_to - q_to))

    sibling = (1 - f, r, c)

    def q_at(line, pair):
        return 2 * line + pair + f * (3 * pair - line)

    def p_at(line, pair):
        return line + 4 * pair + f * (line - 3 * pair)

    def q_parts(v):
        return v // 2 + f * (lax.rem(v, 4) - v // 2), lax.rem(v, 2) + f * (v // 4 - lax.rem(v, 2))

    def p_parts(v):
        return lax.rem(v, 4) + f * (v // 2 - lax.rem(v, 4)), v // 4 + f * (lax.rem(v, 2) - v // 4)

    ql, qh = q_parts(q)
    pl_, ph = p_parts(p)

    def q_line(d):
        return lax.rem(ql + d, 4)

    def p_line(d):
        return lax.rem(pl_ + d, 4)

    def copy(src, dst, snd, rcv, to):
        return pltpu.make_async_remote_copy(
            src_ref=src, dst_ref=dst, send_sem=snd, recv_sem=rcv, device_id=to, device_id_type=MESH
        )

    def q_peer(d):
        return lax.rem(q + d, 8)

    def p_peer(d):
        return lax.rem(p + d, 8)

    def c_peer(d):
        return lax.rem(c + d, 8)

    def r_peer(d):
        return lax.rem(r + d, 8)

    barrier = pltpu.get_barrier_semaphore()

    def greet(to):
        pl.semaphore_signal(barrier, inc=1, device_id=to, device_id_type=MESH)

    greet(sibling)

    def greet_line(d):
        greet(place(p, q_peer(d)))
        greet(place(p_peer(d), q))

    loop(1, 8, greet_line)

    def at_home(p_to, q_to):
        return jnp.logical_and(p_to == p, q_to == q)

    def away(p_to, q_to, fn):
        @pl.when(jnp.logical_not(at_home(p_to, q_to)))
        def _():
            fn()

    def greet_turn(e):
        away(p_at(ql, e), p, lambda: greet(place(p_at(ql, e), p)))
        away(q, q_at(pl_, e), lambda: greet(place(q, q_at(pl_, e))))

    loop(0, 2, greet_turn)
    same = jnp.where(jnp.logical_and(p == q, ql == pl_), 1, 0)
    pl.semaphore_wait(barrier, 19 - 2 * same)

    def rows_of(slice_id):
        return pl.ds(pl.multiple_of(8 * slice_id, 8), 8)

    def s1_copy(h, peer, at):
        lo, n = CHUNKS[h]
        return copy(
            scand.at[pl.ds(lo, n), rows_of(peer + 8 * f), :], s1r[h].at[at],
            snd_s1.at[h, peer], rcv_s1.at[h, at], place(p, peer),
        )

    def s2_copy(h, peer, at):
        lo, n = CHUNKS[h]
        return copy(
            s1.at[pl.ds(lo, n)], s2r[h].at[at],
            snd_s2.at[h, peer], rcv_s2.at[h, at], place(peer, q),
        )

    def s3_copy(h, peer, at):
        lo, n = CHUNKS[h]
        part = s_all.at[pl.ds(lo, n), rows_of(at + 8 * f), :]
        return copy(part, part, snd_s3.at[h, peer], rcv_s3.at[h, at], place(p, peer))

    def sx_copy(h, at, core):
        lo, n = CHUNKS[h]
        part = s_all.at[pl.ds(lo, n), rows_of(at + 8 * core), :]
        return copy(part, part, snd_sx.at[h, at], rcv_sx.at[h, at], sibling)

    def g1_copy(peer, at):
        return copy(pg.at[peer], g1r.at[at], snd_g1.at[peer], rcv_g1.at[at], (f, r, peer))

    def g2_copy(peer, at):
        return copy(g1, g2r.at[at], snd_g2.at[peer], rcv_g2.at[at], (f, peer, c))

    def g4_copy(peer, at):
        return copy(g_out.at[at], g_out.at[at], snd_g4.at[peer], rcv_g4.at[at], (f, r, peer))

    def a_copy(e, line, at):
        return copy(
            ccand.at[q_at(line, e)], par.at[at, e], snd_a.at[e, line], rcv_a.at[e, at], place(p, q_at(line, qh))
        )

    def b_copy():
        return copy(picked.at[1 - qh], other, snd_b, rcv_b, place(p, q_at(ql, 1 - qh)))

    def r1_copy(at):
        return copy(mine, raw.at[f, f, at], snd_r1, rcv_r.at[at], place(p, q_at(ql, 1 - qh)))

    def r2_copy(e, line, at):
        part = raw.at[f, f, at]
        return copy(part, part, snd_r2.at[e, line], rcv_r.at[at], place(p, q_at(line, qh)))

    def t1_copy(e, at):
        return copy(mine, raw.at[1 - f, f, at], snd_t1.at[e], rcv_t.at[at], place(p_at(ql, e), p))

    def t2_copy(e, line, at):
        part = raw.at[1 - f, f, at]
        return copy(part, part, snd_t2.at[e, line], rcv_t.at[at], place(p_at(line, ph), q))

    def x_copy(which, at, core):
        part = raw.at[which, core, at]
        return copy(part, part, snd_x.at[which, at], rcv_x.at[which, at], sibling)

    for h in range(2):
        loop(1, 8, lambda d: s1_copy(h, q_peer(d), q).start())
    loop(1, 8, lambda d: g1_copy(c_peer(d), c).start())
    for h, (lo, n) in enumerate(CHUNKS):
        s1r[h][q] = scand[lo : lo + n, rows_of(q + 8 * f), :]
    g1r[c] = pg[c]
    for e in range(2):
        par[ql, e] = ccand[q_at(ql, e)]

    for h in range(2):
        lo, n = CHUNKS[h]
        loop(1, 8, lambda d: s1_copy(h, q_peer(d), q_peer(d)).wait())
        for e in range(lo, lo + n):
            own_k = lax.rem(member(mem, PAIRS[e][0]), 8)
            own_m = lax.rem(member(mem, PAIRS[e][1]), 8)
            s1[e] = s1r[h][own_m + f * (own_k - own_m), e - lo]
        loop(1, 8, lambda d: s2_copy(h, p_peer(d), p).start())
        s2r[h][p] = s1[lo : lo + n]

    loop(1, 8, lambda d: g1_copy(c_peer(d), c_peer(d)).wait())
    g1[...] = jnp.sum(g1r[...], axis=0)
    loop(1, 8, lambda d: g2_copy(r_peer(d), r).start())
    g2r[r] = g1[...]

    for e in range(2):
        loop(1, 4, lambda d: a_copy(e, q_line(d), ql).start())

    for h in range(2):
        lo, n = CHUNKS[h]
        loop(1, 8, lambda d: s2_copy(h, p_peer(d), p_peer(d)).wait())
        for e in range(lo, lo + n):
            own_k = lax.rem(member(mem, PAIRS[e][0]), 8)
            own_m = lax.rem(member(mem, PAIRS[e][1]), 8)
            s_all[e, rows_of(q + 8 * f), :] = s2r[h][own_k + f * (own_m - own_k), e - lo]
        loop(1, 8, lambda d: s3_copy(h, q_peer(d), q).start())
        sx_copy(h, q, f).start()


    loop(1, 8, lambda d: g2_copy(r_peer(d), r_peer(d)).wait())
    g2[...] = jnp.sum(g2r[...], axis=0)
    g3 = copy(g2, g3r, snd_g3, rcv_g3, sibling)
    g3.start()

    def pass_on(h):
        def one(d):
            s3_copy(h, q_peer(d), q_peer(d)).wait_recv()
            sx_copy(h, q_peer(d), f).start()

        loop(1, 8, one)

    def sx_ready(h):
        loop(0, 8, lambda at: sx_copy(h, at, 1 - f).wait_recv())

    rr = lax.broadcasted_iota(jnp.int32, (BS, BS), 0)
    cc = lax.broadcasted_iota(jnp.int32, (BS, BS), 1)
    low[...] = jnp.zeros_like(low)
    inv[...] = jnp.zeros_like(inv)

    def before(k):
        if k == 0:
            sx_ready(0)
        if k == 2:
            sx_ready(1)
        for m in range(k):
            keep = pat[member(mem, k), member(mem, m)].astype(f32)
            value = s_all[PAIRS.index((k, m))] * keep
            if m:
                value = value - keep * dot_nt(low[k, :, 0 : BS * m], low[m, :, 0 : BS * m])
            low[k, :, BS * m : BS * m + BS] = dot_nt(value, inv[BS * m : BS * m + BS, BS * m : BS * m + BS])
        value = s_all[PAIRS.index((k, k))] * pat[member(mem, k), member(mem, k)].astype(f32)
        value = value + jnp.where(rr == cc, SHIFT, 0.0)
        if k:
            lows = low[k, :, 0 : BS * k]
            value = value - dot_nt(lows, lows)
        cur[...] = value

    def after(k):
        at = slice(BS * k, BS * k + BS)
        inv[at, at] = fac_i[...]
        if k:
            inv[at, 0 : BS * k] = -dot_nn(fac_i[...], dot_nn(low[k, :, 0 : BS * k], inv[0 : BS * k, 0 : BS * k]))
        lower = fac_u[...].T
        low[k, :, at] = lower
        diag[k] = lower
        if k == 0:
            pass_on(1)
            spread_on()
        if k == 2:
            g3.wait()
            g_out[c] = g2[...] + g3r[...]
            loop(1, 8, lambda d: g4_copy(c_peer(d), c).start())

    def owner(k):
        return q_parts(lax.rem(mem[f, k], 8))

    def pick():
        for e in range(2):
            loop(1, 4, lambda d: a_copy(e, q_line(d), q_line(d)).wait())
        for e in range(2):
            for k in range(2):
                picked[e, k] = par[owner(k)[0], e, k]
        b_copy().start()

    def spread_mine():
        b_copy().wait()
        both[qh] = picked[qh]
        both[1 - qh] = other[...]

        @pl.when(f == 0)
        def _():
            for k in range(2):
                mine[k] = both[lax.rem(mem[0, k], 2), k]

        @pl.when(f == 1)
        def _():
            for k in range(2):
                mine[k] = both[lax.rem(mem[1, k], 8) // 4, k].T

        r1_copy(q).start()
        for e in range(2):
            away(p_at(ql, e), p, lambda: t1_copy(e, q).start())
        raw[f, f, q] = mine[...]

        @pl.when(jnp.logical_and(p == q, ql == pl_))
        def _():
            raw[1 - f, f, q] = mine[...]

        x_copy(f, q, f).start()

    def spread_on():
        r1_copy(q_at(ql, 1 - qh)).wait_recv()
        for e in range(2):
            loop(1, 4, lambda d: r2_copy(e, q_line(d), q_at(ql, e)).start())
        for e in range(2):
            at = q_at(pl_, e)
            away(q, at, lambda: t1_copy(e, at).wait_recv())
            loop(1, 4, lambda d: t2_copy(e, p_line(d), at).start())
            x_copy(1 - f, at, f).start()
        x_copy(f, q_at(ql, 1 - qh), f).start()

    def step(k):
        for kk in range(STEPS):
            @pl.when(k == kk)
            def _():
                before(kk)

        upper, inverse = factor_block(cur[...])
        fac_u[...] = upper
        fac_i[...] = inverse
        for kk in range(STEPS):
            @pl.when(k == kk)
            def _():
                after(kk)

    pick()
    pass_on(0)
    spread_mine()
    loop(0, STEPS, step)

    def arrives(d):
        for e in range(2):
            at = q_at(q_line(d), e)
            r2_copy(e, q_line(d), at).wait_recv()
            x_copy(f, at, f).start()
            at = q_at(p_line(d), e)
            t2_copy(e, p_line(d), at).wait_recv()
            x_copy(1 - f, at, f).start()

    loop(1, 4, arrives)

    h, l = split(inv[...])
    wh[...] = h
    wl[...] = l
    half = 2 * BS
    w11 = (wh[0:half, 0:half], wl[0:half, 0:half])
    w21 = (wh[half:, 0:half], wl[half:, 0:half])
    w22 = (wh[half:, half:], wl[half:, half:])

    loop(1, 8, lambda d: g4_copy(c_peer(d), c_peer(d)).wait_recv())
    gp = jnp.concatenate(
        [g_out[member(mem, k) // 8, pl.ds(lax.rem(member(mem, k), 8), 1), :] for k in range(STEPS)], axis=1
    )
    gp = jnp.broadcast_to(gp, (16, WIDE))
    y_out[...] = dot3(split(gp), (wh[...], wl[...]))[0:8]

    def panel(which, t):
        base = r + which * (c - r)
        ones, twos, keeps = [], [], []
        for e in range(2):
            a = 2 * t + e
            x_copy(which, a, 1 - f).wait_recv()
        for e in range(2):
            a = 2 * t + e
            i = 8 * a + base
            pivot = i == member(mem, 0)
            for k in range(1, STEPS):
                pivot = jnp.logical_or(pivot, i == member(mem, k))
            z = jnp.where(pivot, 0.0, 1.0).astype(f32)
            m1 = z * pat[i, member(mem, 0)].astype(f32)
            m2 = z * pat[i, member(mem, 2)].astype(f32)
            ones.append(jnp.concatenate([raw[which, 0, a, 0], raw[which, 0, a, 1]], axis=1) * m1)
            twos.append(jnp.concatenate([raw[which, 1, a, 0], raw[which, 1, a, 1]], axis=1))
            keeps.append(m2)
        one = split(jnp.concatenate(ones, axis=0))
        two = split(jnp.concatenate(twos, axis=0))
        second = dot3(one, w21) + dot3(two, w22)
        rows = pl.ds(pl.multiple_of(half * t, half), half)
        hi, rest = split(dot3(one, w11))
        x_hi[which, rows, 0:half] = hi
        x_lo[which, rows, 0:half] = rest
        second = jnp.concatenate([second[0:BS] * keeps[0], second[BS:half] * keeps[1]], axis=0)
        hi, rest = split(second)
        x_hi[which, rows, half:WIDE] = hi
        x_lo[which, rows, half:WIDE] = rest

    loop(0, 8, lambda t: panel(t // 4, lax.rem(t, 4)))

    def tail(d):
        for h in range(2):
            s3_copy(h, q_peer(d), q).wait_send()
        g4_copy(c_peer(d), c).wait_send()

    loop(1, 8, tail)
    r1_copy(q).wait_send()
    for e in range(2):
        away(p_at(ql, e), p, lambda: t1_copy(e, q).wait_send())

    def tail_line(d):
        for e in range(2):
            r2_copy(e, q_line(d), q_at(ql, e)).wait_send()
            t2_copy(e, p_line(d), q_at(pl_, e)).wait_send()

    loop(1, 4, tail_line)

    def tail_pair(d):
        for h in range(2):
            sx_copy(h, d, f).wait_send()
        for which in range(2):
            x_copy(which, d, f).wait_send()

    loop(0, 8, tail_pair)


def exchange(mem, pat, scand, ccand, pg):
    vmem = pltpu.VMEM
    sem = pltpu.SemaphoreType.DMA
    return pl.pallas_call(
        exchange_kernel,
        out_shape=(
            jax.ShapeDtypeStruct((2, 1024, WIDE), bf16),
            jax.ShapeDtypeStruct((2, 1024, WIDE), bf16),
            jax.ShapeDtypeStruct((STEPS, BS, BS), f32),
            jax.ShapeDtypeStruct((8, WIDE), f32),
            jax.ShapeDtypeStruct((8, 8, BS), f32),
        ),
        in_specs=[SM, SM, VM, VM, VM],
        out_specs=(VM,) * 5,
        scratch_shapes=[
            vmem((NQ, BS, BS), f32),
            vmem((STEPS, BS, WIDE), f32),
            vmem((WIDE, WIDE), f32),
            vmem((BS, BS), f32),
            vmem((BS, BS), f32),
            vmem((BS, BS), f32),
            vmem((2, 2, 8, 2, BS, BS), f32),
            vmem((WIDE, WIDE), bf16),
            vmem((WIDE, WIDE), bf16),
            vmem((8, CHUNKS[0][1], 8, BS), f32),
            vmem((8, CHUNKS[1][1], 8, BS), f32),
            vmem((NQ, 8, BS), f32),
            vmem((8, CHUNKS[0][1], 8, BS), f32),
            vmem((8, CHUNKS[1][1], 8, BS), f32),
            vmem((4, 2, 2, BS, BS), f32),
            vmem((2, 2, BS, BS), f32),
            vmem((2, BS, BS), f32),
            vmem((2, 2, BS, BS), f32),
            vmem((2, BS, BS), f32),
            vmem((8, 8, BS), f32),
            vmem((8, BS), f32),
            vmem((8, 8, BS), f32),
            vmem((8, BS), f32),
            vmem((8, BS), f32),
        ]
        + [sem((2, 8))] * 10
        + [sem((2, 4))] * 4
        + [sem((2,))]
        + [sem((8,))] * 8
        + [sem] * 5,
        compiler_params=pltpu.CompilerParams(
            collective_id=0, has_side_effects=True, vmem_limit_bytes=40 << 20
        ),
        name="exchange",
    )(mem, pat, scand, ccand, pg)


def update_kernel(mem, pat, diag, x_hi, x_lo, y, g, hess, out, grad_out, rows, in_sem, out_sem):
    r = lax.axis_index("prow")
    c = lax.axis_index("pcol")

    def load(a):
        return pltpu.make_async_copy(hess.at[a], rows.at[a], in_sem.at[a])

    def save(a):
        return pltpu.make_async_copy(rows.at[a], out.at[a], out_sem.at[a])

    for a in range(8):
        load(a).start()

    def is_pivot(i):
        pivot = i == member(mem, 0)
        for k in range(1, STEPS):
            pivot = jnp.logical_or(pivot, i == member(mem, k))
        return pivot

    dec = dot3(split(jnp.concatenate([y[...], y[...]], axis=0)), (x_hi[0], x_lo[0]))
    for a in range(8):
        i = 8 * a + r
        val = g[a, pl.ds(r, 1), :] - dec[0:1, BS * a : BS * a + BS]
        for k in range(STEPS):
            val = jnp.where(i == member(mem, k), y[0:1, BS * k : BS * k + BS], val)
        grad_out[a : a + 1, :] = val

    rr = lax.broadcasted_iota(jnp.int32, (BS, BS), 0)
    cc = lax.broadcasted_iota(jnp.int32, (BS, BS), 1)
    shift = jnp.where(rr == cc, SHIFT, 0.0)
    cols = (x_hi[1], x_lo[1])

    def two_rows(t):
        at = pl.ds(pl.multiple_of(2 * BS * t, 2 * BS), 2 * BS)
        upd = dot3((x_hi[0, at, :], x_lo[0, at, :]), cols)
        for e in range(2):
            a = 2 * t + e
            i = 8 * a + r
            live = jnp.where(is_pivot(i), 0.0, 1.0).astype(f32)
            load(a).wait()
            for b in range(8):
                j = 8 * b + c
                keep = live * pat[i, j].astype(f32)
                on = jnp.where(i == j, 1.0, 0.0).astype(f32) * live
                sub = upd[BS * e : BS * e + BS, BS * b : BS * b + BS]
                there = pl.ds(b, BS, stride=8)
                rows[a, there, :] = keep * (rows[a, there, :] - sub) + on * shift
            for k in range(STEPS):
                pk = member(mem, k)

                @pl.when(lax.rem(pk, 8) == c)
                def _():
                    there = pl.ds(pk // 8, BS, stride=8)
                    mine = pl.ds(pl.multiple_of(BS * a, BS), BS)
                    part = slice(BS * k, BS * k + BS)

                    @pl.when(i != pk)
                    def _():
                        rows[a, there, :] = x_hi[0, mine, part].astype(f32) + x_lo[0, mine, part].astype(f32)

                    @pl.when(i == pk)
                    def _():
                        rows[a, there, :] = diag[k]
            save(a).start()

    loop(0, 4, two_rows)
    for a in range(8):
        save(a).wait()


def update(mem, pat, diag, x_hi, x_lo, y, g, hess):
    return pl.pallas_call(
        update_kernel,
        out_shape=(
            jax.ShapeDtypeStruct(hess.shape, f32),
            jax.ShapeDtypeStruct((8, BS), f32),
        ),
        in_specs=[SM, SM, VM, VM, VM, VM, VM, ANY],
        out_specs=(ANY, VM),
        scratch_shapes=[
            pltpu.VMEM((8, 1024, BS), f32),
            pltpu.SemaphoreType.DMA((8,)),
            pltpu.SemaphoreType.DMA((8,)),
        ],
        compiler_params=pltpu.CompilerParams(vmem_limit_bytes=32 << 20),
        name="update",
    )(mem, pat, diag, x_hi, x_lo, y, g, hess)


def shards(
    poses, codebook, offsets, confidence, code_ids, creature_ids, hess_raw, pattern, membership
):
    scand, ccand, pg = prepare(
        membership, hess_raw.reshape(8, BS, 8, 1, BS), poses, codebook, offsets,
        confidence.reshape(16, BS), code_ids.reshape(16, BS), creature_ids.reshape(16, BS),
    )
    x_hi, x_lo, diag, y, g = exchange(membership, pattern, scand, ccand, pg.reshape(8, 8, BS))
    state, grad = update(
        membership, pattern, diag, x_hi, x_lo, y, g, hess_raw.reshape(8, 1024, BS)
    )
    return state.reshape(hess_raw.shape), grad.reshape(8, 1, BS)


def solution(mesh):
    return jax.shard_map(
        shards,
        mesh=mesh,
        in_specs=(
            P(("frames", "prow", "pcol"), None),
            P(),
            P(),
            P(("frames", "prow", "pcol")),
            P(("frames", "prow", "pcol")),
            P(("frames", "prow", "pcol")),
            P(None, "prow", None, None, "pcol", None),
            P(),
            P(),
        ),
        out_specs=(P(None, "prow", None, None, "pcol", None), P(None, "prow", None)),
        check_vma=False,
    )
```

```python
import math

import jax
import jax.numpy as jnp
from jax import lax
from jax.experimental import pallas as pl
from jax.experimental.pallas import tpu as pltpu
from jax.sharding import PartitionSpec as P

NPAN = 8192
BS = 128
STEPS = 4
FRAMES = 262144
CODES = 32
SHIFT = 2.5 * math.sqrt(NPAN)
PAIRS = [(k, m) for k in range(STEPS) for m in range(k + 1)]
NQ = len(PAIRS)
CHUNKS = ((0, 3), (3, 7))
WIDE = STEPS * BS
MESH = pl.DeviceIdType.MESH
precise = lax.Precision.HIGHEST
f32 = jnp.float32
bf16 = jnp.bfloat16
NT = (((1,), (1,)), ((), ()))
NN = (((1,), (0,)), ((), ()))


def loop(lo, hi, fn):
    def body(d, carry):
        fn(d)
        return carry

    lax.fori_loop(lo, hi, body, 0)


def split(x):
    hi = x.astype(bf16)
    return hi, (x - hi.astype(f32)).astype(bf16)


def dot3(a, b):
    (ah, al), (bh, bl) = a, b
    d = lambda x, y: lax.dot_general(x, y, NT, preferred_element_type=f32)
    return d(ah, bh) + (d(ah, bl) + d(al, bh))


def member(mem, k):
    return mem[k // 2, k % 2]


VM = pl.BlockSpec(memory_space=pltpu.VMEM)
SM = pl.BlockSpec(memory_space=pltpu.SMEM)
ANY = pl.BlockSpec(memory_space=pl.ANY)
HBM = pl.BlockSpec(memory_space=pltpu.HBM)


def prepare_kernel(
    mem, hess, poses_at, codebook_at, offsets_at, conf_at, codes_at, kinds_at, scand, ccand, pg,
    poses, codebook, offsets, conf, codes, kinds, sem, in_sem,
):
    fetches = [
        pltpu.make_async_copy(src, dst, in_sem.at[n])
        for n, (src, dst) in enumerate(
            [
                (codes_at, codes), (conf_at, conf), (kinds_at, kinds),
                (poses_at, poses), (codebook_at, codebook), (offsets_at, offsets),
            ]
        )
    ]
    for fetch in fetches:
        fetch.start()
    f = lax.axis_index("frames")
    slot = [member(mem, k) // 8 for k in range(STEPS)]
    copies = [
        pltpu.make_async_copy(hess.at[slot[k], :, slot[m], 0, :], scand.at[q], sem.at[q])
        for q, (k, m) in enumerate(PAIRS)
    ]
    for copy in copies:
        copy.start()
    by_col = [
        pltpu.make_async_copy(hess.at[:, :, slot[k], 0, :], ccand.at[:, k], sem.at[NQ + k])
        for k in range(2)
    ]
    by_row = [
        pltpu.make_async_copy(hess.at[slot[2 + k], :, b, 0, :], ccand.at[b, k], sem.at[NQ + 2 + 8 * k + b])
        for k in range(2)
        for b in range(8)
    ]

    @pl.when(f == 0)
    def _():
        for copy in by_col:
            copy.start()

    @pl.when(f == 1)
    def _():
        for copy in by_row:
            copy.start()

    for fetch in fetches:
        fetch.wait()
    ids = lax.broadcasted_iota(jnp.int32, (CODES, BS), 0)
    weights, marks = [], []
    for s in range(16):
        weights.append(jnp.where(codes[s : s + 1, :] == ids, conf[s : s + 1, :], 0.0))
        marks.append(jnp.where(kinds[s : s + 1, :] == ids, 1.0, 0.0).astype(bf16))
    weight = jnp.concatenate(weights, axis=1)
    mark = jnp.concatenate(marks, axis=1)
    parts = []
    for _ in range(3):
        parts.append(weight.astype(bf16))
        weight = weight - parts[-1].astype(f32)
    stack = jnp.concatenate(parts, axis=0)

    def total(x):
        return x[0:CODES] + (x[CODES : 2 * CODES] + x[2 * CODES : 3 * CODES])

    moment = total(lax.dot_general(stack, poses[...], NN, preferred_element_type=f32))
    pair = total(lax.dot_general(stack, mark, NT, preferred_element_type=f32))
    count = jnp.sum(pair, axis=1, keepdims=True)
    moment = moment - count * codebook[...].astype(f32)
    moment = moment - lax.dot_general(
        pair, offsets[...].astype(f32), NN, precision=precise, preferred_element_type=f32
    )
    moment = moment / math.sqrt(FRAMES / CODES)
    for half in range(2):
        pg[pl.ds(half, CODES, stride=2), :] = moment[:, BS * half : BS * half + BS]

    for copy in copies:
        copy.wait()

    @pl.when(f == 0)
    def _():
        for copy in by_col:
            copy.wait()

    @pl.when(f == 1)
    def _():
        for copy in by_row:
            copy.wait()


def prepare(mem, hess, poses, codebook, offsets, conf, codes, kinds):
    return pl.pallas_call(
        prepare_kernel,
        out_shape=(
            jax.ShapeDtypeStruct((NQ, BS, BS), f32),
            jax.ShapeDtypeStruct((8, 2, BS, BS), f32),
            jax.ShapeDtypeStruct((64, BS), f32),
        ),
        in_specs=[SM] + [HBM] * 7,
        out_specs=(VM, VM, VM),
        scratch_shapes=[pltpu.VMEM(x.shape, x.dtype) for x in (poses, codebook, offsets, conf, codes, kinds)]
        + [pltpu.SemaphoreType.DMA((NQ + 18,)), pltpu.SemaphoreType.DMA((6,))],
        compiler_params=pltpu.CompilerParams(vmem_limit_bytes=24 << 20),
        name="prepare",
    )(mem, hess, poses, codebook, offsets, conf, codes, kinds)


def spread(row):
    return jnp.broadcast_to(row, (8, BS))


def eliminate(upper_ref, inv_ref, first, last):
    groups = BS // 8
    row_ids = lax.broadcasted_iota(jnp.int32, (8, BS), 0)
    upper = {g: upper_ref[8 * g : 8 * g + 8, :] for g in range(first, groups)}
    inv = {g: inv_ref[8 * g : 8 * g + 8, :] for g in range(first, groups)}
    for g in range(first, last):
        k = 8 * g
        v, w = upper[g], inv[g]
        cols = [jnp.broadcast_to(v[:, k + j : k + j + 1], (8, BS)) for j in range(8)]
        rows_v, rows_w, coef = [], [], []
        for j in range(8):
            pivot = spread(cols[j][j : j + 1, :])
            recip = 1.0 / pivot
            rv = spread(v[j : j + 1, :]) * recip
            rw = spread(w[j : j + 1, :]) * recip
            rows_v.append(rv)
            rows_w.append(rw)
            below = jnp.where(row_ids > j, cols[j], 0.0)
            coef.append([None] * 8)
            for t in range(j + 1, 8):
                coef[j][t] = spread(cols[t][j : j + 1, :]) * recip
                cols[t] = cols[t] - below * coef[j][t]
            v = v - below * rv
            w = w - below * rw
        upper[g], inv[g] = v, w
        for h in range(g + 1, groups):
            v, w = upper[h], inv[h]
            cols = [jnp.broadcast_to(v[:, k + j : k + j + 1], (8, BS)) for j in range(8)]
            for j in range(8):
                for t in range(j + 1, 8):
                    cols[t] = cols[t] - cols[j] * coef[j][t]
                v = v - cols[j] * rows_v[j]
                w = w - cols[j] * rows_w[j]
            upper[h], inv[h] = v, w
    for g in range(first, groups):
        upper_ref[8 * g : 8 * g + 8, :] = upper[g]
        inv_ref[8 * g : 8 * g + 8, :] = inv[g]


def dot_nt(a, b):
    return lax.dot_general(a, b, NT, precision=precise, preferred_element_type=f32)


def dot_nn(a, b):
    return lax.dot_general(a, b, (((1,), (0,)), ((), ())), precision=precise, preferred_element_type=f32)


def exchange_kernel(
    mem, pat, scand, ccand, pg,
    x_hi, x_lo, diag, y_out, g_out,
    s_all, low, inv, fac_u, fac_i, raw, wh, wl,
    s1r_a, s1r_b, s1, s2r_a, s2r_b, par_a, par_b, picked, both_a, both_b, mine, g1r, g1, g2r, g2, g3r,
    snd_s1, rcv_s1, snd_s2, rcv_s2, snd_s3, rcv_s3, snd_sx, rcv_sx,
    snd_x, rcv_x, snd_a, rcv_a, snd_r2, snd_t2, snd_t1, rcv_r, rcv_t,
    snd_g1, rcv_g1, snd_g2, rcv_g2, snd_g4, rcv_g4, snd_g3, rcv_g3, snd_b, rcv_b, snd_r1,
):
    s1r, s2r = (s1r_a, s1r_b), (s2r_a, s2r_b)
    par, both = (par_a, par_b), (both_a, both_b)
    f = lax.axis_index("frames")
    r = lax.axis_index("prow")
    c = lax.axis_index("pcol")
    p = r + f * (c - r)
    q = c + f * (r - c)

    def place(p_to, q_to):
        return (f, p_to + f * (q_to - p_to), q_to + f * (p_to - q_to))

    sibling = (1 - f, r, c)

    def q_at(line, pair):
        return 2 * line + pair + f * (3 * pair - line)

    def p_at(line, pair):
        return line + 4 * pair + f * (line - 3 * pair)

    def q_parts(v):
        return v // 2 + f * (lax.rem(v, 4) - v // 2), lax.rem(v, 2) + f * (v // 4 - lax.rem(v, 2))

    def p_parts(v):
        return lax.rem(v, 4) + f * (v // 2 - lax.rem(v, 4)), v // 4 + f * (lax.rem(v, 2) - v // 4)

    ql, qh = q_parts(q)
    pl_, ph = p_parts(p)

    def q_line(d):
        return lax.rem(ql + d, 4)

    def p_line(d):
        return lax.rem(pl_ + d, 4)

    def copy(src, dst, snd, rcv, to):
        return pltpu.make_async_remote_copy(
            src_ref=src, dst_ref=dst, send_sem=snd, recv_sem=rcv, device_id=to, device_id_type=MESH
        )

    def q_peer(d):
        return lax.rem(q + d, 8)

    def p_peer(d):
        return lax.rem(p + d, 8)

    def c_peer(d):
        return lax.rem(c + d, 8)

    def r_peer(d):
        return lax.rem(r + d, 8)

    barrier = pltpu.get_barrier_semaphore()

    def greet(to):
        pl.semaphore_signal(barrier, inc=1, device_id=to, device_id_type=MESH)

    greet(sibling)

    def greet_line(d):
        greet(place(p, q_peer(d)))
        greet(place(p_peer(d), q))

    loop(1, 8, greet_line)

    def at_home(p_to, q_to):
        return jnp.logical_and(p_to == p, q_to == q)

    def away(p_to, q_to, fn):
        @pl.when(jnp.logical_not(at_home(p_to, q_to)))
        def _():
            fn()

    def greet_turn(e):
        away(p_at(ql, e), p, lambda: greet(place(p_at(ql, e), p)))
        away(q, q_at(pl_, e), lambda: greet(place(q, q_at(pl_, e))))

    loop(0, 2, greet_turn)
    same = jnp.where(jnp.logical_and(p == q, ql == pl_), 1, 0)
    pl.semaphore_wait(barrier, 19 - 2 * same)

    def rows_of(slice_id):
        return pl.ds(pl.multiple_of(8 * slice_id, 8), 8)

    def s1_copy(h, peer, at):
        lo, n = CHUNKS[h]
        return copy(
            scand.at[pl.ds(lo, n), rows_of(peer + 8 * f), :], s1r[h].at[at],
            snd_s1.at[h, peer], rcv_s1.at[h, at], place(p, peer),
        )

    def s2_copy(h, peer, at):
        lo, n = CHUNKS[h]
        return copy(
            s1.at[pl.ds(lo, n)], s2r[h].at[at],
            snd_s2.at[h, peer], rcv_s2.at[h, at], place(peer, q),
        )

    def s3_copy(h, peer, at):
        lo, n = CHUNKS[h]
        part = s_all.at[pl.ds(lo, n), rows_of(at + 8 * f), :]
        return copy(part, part, snd_s3.at[h, peer], rcv_s3.at[h, at], place(p, peer))

    def sx_copy(h, at, core):
        lo, n = CHUNKS[h]
        part = s_all.at[pl.ds(lo, n), rows_of(at + 8 * core), :]
        return copy(part, part, snd_sx.at[h, at], rcv_sx.at[h, at], sibling)

    def g1_copy(peer, at):
        return copy(pg.at[peer], g1r.at[at], snd_g1.at[peer], rcv_g1.at[at], (f, r, peer))

    def g2_copy(peer, at):
        return copy(g1, g2r.at[at], snd_g2.at[peer], rcv_g2.at[at], (f, peer, c))

    def g4_copy(peer, at):
        return copy(g_out.at[at], g_out.at[at], snd_g4.at[peer], rcv_g4.at[at], (f, r, peer))

    def a_copy(k, e, line, at):
        return copy(
            ccand.at[q_at(line, e), k], par[k].at[at, e],
            snd_a.at[2 * k + e, line], rcv_a.at[2 * k + e, at], place(p, q_at(line, qh)),
        )

    def b_copy(k):
        return copy(
            picked.at[k, 1 - qh], both[k].at[qh], snd_b.at[k], rcv_b.at[k], place(p, q_at(ql, 1 - qh))
        )

    def r1_copy(k, at):
        return copy(
            mine.at[k], raw.at[f, f, at, k], snd_r1.at[k], rcv_r.at[k, at], place(p, q_at(ql, 1 - qh))
        )

    def r2_copy(k, e, line, at):
        part = raw.at[f, f, at, k]
        return copy(part, part, snd_r2.at[2 * k + e, line], rcv_r.at[k, at], place(p, q_at(line, qh)))

    def t1_copy(k, e, at):
        return copy(
            mine.at[k], raw.at[1 - f, f, at, k], snd_t1.at[k, e], rcv_t.at[k, at], place(p_at(ql, e), p)
        )

    def t2_copy(k, e, line, at):
        part = raw.at[1 - f, f, at, k]
        return copy(part, part, snd_t2.at[2 * k + e, line], rcv_t.at[k, at], place(p_at(line, ph), q))

    def x_copy(which, at, core):
        part = raw.at[which, core, at]
        return copy(part, part, snd_x.at[which, at], rcv_x.at[which, at], sibling)

    def owner(k):
        return q_parts(lax.rem(mem[f, k], 8))

    def pick(k):
        for e in range(2):
            loop(1, 4, lambda d: a_copy(k, e, q_line(d), q_line(d)).wait())
        for e in range(2):
            picked[k, e] = par[k][owner(k)[0], e]
        b_copy(k).start()

    def spread_mine(k):
        both[k][qh] = picked[k, qh]
        b_copy(k).wait()

        @pl.when(f == 0)
        def _():
            mine[k] = both[k][lax.rem(mem[0, k], 2)]

        @pl.when(f == 1)
        def _():
            mine[k] = both[k][lax.rem(mem[1, k], 8) // 4].T

        r1_copy(k, q).start()
        for e in range(2):
            away(p_at(ql, e), p, lambda: t1_copy(k, e, q).start())
        raw[f, f, q, k] = mine[k]

        @pl.when(jnp.logical_and(p == q, ql == pl_))
        def _():
            raw[1 - f, f, q, k] = mine[k]

    def spread_on(k):
        r1_copy(k, q_at(ql, 1 - qh)).wait_recv()
        for e in range(2):
            loop(1, 4, lambda d: r2_copy(k, e, q_line(d), q_at(ql, e)).start())
        for e in range(2):
            at = q_at(pl_, e)
            away(q, at, lambda: t1_copy(k, e, at).wait_recv())
            loop(1, 4, lambda d: t2_copy(k, e, p_line(d), at).start())
        if k:
            for e in range(2):
                x_copy(f, q_at(ql, e), f).start()
                x_copy(1 - f, q_at(pl_, e), f).start()

    for h in range(2):
        loop(1, 8, lambda d: s1_copy(h, q_peer(d), q).start())
    loop(1, 8, lambda d: g1_copy(c_peer(d), c).start())
    for h, (lo, n) in enumerate(CHUNKS):
        s1r[h][q] = scand[lo : lo + n, rows_of(q + 8 * f), :]
    g1r[c] = pg[c]
    for e in range(2):
        for k in range(2):
            par[k][ql, e] = ccand[q_at(ql, e), k]

    for h in range(2):
        lo, n = CHUNKS[h]
        loop(1, 8, lambda d: s1_copy(h, q_peer(d), q_peer(d)).wait())
        for e in range(lo, lo + n):
            own_k = lax.rem(member(mem, PAIRS[e][0]), 8)
            own_m = lax.rem(member(mem, PAIRS[e][1]), 8)
            s1[e] = s1r[h][own_m + f * (own_k - own_m), e - lo]
        loop(1, 8, lambda d: s2_copy(h, p_peer(d), p).start())
        s2r[h][p] = s1[lo : lo + n]

    loop(1, 8, lambda d: g1_copy(c_peer(d), c_peer(d)).wait())
    g1[...] = jnp.sum(g1r[...], axis=0)
    loop(1, 8, lambda d: g2_copy(r_peer(d), r).start())
    g2r[r] = g1[...]

    for k in range(2):
        for e in range(2):
            loop(1, 4, lambda d: a_copy(k, e, q_line(d), ql).start())

    pick(0)
    for h in range(2):
        lo, n = CHUNKS[h]
        loop(1, 8, lambda d: s2_copy(h, p_peer(d), p_peer(d)).wait())
        for e in range(lo, lo + n):
            own_k = lax.rem(member(mem, PAIRS[e][0]), 8)
            own_m = lax.rem(member(mem, PAIRS[e][1]), 8)
            s_all[e, rows_of(q + 8 * f), :] = s2r[h][own_k + f * (own_m - own_k), e - lo]
        loop(1, 8, lambda d: s3_copy(h, q_peer(d), q).start())
        sx_copy(h, q, f).start()
        pick(1) if h == 0 else spread_mine(0)


    loop(1, 8, lambda d: g2_copy(r_peer(d), r_peer(d)).wait())
    g2[...] = jnp.sum(g2r[...], axis=0)
    g3 = copy(g2, g3r, snd_g3, rcv_g3, sibling)
    g3.start()

    def pass_on(h):
        def one(d):
            s3_copy(h, q_peer(d), q_peer(d)).wait_recv()
            sx_copy(h, q_peer(d), f).start()

        loop(1, 8, one)

    def sx_ready(h):
        loop(0, 8, lambda at: sx_copy(h, at, 1 - f).wait_recv())

    rr = lax.broadcasted_iota(jnp.int32, (BS, BS), 0)
    cc = lax.broadcasted_iota(jnp.int32, (BS, BS), 1)
    low[...] = jnp.zeros_like(low)
    inv[...] = jnp.zeros_like(inv)

    def before(k):
        if k == 0:
            sx_ready(0)
        if k == 2:
            sx_ready(1)
        for m in range(k):
            keep = pat[member(mem, k), member(mem, m)].astype(f32)
            value = s_all[PAIRS.index((k, m))] * keep
            if m:
                value = value - keep * dot_nt(low[k, :, 0 : BS * m], low[m, :, 0 : BS * m])
            low[k, :, BS * m : BS * m + BS] = dot_nt(value, inv[BS * m : BS * m + BS, BS * m : BS * m + BS])
        value = s_all[PAIRS.index((k, k))] * pat[member(mem, k), member(mem, k)].astype(f32)
        value = value + jnp.where(rr == cc, SHIFT, 0.0)
        if k:
            lows = low[k, :, 0 : BS * k]
            value = value - dot_nt(lows, lows)
        fac_u[...] = value
        fac_i[...] = jnp.where(rr == cc, 1.0, 0.0)

    def after(k):
        at = slice(BS * k, BS * k + BS)
        inv[at, at] = fac_i[...]
        if k:
            inv[at, 0 : BS * k] = -dot_nn(fac_i[...], dot_nn(low[k, :, 0 : BS * k], inv[0 : BS * k, 0 : BS * k]))
        lower = fac_u[...].T
        low[k, :, at] = lower
        diag[k] = lower
        if k == 0:
            pass_on(1)
            spread_on(1)
        if k == 2:
            g3.wait()
            g_out[c] = g2[...] + g3r[...]
            loop(1, 8, lambda d: g4_copy(c_peer(d), c).start())

    def step(k):
        for kk in range(STEPS):
            @pl.when(k == kk)
            def _():
                before(kk)

        eliminate(fac_u, fac_i, 0, 8)

        @pl.when(k == 0)
        def _():
            spread_on(0)

        eliminate(fac_u, fac_i, 8, 16)
        pivots = jnp.sum(jnp.where(rr == cc, fac_u[...], 0.0), axis=1, keepdims=True)
        scale = 1.0 / jnp.sqrt(pivots)
        fac_u[...] = jnp.where(cc >= rr, fac_u[...] * scale, 0.0)
        fac_i[...] = fac_i[...] * scale
        for kk in range(STEPS):
            @pl.when(k == kk)
            def _():
                after(kk)

    pass_on(0)
    spread_mine(1)
    loop(0, STEPS, step)

    def arrives(d):
        for e in range(2):
            at = q_at(q_line(d), e)
            for k in range(2):
                r2_copy(k, e, q_line(d), at).wait_recv()
            x_copy(f, at, f).start()
            at = q_at(p_line(d), e)
            for k in range(2):
                t2_copy(k, e, p_line(d), at).wait_recv()
            x_copy(1 - f, at, f).start()

    loop(1, 4, arrives)

    h, l = split(inv[...])
    wh[...] = h
    wl[...] = l
    half = 2 * BS
    w11 = (wh[0:half, 0:half], wl[0:half, 0:half])
    w21 = (wh[half:, 0:half], wl[half:, 0:half])
    w22 = (wh[half:, half:], wl[half:, half:])

    loop(1, 8, lambda d: g4_copy(c_peer(d), c_peer(d)).wait_recv())
    gp = jnp.concatenate(
        [g_out[member(mem, k) // 8, pl.ds(lax.rem(member(mem, k), 8), 1), :] for k in range(STEPS)], axis=1
    )
    gp = jnp.broadcast_to(gp, (16, WIDE))
    y_out[...] = dot3(split(gp), (wh[...], wl[...]))[0:8]

    def panel(which, t):
        base = r + which * (c - r)
        ones, twos, keeps = [], [], []
        for e in range(2):
            a = 2 * t + e
            x_copy(which, a, 1 - f).wait_recv()
        for e in range(2):
            a = 2 * t + e
            i = 8 * a + base
            pivot = i == member(mem, 0)
            for k in range(1, STEPS):
                pivot = jnp.logical_or(pivot, i == member(mem, k))
            z = jnp.where(pivot, 0.0, 1.0).astype(f32)
            m1 = z * pat[i, member(mem, 0)].astype(f32)
            m2 = z * pat[i, member(mem, 2)].astype(f32)
            ones.append(jnp.concatenate([raw[which, 0, a, 0], raw[which, 0, a, 1]], axis=1) * m1)
            twos.append(jnp.concatenate([raw[which, 1, a, 0], raw[which, 1, a, 1]], axis=1))
            keeps.append(m2)
        one = split(jnp.concatenate(ones, axis=0))
        two = split(jnp.concatenate(twos, axis=0))
        second = dot3(one, w21) + dot3(two, w22)
        rows = pl.ds(pl.multiple_of(half * t, half), half)
        hi, rest = split(dot3(one, w11))
        x_hi[which, rows, 0:half] = hi
        x_lo[which, rows, 0:half] = rest
        second = jnp.concatenate([second[0:BS] * keeps[0], second[BS:half] * keeps[1]], axis=0)
        hi, rest = split(second)
        x_hi[which, rows, half:WIDE] = hi
        x_lo[which, rows, half:WIDE] = rest

    loop(0, 8, lambda t: panel(t // 4, lax.rem(t, 4)))

    def tail(d):
        for h in range(2):
            s3_copy(h, q_peer(d), q).wait_send()
        g4_copy(c_peer(d), c).wait_send()

    loop(1, 8, tail)
    for k in range(2):
        r1_copy(k, q).wait_send()
        for e in range(2):
            away(p_at(ql, e), p, lambda: t1_copy(k, e, q).wait_send())

    def tail_line(d):
        for k in range(2):
            for e in range(2):
                r2_copy(k, e, q_line(d), q_at(ql, e)).wait_send()
                t2_copy(k, e, p_line(d), q_at(pl_, e)).wait_send()

    loop(1, 4, tail_line)

    def tail_pair(d):
        for h in range(2):
            sx_copy(h, d, f).wait_send()
        for which in range(2):
            x_copy(which, d, f).wait_send()

    loop(0, 8, tail_pair)


def exchange(mem, pat, scand, ccand, pg):
    vmem = pltpu.VMEM
    sem = pltpu.SemaphoreType.DMA
    return pl.pallas_call(
        exchange_kernel,
        out_shape=(
            jax.ShapeDtypeStruct((2, 1024, WIDE), bf16),
            jax.ShapeDtypeStruct((2, 1024, WIDE), bf16),
            jax.ShapeDtypeStruct((STEPS, BS, BS), f32),
            jax.ShapeDtypeStruct((8, WIDE), f32),
            jax.ShapeDtypeStruct((8, 8, BS), f32),
        ),
        in_specs=[SM, SM, VM, VM, VM],
        out_specs=(VM,) * 5,
        scratch_shapes=[
            vmem((NQ, BS, BS), f32),
            vmem((STEPS, BS, WIDE), f32),
            vmem((WIDE, WIDE), f32),
            vmem((BS, BS), f32),
            vmem((BS, BS), f32),
            vmem((2, 2, 8, 2, BS, BS), f32),
            vmem((WIDE, WIDE), bf16),
            vmem((WIDE, WIDE), bf16),
            vmem((8, CHUNKS[0][1], 8, BS), f32),
            vmem((8, CHUNKS[1][1], 8, BS), f32),
            vmem((NQ, 8, BS), f32),
            vmem((8, CHUNKS[0][1], 8, BS), f32),
            vmem((8, CHUNKS[1][1], 8, BS), f32),
            vmem((4, 2, BS, BS), f32),
            vmem((4, 2, BS, BS), f32),
            vmem((2, 2, BS, BS), f32),
            vmem((2, BS, BS), f32),
            vmem((2, BS, BS), f32),
            vmem((2, BS, BS), f32),
            vmem((8, 8, BS), f32),
            vmem((8, BS), f32),
            vmem((8, 8, BS), f32),
            vmem((8, BS), f32),
            vmem((8, BS), f32),
        ]
        + [sem((2, 8))] * 10
        + [sem((4, 4))] * 4
        + [sem((2, 2))]
        + [sem((2, 8))] * 2
        + [sem((8,))] * 6
        + [sem] * 2
        + [sem((2,))] * 3,
        compiler_params=pltpu.CompilerParams(
            collective_id=0, has_side_effects=True, vmem_limit_bytes=40 << 20
        ),
        name="exchange",
    )(mem, pat, scand, ccand, pg)


def update_kernel(mem, pat, diag, x_hi, x_lo, y, g, hess, out, grad_out, rows, in_sem, out_sem):
    r = lax.axis_index("prow")
    c = lax.axis_index("pcol")

    def load(a):
        return pltpu.make_async_copy(hess.at[a], rows.at[a], in_sem.at[a])

    def save(a):
        return pltpu.make_async_copy(rows.at[a], out.at[a], out_sem.at[a])

    for a in range(8):
        load(a).start()

    def is_pivot(i):
        pivot = i == member(mem, 0)
        for k in range(1, STEPS):
            pivot = jnp.logical_or(pivot, i == member(mem, k))
        return pivot

    dec = dot3(split(jnp.concatenate([y[...], y[...]], axis=0)), (x_hi[0], x_lo[0]))
    for a in range(8):
        i = 8 * a + r
        val = g[a, pl.ds(r, 1), :] - dec[0:1, BS * a : BS * a + BS]
        for k in range(STEPS):
            val = jnp.where(i == member(mem, k), y[0:1, BS * k : BS * k + BS], val)
        grad_out[a : a + 1, :] = val

    rr = lax.broadcasted_iota(jnp.int32, (BS, BS), 0)
    cc = lax.broadcasted_iota(jnp.int32, (BS, BS), 1)
    shift = jnp.where(rr == cc, SHIFT, 0.0)
    cols = (x_hi[1], x_lo[1])

    def two_rows(t):
        at = pl.ds(pl.multiple_of(2 * BS * t, 2 * BS), 2 * BS)
        upd = dot3((x_hi[0, at, :], x_lo[0, at, :]), cols)
        for e in range(2):
            a = 2 * t + e
            i = 8 * a + r
            live = jnp.where(is_pivot(i), 0.0, 1.0).astype(f32)
            load(a).wait()
            for b in range(8):
                j = 8 * b + c
                keep = live * pat[i, j].astype(f32)
                on = jnp.where(i == j, 1.0, 0.0).astype(f32) * live
                sub = upd[BS * e : BS * e + BS, BS * b : BS * b + BS]
                there = pl.ds(b, BS, stride=8)
                rows[a, there, :] = keep * (rows[a, there, :] - sub) + on * shift
            for k in range(STEPS):
                pk = member(mem, k)

                @pl.when(lax.rem(pk, 8) == c)
                def _():
                    there = pl.ds(pk // 8, BS, stride=8)
                    mine = pl.ds(pl.multiple_of(BS * a, BS), BS)
                    part = slice(BS * k, BS * k + BS)

                    @pl.when(i != pk)
                    def _():
                        rows[a, there, :] = x_hi[0, mine, part].astype(f32) + x_lo[0, mine, part].astype(f32)

                    @pl.when(i == pk)
                    def _():
                        rows[a, there, :] = diag[k]
            save(a).start()

    loop(0, 4, two_rows)
    for a in range(8):
        save(a).wait()


def update(mem, pat, diag, x_hi, x_lo, y, g, hess):
    return pl.pallas_call(
        update_kernel,
        out_shape=(
            jax.ShapeDtypeStruct(hess.shape, f32),
            jax.ShapeDtypeStruct((8, BS), f32),
        ),
        in_specs=[SM, SM, VM, VM, VM, VM, VM, ANY],
        out_specs=(ANY, VM),
        scratch_shapes=[
            pltpu.VMEM((8, 1024, BS), f32),
            pltpu.SemaphoreType.DMA((8,)),
            pltpu.SemaphoreType.DMA((8,)),
        ],
        compiler_params=pltpu.CompilerParams(vmem_limit_bytes=32 << 20),
        name="update",
    )(mem, pat, diag, x_hi, x_lo, y, g, hess)


def shards(
    poses, codebook, offsets, confidence, code_ids, creature_ids, hess_raw, pattern, membership
):
    scand, ccand, pg = prepare(
        membership, hess_raw.reshape(8, BS, 8, 1, BS), poses, codebook, offsets,
        confidence.reshape(16, BS), code_ids.reshape(16, BS), creature_ids.reshape(16, BS),
    )
    x_hi, x_lo, diag, y, g = exchange(membership, pattern, scand, ccand, pg.reshape(8, 8, BS))
    state, grad = update(
        membership, pattern, diag, x_hi, x_lo, y, g, hess_raw.reshape(8, 1024, BS)
    )
    return state.reshape(hess_raw.shape), grad.reshape(8, 1, BS)


def solution(mesh):
    return jax.shard_map(
        shards,
        mesh=mesh,
        in_specs=(
            P(("frames", "prow", "pcol"), None),
            P(),
            P(),
            P(("frames", "prow", "pcol")),
            P(("frames", "prow", "pcol")),
            P(("frames", "prow", "pcol")),
            P(None, "prow", None, None, "pcol", None),
            P(),
            P(),
        ),
        out_specs=(P(None, "prow", None, None, "pcol", None), P(None, "prow", None)),
        check_vma=False,
    )
```

```python
import math

import jax
import jax.numpy as jnp
from jax import lax
from jax.experimental import pallas as pl
from jax.experimental.pallas import tpu as pltpu
from jax.sharding import PartitionSpec as P

NPAN = 8192
BS = 128
STEPS = 4
FRAMES = 262144
CODES = 32
SHIFT = 2.5 * math.sqrt(NPAN)
PAIRS = [(k, m) for k in range(STEPS) for m in range(k + 1)]
NQ = len(PAIRS)
CHUNKS = ((0, 3), (3, 7))
WIDE = STEPS * BS
MESH = pl.DeviceIdType.MESH
precise = lax.Precision.HIGHEST
f32 = jnp.float32
bf16 = jnp.bfloat16
NT = (((1,), (1,)), ((), ()))
NN = (((1,), (0,)), ((), ()))


def loop(lo, hi, fn):
    def body(d, carry):
        fn(d)
        return carry

    lax.fori_loop(lo, hi, body, 0)


def split(x):
    hi = x.astype(bf16)
    return hi, (x - hi.astype(f32)).astype(bf16)


def dot3(a, b):
    (ah, al), (bh, bl) = a, b
    d = lambda x, y: lax.dot_general(x, y, NT, preferred_element_type=f32)
    return d(ah, bh) + (d(ah, bl) + d(al, bh))


def member(mem, k):
    return mem[k // 2, k % 2]


VM = pl.BlockSpec(memory_space=pltpu.VMEM)
SM = pl.BlockSpec(memory_space=pltpu.SMEM)
ANY = pl.BlockSpec(memory_space=pl.ANY)
HBM = pl.BlockSpec(memory_space=pltpu.HBM)


def prepare_kernel(
    mem, hess, poses_at, codebook_at, offsets_at, conf_at, codes_at, kinds_at, scand, ccand, pg,
    poses, codebook, offsets, conf, codes, kinds, sem, in_sem,
):
    fetches = [
        pltpu.make_async_copy(src, dst, in_sem.at[n])
        for n, (src, dst) in enumerate(
            [
                (codes_at, codes), (conf_at, conf), (kinds_at, kinds),
                (poses_at, poses), (codebook_at, codebook), (offsets_at, offsets),
            ]
        )
    ]
    for fetch in fetches:
        fetch.start()
    f = lax.axis_index("frames")
    slot = [member(mem, k) // 8 for k in range(STEPS)]
    copies = [
        pltpu.make_async_copy(hess.at[slot[k], :, slot[m], 0, :], scand.at[q], sem.at[q])
        for q, (k, m) in enumerate(PAIRS)
    ]
    for copy in copies:
        copy.start()
    by_col = [
        pltpu.make_async_copy(hess.at[:, :, slot[k], 0, :], ccand.at[:, k], sem.at[NQ + k])
        for k in range(2)
    ]
    by_row = [
        pltpu.make_async_copy(hess.at[slot[2 + k], :, b, 0, :], ccand.at[b, k], sem.at[NQ + 2 + 8 * k + b])
        for k in range(2)
        for b in range(8)
    ]

    @pl.when(f == 0)
    def _():
        for copy in by_col:
            copy.start()

    @pl.when(f == 1)
    def _():
        for copy in by_row:
            copy.start()

    for fetch in fetches:
        fetch.wait()
    ids = lax.broadcasted_iota(jnp.int32, (CODES, BS), 0)
    weights, marks = [], []
    for s in range(16):
        weights.append(jnp.where(codes[s : s + 1, :] == ids, conf[s : s + 1, :], 0.0))
        marks.append(jnp.where(kinds[s : s + 1, :] == ids, 1.0, 0.0).astype(bf16))
    weight = jnp.concatenate(weights, axis=1)
    mark = jnp.concatenate(marks, axis=1)
    parts = []
    for _ in range(3):
        parts.append(weight.astype(bf16))
        weight = weight - parts[-1].astype(f32)
    stack = jnp.concatenate(parts, axis=0)

    def total(x):
        return x[0:CODES] + (x[CODES : 2 * CODES] + x[2 * CODES : 3 * CODES])

    moment = total(lax.dot_general(stack, poses[...], NN, preferred_element_type=f32))
    pair = total(lax.dot_general(stack, mark, NT, preferred_element_type=f32))
    count = jnp.sum(pair, axis=1, keepdims=True)
    moment = moment - count * codebook[...].astype(f32)
    moment = moment - lax.dot_general(
        pair, offsets[...].astype(f32), NN, precision=precise, preferred_element_type=f32
    )
    moment = moment / math.sqrt(FRAMES / CODES)
    for half in range(2):
        pg[pl.ds(half, CODES, stride=2), :] = moment[:, BS * half : BS * half + BS]

    for copy in copies:
        copy.wait()

    @pl.when(f == 0)
    def _():
        for copy in by_col:
            copy.wait()

    @pl.when(f == 1)
    def _():
        for copy in by_row:
            copy.wait()


def prepare(mem, hess, poses, codebook, offsets, conf, codes, kinds):
    return pl.pallas_call(
        prepare_kernel,
        out_shape=(
            jax.ShapeDtypeStruct((NQ, BS, BS), f32),
            jax.ShapeDtypeStruct((8, 2, BS, BS), f32),
            jax.ShapeDtypeStruct((64, BS), f32),
        ),
        in_specs=[SM] + [HBM] * 7,
        out_specs=(VM, VM, VM),
        scratch_shapes=[pltpu.VMEM(x.shape, x.dtype) for x in (poses, codebook, offsets, conf, codes, kinds)]
        + [pltpu.SemaphoreType.DMA((NQ + 18,)), pltpu.SemaphoreType.DMA((6,))],
        compiler_params=pltpu.CompilerParams(vmem_limit_bytes=24 << 20),
        name="prepare",
    )(
        mem,
        *(
            pltpu.with_memory_space_constraint(x, pltpu.HBM)
            for x in (hess, poses, codebook, offsets, conf, codes, kinds)
        ),
    )


def spread(row):
    return jnp.broadcast_to(row, (8, BS))


def eliminate(upper_ref, inv_ref, first, last):
    groups = BS // 8
    row_ids = lax.broadcasted_iota(jnp.int32, (8, BS), 0)
    upper = {g: upper_ref[8 * g : 8 * g + 8, :] for g in range(first, groups)}
    inv = {g: inv_ref[8 * g : 8 * g + 8, :] for g in range(first, groups)}
    for g in range(first, last):
        k = 8 * g
        v, w = upper[g], inv[g]
        cols = [jnp.broadcast_to(v[:, k + j : k + j + 1], (8, BS)) for j in range(8)]
        rows_v, rows_w, coef = [], [], []
        for j in range(8):
            pivot = spread(cols[j][j : j + 1, :])
            recip = 1.0 / pivot
            rv = spread(v[j : j + 1, :]) * recip
            rw = spread(w[j : j + 1, :]) * recip
            rows_v.append(rv)
            rows_w.append(rw)
            below = jnp.where(row_ids > j, cols[j], 0.0)
            coef.append([None] * 8)
            for t in range(j + 1, 8):
                coef[j][t] = spread(cols[t][j : j + 1, :]) * recip
                cols[t] = cols[t] - below * coef[j][t]
            v = v - below * rv
            w = w - below * rw
        upper[g], inv[g] = v, w
        for h in range(g + 1, groups):
            v, w = upper[h], inv[h]
            cols = [jnp.broadcast_to(v[:, k + j : k + j + 1], (8, BS)) for j in range(8)]
            for j in range(8):
                for t in range(j + 1, 8):
                    cols[t] = cols[t] - cols[j] * coef[j][t]
                v = v - cols[j] * rows_v[j]
                w = w - cols[j] * rows_w[j]
            upper[h], inv[h] = v, w
    for g in range(first, groups):
        upper_ref[8 * g : 8 * g + 8, :] = upper[g]
        inv_ref[8 * g : 8 * g + 8, :] = inv[g]


def dot_nt(a, b):
    return lax.dot_general(a, b, NT, precision=precise, preferred_element_type=f32)


def dot_nn(a, b):
    return lax.dot_general(a, b, (((1,), (0,)), ((), ())), precision=precise, preferred_element_type=f32)


def exchange_kernel(
    mem, pat, scand, ccand, pg,
    x_hi, x_lo, diag, y_out, g_out,
    s_all, low, inv, fac_u, fac_i, raw, wh, wl,
    s1r_a, s1r_b, s1, s2r_a, s2r_b, par_a, par_b, picked, both_a, both_b, mine, g1r, g1, g2r, g2, g3r,
    snd_s1, rcv_s1, snd_s2, rcv_s2, snd_s3, rcv_s3, snd_sx, rcv_sx,
    snd_x, rcv_x, snd_a, rcv_a, snd_r2, snd_t2, snd_t1, rcv_r, rcv_t,
    snd_g1, rcv_g1, snd_g2, rcv_g2, snd_g4, rcv_g4, snd_g3, rcv_g3, snd_b, rcv_b, snd_r1,
):
    s1r, s2r = (s1r_a, s1r_b), (s2r_a, s2r_b)
    par, both = (par_a, par_b), (both_a, both_b)
    f = lax.axis_index("frames")
    r = lax.axis_index("prow")
    c = lax.axis_index("pcol")
    p = r + f * (c - r)
    q = c + f * (r - c)

    def place(p_to, q_to):
        return (f, p_to + f * (q_to - p_to), q_to + f * (p_to - q_to))

    sibling = (1 - f, r, c)

    def q_at(line, pair):
        return 2 * line + pair + f * (3 * pair - line)

    def p_at(line, pair):
        return line + 4 * pair + f * (line - 3 * pair)

    def q_parts(v):
        return v // 2 + f * (lax.rem(v, 4) - v // 2), lax.rem(v, 2) + f * (v // 4 - lax.rem(v, 2))

    def p_parts(v):
        return lax.rem(v, 4) + f * (v // 2 - lax.rem(v, 4)), v // 4 + f * (lax.rem(v, 2) - v // 4)

    ql, qh = q_parts(q)
    pl_, ph = p_parts(p)

    def q_line(d):
        return lax.rem(ql + d, 4)

    def p_line(d):
        return lax.rem(pl_ + d, 4)

    def copy(src, dst, snd, rcv, to):
        return pltpu.make_async_remote_copy(
            src_ref=src, dst_ref=dst, send_sem=snd, recv_sem=rcv, device_id=to, device_id_type=MESH
        )

    def q_peer(d):
        return lax.rem(q + d, 8)

    def p_peer(d):
        return lax.rem(p + d, 8)

    def c_peer(d):
        return lax.rem(c + d, 8)

    def r_peer(d):
        return lax.rem(r + d, 8)

    barrier = pltpu.get_barrier_semaphore()

    def greet(to):
        pl.semaphore_signal(barrier, inc=1, device_id=to, device_id_type=MESH)

    greet(sibling)

    def greet_line(d):
        greet(place(p, q_peer(d)))
        greet(place(p_peer(d), q))

    loop(1, 8, greet_line)

    def at_home(p_to, q_to):
        return jnp.logical_and(p_to == p, q_to == q)

    def away(p_to, q_to, fn):
        @pl.when(jnp.logical_not(at_home(p_to, q_to)))
        def _():
            fn()

    def greet_turn(e):
        away(p_at(ql, e), p, lambda: greet(place(p_at(ql, e), p)))
        away(q, q_at(pl_, e), lambda: greet(place(q, q_at(pl_, e))))

    loop(0, 2, greet_turn)
    same = jnp.where(jnp.logical_and(p == q, ql == pl_), 1, 0)
    pl.semaphore_wait(barrier, 19 - 2 * same)

    def rows_of(slice_id):
        return pl.ds(pl.multiple_of(8 * slice_id, 8), 8)

    def s1_copy(h, peer, at):
        lo, n = CHUNKS[h]
        return copy(
            scand.at[pl.ds(lo, n), rows_of(peer + 8 * f), :], s1r[h].at[at],
            snd_s1.at[h, peer], rcv_s1.at[h, at], place(p, peer),
        )

    def s2_copy(h, peer, at):
        lo, n = CHUNKS[h]
        return copy(
            s1.at[pl.ds(lo, n)], s2r[h].at[at],
            snd_s2.at[h, peer], rcv_s2.at[h, at], place(peer, q),
        )

    def s3_copy(h, peer, at):
        lo, n = CHUNKS[h]
        part = s_all.at[pl.ds(lo, n), rows_of(at + 8 * f), :]
        return copy(part, part, snd_s3.at[h, peer], rcv_s3.at[h, at], place(p, peer))

    def sx_copy(h, at, core):
        lo, n = CHUNKS[h]
        part = s_all.at[pl.ds(lo, n), rows_of(at + 8 * core), :]
        return copy(part, part, snd_sx.at[h, at], rcv_sx.at[h, at], sibling)

    def g1_copy(peer, at):
        return copy(pg.at[peer], g1r.at[at], snd_g1.at[peer], rcv_g1.at[at], (f, r, peer))

    def g2_copy(peer, at):
        return copy(g1, g2r.at[at], snd_g2.at[peer], rcv_g2.at[at], (f, peer, c))

    def g4_copy(peer, at):
        return copy(g_out.at[at], g_out.at[at], snd_g4.at[peer], rcv_g4.at[at], (f, r, peer))

    def a_copy(k, e, line, at):
        return copy(
            ccand.at[q_at(line, e), k], par[k].at[at, e],
            snd_a.at[2 * k + e, line], rcv_a.at[2 * k + e, at], place(p, q_at(line, qh)),
        )

    def b_copy(k):
        return copy(
            picked.at[k, 1 - qh], both[k].at[qh], snd_b.at[k], rcv_b.at[k], place(p, q_at(ql, 1 - qh))
        )

    def r1_copy(k, at):
        return copy(
            mine.at[k], raw.at[f, f, at, k], snd_r1.at[k], rcv_r.at[k, at], place(p, q_at(ql, 1 - qh))
        )

    def r2_copy(k, e, line, at):
        part = raw.at[f, f, at, k]
        return copy(part, part, snd_r2.at[2 * k + e, line], rcv_r.at[k, at], place(p, q_at(line, qh)))

    def t1_copy(k, e, at):
        return copy(
            mine.at[k], raw.at[1 - f, f, at, k], snd_t1.at[k, e], rcv_t.at[k, at], place(p_at(ql, e), p)
        )

    def t2_copy(k, e, line, at):
        part = raw.at[1 - f, f, at, k]
        return copy(part, part, snd_t2.at[2 * k + e, line], rcv_t.at[k, at], place(p_at(line, ph), q))

    def x_copy(which, at, core):
        part = raw.at[which, core, at]
        return copy(part, part, snd_x.at[which, at], rcv_x.at[which, at], sibling)

    def owner(k):
        return q_parts(lax.rem(mem[f, k], 8))

    def pick(k):
        for e in range(2):
            loop(1, 4, lambda d: a_copy(k, e, q_line(d), q_line(d)).wait())
        for e in range(2):
            picked[k, e] = par[k][owner(k)[0], e]
        b_copy(k).start()

    def spread_mine(k):
        both[k][qh] = picked[k, qh]
        b_copy(k).wait()

        @pl.when(f == 0)
        def _():
            mine[k] = both[k][lax.rem(mem[0, k], 2)]

        @pl.when(f == 1)
        def _():
            mine[k] = both[k][lax.rem(mem[1, k], 8) // 4].T

        r1_copy(k, q).start()
        for e in range(2):
            away(p_at(ql, e), p, lambda: t1_copy(k, e, q).start())
        raw[f, f, q, k] = mine[k]

        @pl.when(jnp.logical_and(p == q, ql == pl_))
        def _():
            raw[1 - f, f, q, k] = mine[k]

    def spread_on(k):
        r1_copy(k, q_at(ql, 1 - qh)).wait_recv()
        for e in range(2):
            loop(1, 4, lambda d: r2_copy(k, e, q_line(d), q_at(ql, e)).start())
        for e in range(2):
            at = q_at(pl_, e)
            away(q, at, lambda: t1_copy(k, e, at).wait_recv())
            loop(1, 4, lambda d: t2_copy(k, e, p_line(d), at).start())
        if k:
            for e in range(2):
                x_copy(f, q_at(ql, e), f).start()
                x_copy(1 - f, q_at(pl_, e), f).start()

    for h in range(2):
        loop(1, 8, lambda d: s1_copy(h, q_peer(d), q).start())
    loop(1, 8, lambda d: g1_copy(c_peer(d), c).start())
    for h, (lo, n) in enumerate(CHUNKS):
        s1r[h][q] = scand[lo : lo + n, rows_of(q + 8 * f), :]
    g1r[c] = pg[c]
    for e in range(2):
        for k in range(2):
            par[k][ql, e] = ccand[q_at(ql, e), k]

    for h in range(2):
        lo, n = CHUNKS[h]
        loop(1, 8, lambda d: s1_copy(h, q_peer(d), q_peer(d)).wait())
        for e in range(lo, lo + n):
            own_k = lax.rem(member(mem, PAIRS[e][0]), 8)
            own_m = lax.rem(member(mem, PAIRS[e][1]), 8)
            s1[e] = s1r[h][own_m + f * (own_k - own_m), e - lo]
        loop(1, 8, lambda d: s2_copy(h, p_peer(d), p).start())
        s2r[h][p] = s1[lo : lo + n]

    loop(1, 8, lambda d: g1_copy(c_peer(d), c_peer(d)).wait())
    g1[...] = jnp.sum(g1r[...], axis=0)
    loop(1, 8, lambda d: g2_copy(r_peer(d), r).start())
    g2r[r] = g1[...]

    for k in range(2):
        for e in range(2):
            loop(1, 4, lambda d: a_copy(k, e, q_line(d), ql).start())

    for h in range(2):
        lo, n = CHUNKS[h]
        loop(1, 8, lambda d: s2_copy(h, p_peer(d), p_peer(d)).wait())
        for e in range(lo, lo + n):
            own_k = lax.rem(member(mem, PAIRS[e][0]), 8)
            own_m = lax.rem(member(mem, PAIRS[e][1]), 8)
            s_all[e, rows_of(q + 8 * f), :] = s2r[h][own_k + f * (own_m - own_k), e - lo]
        loop(1, 8, lambda d: s3_copy(h, q_peer(d), q).start())
        sx_copy(h, q, f).start()


    loop(1, 8, lambda d: g2_copy(r_peer(d), r_peer(d)).wait())
    g2[...] = jnp.sum(g2r[...], axis=0)
    g3 = copy(g2, g3r, snd_g3, rcv_g3, sibling)
    g3.start()

    def pass_on(h):
        def one(d):
            s3_copy(h, q_peer(d), q_peer(d)).wait_recv()
            sx_copy(h, q_peer(d), f).start()

        loop(1, 8, one)

    def sx_ready(h):
        loop(0, 8, lambda at: sx_copy(h, at, 1 - f).wait_recv())

    rr = lax.broadcasted_iota(jnp.int32, (BS, BS), 0)
    cc = lax.broadcasted_iota(jnp.int32, (BS, BS), 1)
    low[...] = jnp.zeros_like(low)
    inv[...] = jnp.zeros_like(inv)

    def before(k):
        if k == 0:
            sx_ready(0)
        if k == 2:
            sx_ready(1)
        for m in range(k):
            keep = pat[member(mem, k), member(mem, m)].astype(f32)
            value = s_all[PAIRS.index((k, m))] * keep
            if m:
                value = value - keep * dot_nt(low[k, :, 0 : BS * m], low[m, :, 0 : BS * m])
            low[k, :, BS * m : BS * m + BS] = dot_nt(value, inv[BS * m : BS * m + BS, BS * m : BS * m + BS])
        value = s_all[PAIRS.index((k, k))] * pat[member(mem, k), member(mem, k)].astype(f32)
        value = value + jnp.where(rr == cc, SHIFT, 0.0)
        if k:
            lows = low[k, :, 0 : BS * k]
            value = value - dot_nt(lows, lows)
        fac_u[...] = value
        fac_i[...] = jnp.where(rr == cc, 1.0, 0.0)

    def after(k):
        at = slice(BS * k, BS * k + BS)
        inv[at, at] = fac_i[...]
        if k:
            inv[at, 0 : BS * k] = -dot_nn(fac_i[...], dot_nn(low[k, :, 0 : BS * k], inv[0 : BS * k, 0 : BS * k]))
        lower = fac_u[...].T
        low[k, :, at] = lower
        diag[k] = lower
        if k == 0:
            pass_on(1)
        if k == 1:
            spread_on(1)
        if k == 2:
            g3.wait()
            g_out[c] = g2[...] + g3r[...]
            loop(1, 8, lambda d: g4_copy(c_peer(d), c).start())

    def step(k):
        for kk in range(STEPS):
            @pl.when(k == kk)
            def _():
                before(kk)

        eliminate(fac_u, fac_i, 0, 8)

        @pl.when(k == 0)
        def _():
            spread_mine(0)
            spread_mine(1)

        @pl.when(k == 1)
        def _():
            spread_on(0)

        eliminate(fac_u, fac_i, 8, 16)
        pivots = jnp.sum(jnp.where(rr == cc, fac_u[...], 0.0), axis=1, keepdims=True)
        scale = 1.0 / jnp.sqrt(pivots)
        fac_u[...] = jnp.where(cc >= rr, fac_u[...] * scale, 0.0)
        fac_i[...] = fac_i[...] * scale
        for kk in range(STEPS):
            @pl.when(k == kk)
            def _():
                after(kk)

    pick(0)
    pick(1)
    pass_on(0)
    loop(0, STEPS, step)

    def arrives(d):
        for e in range(2):
            at = q_at(q_line(d), e)
            for k in range(2):
                r2_copy(k, e, q_line(d), at).wait_recv()
            x_copy(f, at, f).start()
            at = q_at(p_line(d), e)
            for k in range(2):
                t2_copy(k, e, p_line(d), at).wait_recv()
            x_copy(1 - f, at, f).start()

    loop(1, 4, arrives)

    h, l = split(inv[...])
    wh[...] = h
    wl[...] = l
    half = 2 * BS
    w11 = (wh[0:half, 0:half], wl[0:half, 0:half])
    w21 = (wh[half:, 0:half], wl[half:, 0:half])
    w22 = (wh[half:, half:], wl[half:, half:])

    loop(1, 8, lambda d: g4_copy(c_peer(d), c_peer(d)).wait_recv())
    gp = jnp.concatenate(
        [g_out[member(mem, k) // 8, pl.ds(lax.rem(member(mem, k), 8), 1), :] for k in range(STEPS)], axis=1
    )
    gp = jnp.broadcast_to(gp, (16, WIDE))
    y_out[...] = dot3(split(gp), (wh[...], wl[...]))[0:8]

    def panel(which, t):
        base = r + which * (c - r)
        ones, twos, keeps = [], [], []
        for e in range(2):
            a = 2 * t + e
            x_copy(which, a, 1 - f).wait_recv()
        for e in range(2):
            a = 2 * t + e
            i = 8 * a + base
            pivot = i == member(mem, 0)
            for k in range(1, STEPS):
                pivot = jnp.logical_or(pivot, i == member(mem, k))
            z = jnp.where(pivot, 0.0, 1.0).astype(f32)
            m1 = z * pat[i, member(mem, 0)].astype(f32)
            m2 = z * pat[i, member(mem, 2)].astype(f32)
            ones.append(jnp.concatenate([raw[which, 0, a, 0], raw[which, 0, a, 1]], axis=1) * m1)
            twos.append(jnp.concatenate([raw[which, 1, a, 0], raw[which, 1, a, 1]], axis=1))
            keeps.append(m2)
        one = split(jnp.concatenate(ones, axis=0))
        two = split(jnp.concatenate(twos, axis=0))
        second = dot3(one, w21) + dot3(two, w22)
        rows = pl.ds(pl.multiple_of(half * t, half), half)
        hi, rest = split(dot3(one, w11))
        x_hi[which, rows, 0:half] = hi
        x_lo[which, rows, 0:half] = rest
        second = jnp.concatenate([second[0:BS] * keeps[0], second[BS:half] * keeps[1]], axis=0)
        hi, rest = split(second)
        x_hi[which, rows, half:WIDE] = hi
        x_lo[which, rows, half:WIDE] = rest

    loop(0, 8, lambda t: panel(t // 4, lax.rem(t, 4)))

    def tail(d):
        for h in range(2):
            s3_copy(h, q_peer(d), q).wait_send()
        g4_copy(c_peer(d), c).wait_send()

    loop(1, 8, tail)
    for k in range(2):
        r1_copy(k, q).wait_send()
        for e in range(2):
            away(p_at(ql, e), p, lambda: t1_copy(k, e, q).wait_send())

    def tail_line(d):
        for k in range(2):
            for e in range(2):
                r2_copy(k, e, q_line(d), q_at(ql, e)).wait_send()
                t2_copy(k, e, p_line(d), q_at(pl_, e)).wait_send()

    loop(1, 4, tail_line)

    def tail_pair(d):
        for h in range(2):
            sx_copy(h, d, f).wait_send()
        for which in range(2):
            x_copy(which, d, f).wait_send()

    loop(0, 8, tail_pair)


def exchange(mem, pat, scand, ccand, pg):
    vmem = pltpu.VMEM
    sem = pltpu.SemaphoreType.DMA
    return pl.pallas_call(
        exchange_kernel,
        out_shape=(
            jax.ShapeDtypeStruct((2, 1024, WIDE), bf16),
            jax.ShapeDtypeStruct((2, 1024, WIDE), bf16),
            jax.ShapeDtypeStruct((STEPS, BS, BS), f32),
            jax.ShapeDtypeStruct((8, WIDE), f32),
            jax.ShapeDtypeStruct((8, 8, BS), f32),
        ),
        in_specs=[SM, SM, VM, VM, VM],
        out_specs=(VM,) * 5,
        scratch_shapes=[
            vmem((NQ, BS, BS), f32),
            vmem((STEPS, BS, WIDE), f32),
            vmem((WIDE, WIDE), f32),
            vmem((BS, BS), f32),
            vmem((BS, BS), f32),
            vmem((2, 2, 8, 2, BS, BS), f32),
            vmem((WIDE, WIDE), bf16),
            vmem((WIDE, WIDE), bf16),
            vmem((8, CHUNKS[0][1], 8, BS), f32),
            vmem((8, CHUNKS[1][1], 8, BS), f32),
            vmem((NQ, 8, BS), f32),
            vmem((8, CHUNKS[0][1], 8, BS), f32),
            vmem((8, CHUNKS[1][1], 8, BS), f32),
            vmem((4, 2, BS, BS), f32),
            vmem((4, 2, BS, BS), f32),
            vmem((2, 2, BS, BS), f32),
            vmem((2, BS, BS), f32),
            vmem((2, BS, BS), f32),
            vmem((2, BS, BS), f32),
            vmem((8, 8, BS), f32),
            vmem((8, BS), f32),
            vmem((8, 8, BS), f32),
            vmem((8, BS), f32),
            vmem((8, BS), f32),
        ]
        + [sem((2, 8))] * 10
        + [sem((4, 4))] * 4
        + [sem((2, 2))]
        + [sem((2, 8))] * 2
        + [sem((8,))] * 6
        + [sem] * 2
        + [sem((2,))] * 3,
        compiler_params=pltpu.CompilerParams(
            collective_id=0, has_side_effects=True, vmem_limit_bytes=40 << 20
        ),
        name="exchange",
    )(mem, pat, scand, ccand, pg)


def update_kernel(mem, pat, diag, x_hi, x_lo, y, g, hess, out, grad_out, rows, in_sem, out_sem):
    r = lax.axis_index("prow")
    c = lax.axis_index("pcol")

    def load(a):
        return pltpu.make_async_copy(hess.at[a], rows.at[a], in_sem.at[a])

    def save(a):
        return pltpu.make_async_copy(rows.at[a], out.at[a], out_sem.at[a])

    for a in range(8):
        load(a).start()

    def is_pivot(i):
        pivot = i == member(mem, 0)
        for k in range(1, STEPS):
            pivot = jnp.logical_or(pivot, i == member(mem, k))
        return pivot

    dec = dot3(split(jnp.concatenate([y[...], y[...]], axis=0)), (x_hi[0], x_lo[0]))
    for a in range(8):
        i = 8 * a + r
        val = g[a, pl.ds(r, 1), :] - dec[0:1, BS * a : BS * a + BS]
        for k in range(STEPS):
            val = jnp.where(i == member(mem, k), y[0:1, BS * k : BS * k + BS], val)
        grad_out[a : a + 1, :] = val

    rr = lax.broadcasted_iota(jnp.int32, (BS, BS), 0)
    cc = lax.broadcasted_iota(jnp.int32, (BS, BS), 1)
    shift = jnp.where(rr == cc, SHIFT, 0.0)
    cols = (x_hi[1], x_lo[1])

    def two_rows(t):
        at = pl.ds(pl.multiple_of(2 * BS * t, 2 * BS), 2 * BS)
        upd = dot3((x_hi[0, at, :], x_lo[0, at, :]), cols)
        for e in range(2):
            a = 2 * t + e
            i = 8 * a + r
            live = jnp.where(is_pivot(i), 0.0, 1.0).astype(f32)
            load(a).wait()
            for b in range(8):
                j = 8 * b + c
                keep = live * pat[i, j].astype(f32)
                on = jnp.where(i == j, 1.0, 0.0).astype(f32) * live
                sub = upd[BS * e : BS * e + BS, BS * b : BS * b + BS]
                there = pl.ds(b, BS, stride=8)
                rows[a, there, :] = keep * (rows[a, there, :] - sub) + on * shift
            for k in range(STEPS):
                pk = member(mem, k)

                @pl.when(lax.rem(pk, 8) == c)
                def _():
                    there = pl.ds(pk // 8, BS, stride=8)
                    mine = pl.ds(pl.multiple_of(BS * a, BS), BS)
                    part = slice(BS * k, BS * k + BS)

                    @pl.when(i != pk)
                    def _():
                        rows[a, there, :] = x_hi[0, mine, part].astype(f32) + x_lo[0, mine, part].astype(f32)

                    @pl.when(i == pk)
                    def _():
                        rows[a, there, :] = diag[k]
            save(a).start()

    loop(0, 4, two_rows)
    for a in range(8):
        save(a).wait()


def update(mem, pat, diag, x_hi, x_lo, y, g, hess):
    return pl.pallas_call(
        update_kernel,
        out_shape=(
            jax.ShapeDtypeStruct(hess.shape, f32),
            jax.ShapeDtypeStruct((8, BS), f32),
        ),
        in_specs=[SM, SM, VM, VM, VM, VM, VM, ANY],
        out_specs=(ANY, VM),
        scratch_shapes=[
            pltpu.VMEM((8, 1024, BS), f32),
            pltpu.SemaphoreType.DMA((8,)),
            pltpu.SemaphoreType.DMA((8,)),
        ],
        compiler_params=pltpu.CompilerParams(vmem_limit_bytes=32 << 20),
        name="update",
    )(mem, pat, diag, x_hi, x_lo, y, g, hess)


def shards(
    poses, codebook, offsets, confidence, code_ids, creature_ids, hess_raw, pattern, membership
):
    scand, ccand, pg = prepare(
        membership, hess_raw.reshape(8, BS, 8, 1, BS), poses, codebook, offsets,
        confidence.reshape(16, BS), code_ids.reshape(16, BS), creature_ids.reshape(16, BS),
    )
    x_hi, x_lo, diag, y, g = exchange(membership, pattern, scand, ccand, pg.reshape(8, 8, BS))
    state, grad = update(
        membership, pattern, diag, x_hi, x_lo, y, g, hess_raw.reshape(8, 1024, BS)
    )
    return state.reshape(hess_raw.shape), grad.reshape(8, 1, BS)


def solution(mesh):
    return jax.shard_map(
        shards,
        mesh=mesh,
        in_specs=(
            P(("frames", "prow", "pcol"), None),
            P(),
            P(),
            P(("frames", "prow", "pcol")),
            P(("frames", "prow", "pcol")),
            P(("frames", "prow", "pcol")),
            P(None, "prow", None, None, "pcol", None),
            P(),
            P(),
        ),
        out_specs=(P(None, "prow", None, None, "pcol", None), P(None, "prow", None)),
        check_vma=False,
    )
```

```python
import math

import jax
import jax.numpy as jnp
from jax import lax
from jax.experimental import pallas as pl
from jax.experimental.pallas import tpu as pltpu
from jax.sharding import PartitionSpec as P

NPAN = 8192
BS = 128
STEPS = 4
FRAMES = 262144
CODES = 32
SHIFT = 2.5 * math.sqrt(NPAN)
PAIRS = [(k, m) for k in range(STEPS) for m in range(k + 1)]
NQ = len(PAIRS)
CHUNKS = ((0, 3), (3, 7))
WIDE = STEPS * BS
MESH = pl.DeviceIdType.MESH
precise = lax.Precision.HIGHEST
f32 = jnp.float32
bf16 = jnp.bfloat16
NT = (((1,), (1,)), ((), ()))
NN = (((1,), (0,)), ((), ()))


def loop(lo, hi, fn):
    def body(d, carry):
        fn(d)
        return carry

    lax.fori_loop(lo, hi, body, 0)


def split(x):
    hi = x.astype(bf16)
    return hi, (x - hi.astype(f32)).astype(bf16)


def dot3(a, b):
    (ah, al), (bh, bl) = a, b
    d = lambda x, y: lax.dot_general(x, y, NT, preferred_element_type=f32)
    return d(ah, bh) + (d(ah, bl) + d(al, bh))


def member(mem, k):
    return mem[k // 2, k % 2]


VM = pl.BlockSpec(memory_space=pltpu.VMEM)
SM = pl.BlockSpec(memory_space=pltpu.SMEM)
ANY = pl.BlockSpec(memory_space=pl.ANY)
HBM = pl.BlockSpec(memory_space=pltpu.HBM)


def moments(poses, codebook, offsets, conf, codes, kinds):
    ids = lax.broadcasted_iota(jnp.int32, (CODES, BS), 0)
    weights, marks = [], []
    for s in range(16):
        weights.append(jnp.where(codes[s : s + 1, :] == ids, conf[s : s + 1, :], 0.0))
        marks.append(jnp.where(kinds[s : s + 1, :] == ids, 1.0, 0.0).astype(bf16))
    weight = jnp.concatenate(weights, axis=1)
    mark = jnp.concatenate(marks, axis=1)
    parts = []
    for _ in range(3):
        parts.append(weight.astype(bf16))
        weight = weight - parts[-1].astype(f32)
    stack = jnp.concatenate(parts, axis=0)

    def total(x):
        return x[0:CODES] + (x[CODES : 2 * CODES] + x[2 * CODES : 3 * CODES])

    moment = total(lax.dot_general(stack, poses[...], NN, preferred_element_type=f32))
    pair = total(lax.dot_general(stack, mark, NT, preferred_element_type=f32))
    count = jnp.sum(pair, axis=1, keepdims=True)
    moment = moment - count * codebook[...].astype(f32)
    moment = moment - lax.dot_general(
        pair, offsets[...].astype(f32), NN, precision=precise, preferred_element_type=f32
    )
    return moment / math.sqrt(FRAMES / CODES)


def spread(row):
    return jnp.broadcast_to(row, (8, BS))


def eliminate(upper_ref, inv_ref, first, last):
    groups = BS // 8
    row_ids = lax.broadcasted_iota(jnp.int32, (8, BS), 0)
    upper = {g: upper_ref[8 * g : 8 * g + 8, :] for g in range(first, groups)}
    inv = {g: inv_ref[8 * g : 8 * g + 8, :] for g in range(first, groups)}
    for g in range(first, last):
        k = 8 * g
        v, w = upper[g], inv[g]
        cols = [jnp.broadcast_to(v[:, k + j : k + j + 1], (8, BS)) for j in range(8)]
        rows_v, rows_w, coef = [], [], []
        for j in range(8):
            pivot = spread(cols[j][j : j + 1, :])
            recip = 1.0 / pivot
            rv = spread(v[j : j + 1, :]) * recip
            rw = spread(w[j : j + 1, :]) * recip
            rows_v.append(rv)
            rows_w.append(rw)
            below = jnp.where(row_ids > j, cols[j], 0.0)
            coef.append([None] * 8)
            for t in range(j + 1, 8):
                coef[j][t] = spread(cols[t][j : j + 1, :]) * recip
                cols[t] = cols[t] - below * coef[j][t]
            v = v - below * rv
            w = w - below * rw
        upper[g], inv[g] = v, w
        for h in range(g + 1, groups):
            v, w = upper[h], inv[h]
            cols = [jnp.broadcast_to(v[:, k + j : k + j + 1], (8, BS)) for j in range(8)]
            for j in range(8):
                for t in range(j + 1, 8):
                    cols[t] = cols[t] - cols[j] * coef[j][t]
                v = v - cols[j] * rows_v[j]
                w = w - cols[j] * rows_w[j]
            upper[h], inv[h] = v, w
    for g in range(first, groups):
        upper_ref[8 * g : 8 * g + 8, :] = upper[g]
        inv_ref[8 * g : 8 * g + 8, :] = inv[g]


def dot_nt(a, b):
    return lax.dot_general(a, b, NT, precision=precise, preferred_element_type=f32)


def dot_nn(a, b):
    return lax.dot_general(a, b, (((1,), (0,)), ((), ())), precision=precise, preferred_element_type=f32)


def exchange_kernel(
    mem, pat, hess_at, poses_at, codebook_at, offsets_at, conf_at, codes_at, kinds_at,
    x_row, x_col, diag, y_out, g_out,
    hess, poses, codebook, offsets, conf, codes, kinds, scand, ccand, pg, s_all, low, inv, fac_u, fac_i, raw, wh, wl,
    s1r_a, s1r_b, s1, s2r_a, s2r_b, par_a, par_b, picked, both_a, both_b, mine, g1r, g1, g2r, g2, g3r,
    snd_s1, rcv_s1, snd_s2, rcv_s2, snd_s3, rcv_s3, snd_sx, rcv_sx,
    snd_x, rcv_x, snd_a, rcv_a, snd_r2, snd_t2, snd_t1, rcv_r, rcv_t,
    snd_g1, rcv_g1, snd_g2, rcv_g2, snd_g4, rcv_g4, snd_g3, rcv_g3, snd_b, rcv_b, snd_r1, in_sem,
):
    fetches = [
        pltpu.make_async_copy(src, dst, in_sem.at[n])
        for n, (src, dst) in enumerate(
            [
                (hess_at, hess), (codes_at, codes), (conf_at, conf), (kinds_at, kinds),
                (poses_at, poses), (codebook_at, codebook), (offsets_at, offsets),
            ]
        )
    ]
    for fetch in fetches:
        fetch.start()
    s1r, s2r = (s1r_a, s1r_b), (s2r_a, s2r_b)
    par, both = (par_a, par_b), (both_a, both_b)
    f = lax.axis_index("frames")
    r = lax.axis_index("prow")
    c = lax.axis_index("pcol")
    p = r + f * (c - r)
    q = c + f * (r - c)

    def place(p_to, q_to):
        return (f, p_to + f * (q_to - p_to), q_to + f * (p_to - q_to))

    sibling = (1 - f, r, c)

    def q_at(line, pair):
        return 2 * line + pair + f * (3 * pair - line)

    def p_at(line, pair):
        return line + 4 * pair + f * (line - 3 * pair)

    def q_parts(v):
        return v // 2 + f * (lax.rem(v, 4) - v // 2), lax.rem(v, 2) + f * (v // 4 - lax.rem(v, 2))

    def p_parts(v):
        return lax.rem(v, 4) + f * (v // 2 - lax.rem(v, 4)), v // 4 + f * (lax.rem(v, 2) - v // 4)

    ql, qh = q_parts(q)
    pl_, ph = p_parts(p)

    def q_line(d):
        return lax.rem(ql + d, 4)

    def p_line(d):
        return lax.rem(pl_ + d, 4)

    def copy(src, dst, snd, rcv, to):
        return pltpu.make_async_remote_copy(
            src_ref=src, dst_ref=dst, send_sem=snd, recv_sem=rcv, device_id=to, device_id_type=MESH
        )

    def q_peer(d):
        return lax.rem(q + d, 8)

    def p_peer(d):
        return lax.rem(p + d, 8)

    def c_peer(d):
        return lax.rem(c + d, 8)

    def r_peer(d):
        return lax.rem(r + d, 8)

    barrier = pltpu.get_barrier_semaphore()

    def greet(to):
        pl.semaphore_signal(barrier, inc=1, device_id=to, device_id_type=MESH)

    greet(sibling)

    def greet_line(d):
        greet(place(p, q_peer(d)))
        greet(place(p_peer(d), q))

    loop(1, 8, greet_line)

    def at_home(p_to, q_to):
        return jnp.logical_and(p_to == p, q_to == q)

    def away(p_to, q_to, fn):
        @pl.when(jnp.logical_not(at_home(p_to, q_to)))
        def _():
            fn()

    def greet_turn(e):
        away(p_at(ql, e), p, lambda: greet(place(p_at(ql, e), p)))
        away(q, q_at(pl_, e), lambda: greet(place(q, q_at(pl_, e))))

    loop(0, 2, greet_turn)
    same = jnp.where(jnp.logical_and(p == q, ql == pl_), 1, 0)

    slot = [member(mem, k) // 8 for k in range(STEPS)]
    fetches[0].wait()
    for e, (k, m) in enumerate(PAIRS):
        scand[e] = hess[slot[k], pl.ds(slot[m], BS, stride=8), :]

    @pl.when(f == 0)
    def _():
        for k in range(2):
            for v in range(8):
                ccand[v, k] = hess[v, pl.ds(slot[k], BS, stride=8), :]

    @pl.when(f == 1)
    def _():
        for k in range(2):
            for v in range(8):
                ccand[v, k] = hess[slot[2 + k], pl.ds(v, BS, stride=8), :]

    pl.semaphore_wait(barrier, 19 - 2 * same)

    def rows_of(slice_id):
        return pl.ds(pl.multiple_of(8 * slice_id, 8), 8)

    def s1_copy(h, peer, at):
        lo, n = CHUNKS[h]
        return copy(
            scand.at[pl.ds(lo, n), rows_of(peer + 8 * f), :], s1r[h].at[at],
            snd_s1.at[h, peer], rcv_s1.at[h, at], place(p, peer),
        )

    def s2_copy(h, peer, at):
        lo, n = CHUNKS[h]
        return copy(
            s1.at[pl.ds(lo, n)], s2r[h].at[at],
            snd_s2.at[h, peer], rcv_s2.at[h, at], place(peer, q),
        )

    def s3_copy(h, peer, at):
        lo, n = CHUNKS[h]
        part = s_all.at[pl.ds(lo, n), rows_of(at + 8 * f), :]
        return copy(part, part, snd_s3.at[h, peer], rcv_s3.at[h, at], place(p, peer))

    def sx_copy(h, at, core):
        lo, n = CHUNKS[h]
        part = s_all.at[pl.ds(lo, n), rows_of(at + 8 * core), :]
        return copy(part, part, snd_sx.at[h, at], rcv_sx.at[h, at], sibling)

    def g1_copy(peer, at):
        return copy(pg.at[rows_of(peer)], g1r.at[at], snd_g1.at[peer], rcv_g1.at[at], (f, r, peer))

    def g2_copy(peer, at):
        return copy(g1, g2r.at[at], snd_g2.at[peer], rcv_g2.at[at], (f, peer, c))

    def g4_copy(peer, at):
        return copy(g_out.at[at], g_out.at[at], snd_g4.at[peer], rcv_g4.at[at], (f, r, peer))

    def a_copy(k, e, line, at):
        return copy(
            ccand.at[q_at(line, e), k], par[k].at[at, e],
            snd_a.at[2 * k + e, line], rcv_a.at[2 * k + e, at], place(p, q_at(line, qh)),
        )

    def b_copy(k):
        return copy(
            picked.at[k, 1 - qh], both[k].at[qh], snd_b.at[k], rcv_b.at[k], place(p, q_at(ql, 1 - qh))
        )

    def r1_copy(k, at):
        return copy(
            mine.at[k], raw.at[f, f, at, k], snd_r1.at[k], rcv_r.at[k, at], place(p, q_at(ql, 1 - qh))
        )

    def r2_copy(k, e, line, at):
        part = raw.at[f, f, at, k]
        return copy(part, part, snd_r2.at[2 * k + e, line], rcv_r.at[k, at], place(p, q_at(line, qh)))

    def t1_copy(k, e, at):
        return copy(
            mine.at[k], raw.at[1 - f, f, at, k], snd_t1.at[k, e], rcv_t.at[k, at], place(p_at(ql, e), p)
        )

    def t2_copy(k, e, line, at):
        part = raw.at[1 - f, f, at, k]
        return copy(part, part, snd_t2.at[2 * k + e, line], rcv_t.at[k, at], place(p_at(line, ph), q))

    def x_copy(which, at, core):
        part = raw.at[which, core, at]
        return copy(part, part, snd_x.at[which, at], rcv_x.at[which, at], sibling)

    def owner(k):
        return q_parts(lax.rem(mem[f, k], 8))

    def pick(k):
        for e in range(2):
            loop(1, 4, lambda d: a_copy(k, e, q_line(d), q_line(d)).wait())
        for e in range(2):
            picked[k, e] = par[k][owner(k)[0], e]
        b_copy(k).start()

    def spread_mine(k):
        both[k][qh] = picked[k, qh]
        b_copy(k).wait()

        @pl.when(f == 0)
        def _():
            mine[k] = both[k][lax.rem(mem[0, k], 2)]

        @pl.when(f == 1)
        def _():
            mine[k] = both[k][lax.rem(mem[1, k], 8) // 4].T

        r1_copy(k, q).start()
        for e in range(2):
            away(p_at(ql, e), p, lambda: t1_copy(k, e, q).start())
        raw[f, f, q, k] = mine[k]

        @pl.when(jnp.logical_and(p == q, ql == pl_))
        def _():
            raw[1 - f, f, q, k] = mine[k]

    def spread_on(k):
        r1_copy(k, q_at(ql, 1 - qh)).wait_recv()
        for e in range(2):
            loop(1, 4, lambda d: r2_copy(k, e, q_line(d), q_at(ql, e)).start())
        for e in range(2):
            at = q_at(pl_, e)
            away(q, at, lambda: t1_copy(k, e, at).wait_recv())
            loop(1, 4, lambda d: t2_copy(k, e, p_line(d), at).start())
        if k:
            for e in range(2):
                x_copy(f, q_at(ql, e), f).start()
                x_copy(1 - f, q_at(pl_, e), f).start()

    for h in range(2):
        loop(1, 8, lambda d: s1_copy(h, q_peer(d), q).start())
    for k in range(2):
        for e in range(2):
            loop(1, 4, lambda d: a_copy(k, e, q_line(d), ql).start())
    for h, (lo, n) in enumerate(CHUNKS):
        s1r[h][q] = scand[lo : lo + n, rows_of(q + 8 * f), :]
    for e in range(2):
        for k in range(2):
            par[k][ql, e] = ccand[q_at(ql, e), k]
    for fetch in fetches[1:]:
        fetch.wait()
    moment = moments(poses, codebook, offsets, conf, codes, kinds)
    for half in range(2):
        pg[pl.ds(half, CODES, stride=2), :] = moment[:, BS * half : BS * half + BS]
    loop(1, 8, lambda d: g1_copy(c_peer(d), c).start())
    g1r[c] = pg[rows_of(c), :]

    for h in range(2):
        lo, n = CHUNKS[h]
        loop(1, 8, lambda d: s1_copy(h, q_peer(d), q_peer(d)).wait())
        for e in range(lo, lo + n):
            own_k = lax.rem(member(mem, PAIRS[e][0]), 8)
            own_m = lax.rem(member(mem, PAIRS[e][1]), 8)
            s1[e] = s1r[h][own_m + f * (own_k - own_m), e - lo]
        loop(1, 8, lambda d: s2_copy(h, p_peer(d), p).start())
        s2r[h][p] = s1[lo : lo + n]

    loop(1, 8, lambda d: g1_copy(c_peer(d), c_peer(d)).wait())
    g1[...] = jnp.sum(g1r[...], axis=0)
    loop(1, 8, lambda d: g2_copy(r_peer(d), r).start())
    g2r[r] = g1[...]


    for h in range(2):
        lo, n = CHUNKS[h]
        loop(1, 8, lambda d: s2_copy(h, p_peer(d), p_peer(d)).wait())
        for e in range(lo, lo + n):
            own_k = lax.rem(member(mem, PAIRS[e][0]), 8)
            own_m = lax.rem(member(mem, PAIRS[e][1]), 8)
            s_all[e, rows_of(q + 8 * f), :] = s2r[h][own_k + f * (own_m - own_k), e - lo]
        loop(1, 8, lambda d: s3_copy(h, q_peer(d), q).start())
        sx_copy(h, q, f).start()


    loop(1, 8, lambda d: g2_copy(r_peer(d), r_peer(d)).wait())
    g2[...] = jnp.sum(g2r[...], axis=0)
    g3 = copy(g2, g3r, snd_g3, rcv_g3, sibling)
    g3.start()

    def pass_on(h):
        def one(d):
            s3_copy(h, q_peer(d), q_peer(d)).wait_recv()
            sx_copy(h, q_peer(d), f).start()

        loop(1, 8, one)

    def sx_ready(h):
        loop(0, 8, lambda at: sx_copy(h, at, 1 - f).wait_recv())

    rr = lax.broadcasted_iota(jnp.int32, (BS, BS), 0)
    cc = lax.broadcasted_iota(jnp.int32, (BS, BS), 1)
    low[...] = jnp.zeros_like(low)
    inv[...] = jnp.zeros_like(inv)

    def before(k):
        if k == 0:
            sx_ready(0)
        if k == 2:
            sx_ready(1)
        if k:
            row = jnp.concatenate(
                [
                    s_all[PAIRS.index((k, m))] * pat[member(mem, k), member(mem, m)].astype(f32)
                    for m in range(k)
                ],
                axis=1,
            )
            low[k, :, 0 : BS * k] = dot_nt(row, inv[0 : BS * k, 0 : BS * k])
        value = s_all[PAIRS.index((k, k))] * pat[member(mem, k), member(mem, k)].astype(f32)
        value = value + jnp.where(rr == cc, SHIFT, 0.0)
        if k:
            lows = low[k, :, 0 : BS * k]
            value = value - dot_nt(lows, lows)
        fac_u[...] = value
        fac_i[...] = jnp.where(rr == cc, 1.0, 0.0)

    def after(k):
        at = slice(BS * k, BS * k + BS)
        inv[at, at] = fac_i[...]
        if k:
            inv[at, 0 : BS * k] = -dot_nn(fac_i[...], dot_nn(low[k, :, 0 : BS * k], inv[0 : BS * k, 0 : BS * k]))
        lower = fac_u[...].T
        low[k, :, at] = lower
        diag[k] = lower
        if k == 0:
            pass_on(1)
        if k == 1:
            spread_on(1)
        if k == 2:
            g3.wait()
            g_out[c] = g2[...] + g3r[...]
            loop(1, 8, lambda d: g4_copy(c_peer(d), c).start())

    def step(k):
        for kk in range(STEPS):
            @pl.when(k == kk)
            def _():
                before(kk)

        eliminate(fac_u, fac_i, 0, 8)

        @pl.when(k == 0)
        def _():
            spread_mine(0)
            spread_mine(1)

        @pl.when(k == 1)
        def _():
            spread_on(0)

        eliminate(fac_u, fac_i, 8, 16)
        pivots = jnp.sum(jnp.where(rr == cc, fac_u[...], 0.0), axis=1, keepdims=True)
        scale = 1.0 / jnp.sqrt(pivots)
        fac_u[...] = jnp.where(cc >= rr, fac_u[...] * scale, 0.0)
        fac_i[...] = fac_i[...] * scale
        for kk in range(STEPS):
            @pl.when(k == kk)
            def _():
                after(kk)

    pick(0)
    pick(1)
    pass_on(0)
    loop(0, STEPS, step)

    def arrives(d):
        for e in range(2):
            at = q_at(q_line(d), e)
            for k in range(2):
                r2_copy(k, e, q_line(d), at).wait_recv()
            x_copy(f, at, f).start()
            at = q_at(p_line(d), e)
            for k in range(2):
                t2_copy(k, e, p_line(d), at).wait_recv()
            x_copy(1 - f, at, f).start()

    loop(1, 4, arrives)

    h, l = split(inv[...])
    wh[...] = h
    wl[...] = l
    half = 2 * BS
    w11 = (wh[0:half, 0:half], wl[0:half, 0:half])
    w21 = (wh[half:, 0:half], wl[half:, 0:half])
    w22 = (wh[half:, half:], wl[half:, half:])

    loop(1, 8, lambda d: g4_copy(c_peer(d), c_peer(d)).wait_recv())
    gp = jnp.concatenate(
        [g_out[member(mem, k) // 8, pl.ds(lax.rem(member(mem, k), 8), 1), :] for k in range(STEPS)], axis=1
    )
    gp = jnp.broadcast_to(gp, (16, WIDE))
    y_out[...] = dot3(split(gp), (wh[...], wl[...]))[0:8]

    def store(which, rows, at, x):
        hi, rest = split(x)
        for target, parts in ((x_row, (hi, rest, hi)), (x_col, (hi, hi, rest))):
            @pl.when(which == (1 if target is x_col else 0))
            def _():
                for n, part in enumerate(parts):
                    target[rows, WIDE * n + at : WIDE * n + at + half] = part

    def panel(which, t):
        base = r + which * (c - r)
        ones, twos, keeps = [], [], []
        for e in range(2):
            a = 2 * t + e
            x_copy(which, a, 1 - f).wait_recv()
        for e in range(2):
            a = 2 * t + e
            i = 8 * a + base
            pivot = i == member(mem, 0)
            for k in range(1, STEPS):
                pivot = jnp.logical_or(pivot, i == member(mem, k))
            z = jnp.where(pivot, 0.0, 1.0).astype(f32)
            m1 = z * pat[i, member(mem, 0)].astype(f32)
            m2 = z * pat[i, member(mem, 2)].astype(f32)
            ones.append(jnp.concatenate([raw[which, 0, a, 0], raw[which, 0, a, 1]], axis=1) * m1)
            twos.append(jnp.concatenate([raw[which, 1, a, 0], raw[which, 1, a, 1]], axis=1))
            keeps.append(m2)
        one = split(jnp.concatenate(ones, axis=0))
        two = split(jnp.concatenate(twos, axis=0))
        second = dot3(one, w21) + dot3(two, w22)
        rows = pl.ds(pl.multiple_of(half * t, half), half)
        store(which, rows, 0, dot3(one, w11))
        second = jnp.concatenate([second[0:BS] * keeps[0], second[BS:half] * keeps[1]], axis=0)
        store(which, rows, half, second)

    loop(0, 8, lambda t: panel(t // 4, lax.rem(t, 4)))

    def tail(d):
        for h in range(2):
            s3_copy(h, q_peer(d), q).wait_send()
        g4_copy(c_peer(d), c).wait_send()

    loop(1, 8, tail)
    for k in range(2):
        r1_copy(k, q).wait_send()
        for e in range(2):
            away(p_at(ql, e), p, lambda: t1_copy(k, e, q).wait_send())

    def tail_line(d):
        for k in range(2):
            for e in range(2):
                r2_copy(k, e, q_line(d), q_at(ql, e)).wait_send()
                t2_copy(k, e, p_line(d), q_at(pl_, e)).wait_send()

    loop(1, 4, tail_line)

    def tail_pair(d):
        for h in range(2):
            sx_copy(h, d, f).wait_send()
        for which in range(2):
            x_copy(which, d, f).wait_send()

    loop(0, 8, tail_pair)


def exchange(mem, pat, *operands):
    vmem = pltpu.VMEM
    sem = pltpu.SemaphoreType.DMA
    return pl.pallas_call(
        exchange_kernel,
        out_shape=(
            jax.ShapeDtypeStruct((1024, 3 * WIDE), bf16),
            jax.ShapeDtypeStruct((1024, 3 * WIDE), bf16),
            jax.ShapeDtypeStruct((STEPS, BS, BS), f32),
            jax.ShapeDtypeStruct((8, WIDE), f32),
            jax.ShapeDtypeStruct((8, 8, BS), f32),
        ),
        in_specs=[SM, SM] + [HBM] * 7,
        out_specs=(VM,) * 5,
        scratch_shapes=[vmem(x.shape, x.dtype) for x in operands]
        + [
            vmem((NQ, BS, BS), f32),
            vmem((8, 2, BS, BS), f32),
            vmem((64, BS), f32),
            vmem((NQ, BS, BS), f32),
            vmem((STEPS, BS, WIDE), f32),
            vmem((WIDE, WIDE), f32),
            vmem((BS, BS), f32),
            vmem((BS, BS), f32),
            vmem((2, 2, 8, 2, BS, BS), f32),
            vmem((WIDE, WIDE), bf16),
            vmem((WIDE, WIDE), bf16),
            vmem((8, CHUNKS[0][1], 8, BS), f32),
            vmem((8, CHUNKS[1][1], 8, BS), f32),
            vmem((NQ, 8, BS), f32),
            vmem((8, CHUNKS[0][1], 8, BS), f32),
            vmem((8, CHUNKS[1][1], 8, BS), f32),
            vmem((4, 2, BS, BS), f32),
            vmem((4, 2, BS, BS), f32),
            vmem((2, 2, BS, BS), f32),
            vmem((2, BS, BS), f32),
            vmem((2, BS, BS), f32),
            vmem((2, BS, BS), f32),
            vmem((8, 8, BS), f32),
            vmem((8, BS), f32),
            vmem((8, 8, BS), f32),
            vmem((8, BS), f32),
            vmem((8, BS), f32),
        ]
        + [sem((2, 8))] * 10
        + [sem((4, 4))] * 4
        + [sem((2, 2))]
        + [sem((2, 8))] * 2
        + [sem((8,))] * 6
        + [sem] * 2
        + [sem((2,))] * 3
        + [sem((7,))],
        compiler_params=pltpu.CompilerParams(
            collective_id=0, has_side_effects=True, vmem_limit_bytes=40 << 20
        ),
        name="exchange",
    )(mem, pat, *(pltpu.with_memory_space_constraint(x, pltpu.HBM) for x in operands))


def update_kernel(mem, pat, diag, x_row, x_col, y, g, hess, out, grad_out, rows, in_sem, out_sem):
    r = lax.axis_index("prow")
    c = lax.axis_index("pcol")

    def load(a):
        return pltpu.make_async_copy(hess.at[a], rows.at[a], in_sem.at[a])

    def save(a):
        return pltpu.make_async_copy(rows.at[a], out.at[a], out_sem.at[a])

    for a in range(8):
        load(a).start()

    def is_pivot(i):
        pivot = i == member(mem, 0)
        for k in range(1, STEPS):
            pivot = jnp.logical_or(pivot, i == member(mem, k))
        return pivot

    dec = dot3(split(jnp.concatenate([y[...], y[...]], axis=0)), (x_row[:, 0:WIDE], x_row[:, WIDE : 2 * WIDE]))
    for a in range(8):
        i = 8 * a + r
        val = g[a, pl.ds(r, 1), :] - dec[0:1, BS * a : BS * a + BS]
        for k in range(STEPS):
            val = jnp.where(i == member(mem, k), y[0:1, BS * k : BS * k + BS], val)
        grad_out[a : a + 1, :] = val

    rr = lax.broadcasted_iota(jnp.int32, (BS, BS), 0)
    cc = lax.broadcasted_iota(jnp.int32, (BS, BS), 1)
    shift = jnp.where(rr == cc, SHIFT, 0.0)

    def two_rows(t):
        at = pl.ds(pl.multiple_of(2 * BS * t, 2 * BS), 2 * BS)
        upd = lax.dot_general(x_row[at, :], x_col[...], NT, preferred_element_type=f32)
        for e in range(2):
            a = 2 * t + e
            i = 8 * a + r
            live = jnp.where(is_pivot(i), 0.0, 1.0).astype(f32)
            load(a).wait()
            for b in range(8):
                j = 8 * b + c
                keep = live * pat[i, j].astype(f32)
                on = jnp.where(i == j, 1.0, 0.0).astype(f32) * live
                sub = upd[BS * e : BS * e + BS, BS * b : BS * b + BS]
                there = pl.ds(b, BS, stride=8)
                rows[a, there, :] = keep * (rows[a, there, :] - sub) + on * shift
            for k in range(STEPS):
                pk = member(mem, k)

                @pl.when(lax.rem(pk, 8) == c)
                def _():
                    there = pl.ds(pk // 8, BS, stride=8)
                    mine = pl.ds(pl.multiple_of(BS * a, BS), BS)
                    part = slice(BS * k, BS * k + BS)
                    rest = slice(WIDE + BS * k, WIDE + BS * k + BS)

                    @pl.when(i != pk)
                    def _():
                        rows[a, there, :] = x_row[mine, part].astype(f32) + x_row[mine, rest].astype(f32)

                    @pl.when(i == pk)
                    def _():
                        rows[a, there, :] = diag[k]
            save(a).start()

    loop(0, 4, two_rows)
    for a in range(8):
        save(a).wait()


def update(mem, pat, diag, x_row, x_col, y, g, hess):
    return pl.pallas_call(
        update_kernel,
        out_shape=(
            jax.ShapeDtypeStruct(hess.shape, f32),
            jax.ShapeDtypeStruct((8, BS), f32),
        ),
        in_specs=[SM, SM, VM, VM, VM, VM, VM, ANY],
        out_specs=(ANY, VM),
        scratch_shapes=[
            pltpu.VMEM((8, 1024, BS), f32),
            pltpu.SemaphoreType.DMA((8,)),
            pltpu.SemaphoreType.DMA((8,)),
        ],
        compiler_params=pltpu.CompilerParams(vmem_limit_bytes=32 << 20),
        name="update",
    )(mem, pat, diag, x_row, x_col, y, g, hess)


def shards(
    poses, codebook, offsets, confidence, code_ids, creature_ids, hess_raw, pattern, membership
):
    hess = hess_raw.reshape(8, 1024, BS)
    x_row, x_col, diag, y, g = exchange(
        membership, pattern, hess, poses, codebook, offsets,
        confidence.reshape(16, BS), code_ids.reshape(16, BS), creature_ids.reshape(16, BS),
    )
    state, grad = update(membership, pattern, diag, x_row, x_col, y, g, hess)
    return state.reshape(hess_raw.shape), grad.reshape(8, 1, BS)


def solution(mesh):
    return jax.shard_map(
        shards,
        mesh=mesh,
        in_specs=(
            P(("frames", "prow", "pcol"), None),
            P(),
            P(),
            P(("frames", "prow", "pcol")),
            P(("frames", "prow", "pcol")),
            P(("frames", "prow", "pcol")),
            P(None, "prow", None, None, "pcol", None),
            P(),
            P(),
        ),
        out_specs=(P(None, "prow", None, None, "pcol", None), P(None, "prow", None)),
        check_vma=False,
    )
```

```python
import math

import jax
import jax.numpy as jnp
from jax import lax
from jax.experimental import pallas as pl
from jax.experimental.pallas import tpu as pltpu
from jax.sharding import PartitionSpec as P

NPAN = 8192
BS = 128
STEPS = 4
FRAMES = 262144
CODES = 32
SHIFT = 2.5 * math.sqrt(NPAN)
PAIRS = [(k, m) for k in range(STEPS) for m in range(k + 1)]
NQ = len(PAIRS)
CHUNKS = ((0, 3), (3, 7))
WIDE = STEPS * BS
MESH = pl.DeviceIdType.MESH
precise = lax.Precision.HIGHEST
f32 = jnp.float32
bf16 = jnp.bfloat16
NT = (((1,), (1,)), ((), ()))
NN = (((1,), (0,)), ((), ()))


def loop(lo, hi, fn):
    def body(d, carry):
        fn(d)
        return carry

    lax.fori_loop(lo, hi, body, 0)


def split(x):
    hi = x.astype(bf16)
    return hi, (x - hi.astype(f32)).astype(bf16)


def dot3(a, b):
    (ah, al), (bh, bl) = a, b
    d = lambda x, y: lax.dot_general(x, y, NT, preferred_element_type=f32)
    return d(ah, bh) + (d(ah, bl) + d(al, bh))


def member(mem, k):
    return mem[k // 2, k % 2]


VM = pl.BlockSpec(memory_space=pltpu.VMEM)
SM = pl.BlockSpec(memory_space=pltpu.SMEM)
ANY = pl.BlockSpec(memory_space=pl.ANY)
HBM = pl.BlockSpec(memory_space=pltpu.HBM)


def moments(poses, codebook, offsets, conf, codes, kinds):
    ids = lax.broadcasted_iota(jnp.int32, (CODES, BS), 0)
    weights, marks = [], []
    for s in range(16):
        weights.append(jnp.where(codes[s : s + 1, :] == ids, conf[s : s + 1, :], 0.0))
        marks.append(jnp.where(kinds[s : s + 1, :] == ids, 1.0, 0.0).astype(bf16))
    weight = jnp.concatenate(weights, axis=1)
    mark = jnp.concatenate(marks, axis=1)
    parts = []
    for _ in range(3):
        parts.append(weight.astype(bf16))
        weight = weight - parts[-1].astype(f32)
    stack = jnp.concatenate(parts, axis=0)

    def total(x):
        return x[0:CODES] + (x[CODES : 2 * CODES] + x[2 * CODES : 3 * CODES])

    moment = total(lax.dot_general(stack, poses[...], NN, preferred_element_type=f32))
    pair = total(lax.dot_general(stack, mark, NT, preferred_element_type=f32))
    count = jnp.sum(pair, axis=1, keepdims=True)
    moment = moment - count * codebook[...].astype(f32)
    moment = moment - lax.dot_general(
        pair, offsets[...].astype(f32), NN, precision=precise, preferred_element_type=f32
    )
    return moment / math.sqrt(FRAMES / CODES)


def spread(row):
    return jnp.broadcast_to(row, (8, BS))


def eliminate(upper_ref, inv_ref, first, last):
    groups = BS // 8
    row_ids = lax.broadcasted_iota(jnp.int32, (8, BS), 0)
    upper = {g: upper_ref[8 * g : 8 * g + 8, :] for g in range(first, groups)}
    inv = {g: inv_ref[8 * g : 8 * g + 8, :] for g in range(first, groups)}
    for g in range(first, last):
        k = 8 * g
        v, w = upper[g], inv[g]
        cols = [jnp.broadcast_to(v[:, k + j : k + j + 1], (8, BS)) for j in range(8)]
        rows_v, rows_w, coef = [], [], []
        for j in range(8):
            pivot = spread(cols[j][j : j + 1, :])
            recip = 1.0 / pivot
            rv = spread(v[j : j + 1, :]) * recip
            rw = spread(w[j : j + 1, :]) * recip
            rows_v.append(rv)
            rows_w.append(rw)
            below = jnp.where(row_ids > j, cols[j], 0.0)
            coef.append([None] * 8)
            for t in range(j + 1, 8):
                coef[j][t] = spread(cols[t][j : j + 1, :]) * recip
                cols[t] = cols[t] - below * coef[j][t]
            v = v - below * rv
            w = w - below * rw
        upper[g], inv[g] = v, w
        for h in range(g + 1, groups):
            v, w = upper[h], inv[h]
            cols = [jnp.broadcast_to(v[:, k + j : k + j + 1], (8, BS)) for j in range(8)]
            for j in range(8):
                for t in range(j + 1, 8):
                    cols[t] = cols[t] - cols[j] * coef[j][t]
                v = v - cols[j] * rows_v[j]
                w = w - cols[j] * rows_w[j]
            upper[h], inv[h] = v, w
    for g in range(first, groups):
        upper_ref[8 * g : 8 * g + 8, :] = upper[g]
        inv_ref[8 * g : 8 * g + 8, :] = inv[g]


def dot_nt(a, b):
    return lax.dot_general(a, b, NT, precision=precise, preferred_element_type=f32)


def dot_nn(a, b):
    return lax.dot_general(a, b, (((1,), (0,)), ((), ())), precision=precise, preferred_element_type=f32)


def exchange_kernel(
    mem, pat, hess_at, poses_at, codebook_at, offsets_at, conf_at, codes_at, kinds_at,
    x_row, x_col, diag, y_out, g_out,
    hess, poses, codebook, offsets, conf, codes, kinds, scand, ccand, pg, s_all, low, inv, fac_u, fac_i, raw, wh, wl,
    s1r_a, s1r_b, s1, s2r_a, s2r_b, par_a, par_b, picked, both_a, both_b, mine, g1r, g1, g2r, g2, g3r,
    snd_s1, rcv_s1, snd_s2, rcv_s2, snd_s3, rcv_s3, snd_sx, rcv_sx,
    snd_x, rcv_x, snd_a, rcv_a, snd_r2, snd_t2, snd_t1, rcv_r, rcv_t,
    snd_g1, rcv_g1, snd_g2, rcv_g2, snd_g4, rcv_g4, snd_g3, rcv_g3, snd_b, rcv_b, snd_r1, in_sem,
):
    fetches = [
        pltpu.make_async_copy(src, dst, in_sem.at[n])
        for n, (src, dst) in enumerate(
            [
                (hess_at, hess), (codes_at, codes), (conf_at, conf), (kinds_at, kinds),
                (poses_at, poses), (codebook_at, codebook), (offsets_at, offsets),
            ]
        )
    ]
    for fetch in fetches:
        fetch.start()
    s1r, s2r = (s1r_a, s1r_b), (s2r_a, s2r_b)
    par, both = (par_a, par_b), (both_a, both_b)
    f = lax.axis_index("frames")
    r = lax.axis_index("prow")
    c = lax.axis_index("pcol")
    p = r + f * (c - r)
    q = c + f * (r - c)

    def place(p_to, q_to):
        return (f, p_to + f * (q_to - p_to), q_to + f * (p_to - q_to))

    sibling = (1 - f, r, c)

    def q_at(line, pair):
        return 2 * line + pair + f * (3 * pair - line)

    def p_at(line, pair):
        return line + 4 * pair + f * (line - 3 * pair)

    def q_parts(v):
        return v // 2 + f * (lax.rem(v, 4) - v // 2), lax.rem(v, 2) + f * (v // 4 - lax.rem(v, 2))

    def p_parts(v):
        return lax.rem(v, 4) + f * (v // 2 - lax.rem(v, 4)), v // 4 + f * (lax.rem(v, 2) - v // 4)

    ql, qh = q_parts(q)
    pl_, ph = p_parts(p)

    hub = lax.rem(pl_ + ql, 4)

    def turn(v):
        return lax.rem(v - p_parts(q)[0] + 4, 4)

    def q_line(d):
        return lax.rem(ql + d, 4)

    def p_line(d):
        return lax.rem(pl_ + d, 4)

    def copy(src, dst, snd, rcv, to):
        return pltpu.make_async_remote_copy(
            src_ref=src, dst_ref=dst, send_sem=snd, recv_sem=rcv, device_id=to, device_id_type=MESH
        )

    def q_peer(d):
        return lax.rem(q + d, 8)

    def p_peer(d):
        return lax.rem(p + d, 8)

    def c_peer(d):
        return lax.rem(c + d, 8)

    def r_peer(d):
        return lax.rem(r + d, 8)

    barrier = pltpu.get_barrier_semaphore()

    def greet(to):
        pl.semaphore_signal(barrier, inc=1, device_id=to, device_id_type=MESH)

    greet(sibling)

    def greet_line(d):
        greet(place(p, q_peer(d)))
        greet(place(p_peer(d), q))

    loop(1, 8, greet_line)

    def at_home(p_to, q_to):
        return jnp.logical_and(p_to == p, q_to == q)

    def away(p_to, q_to, fn):
        @pl.when(jnp.logical_not(at_home(p_to, q_to)))
        def _():
            fn()

    def greet_turn(e):
        away(p_at(hub, e), p, lambda: greet(place(p_at(hub, e), p)))
        away(q, q_at(turn(pl_), e), lambda: greet(place(q, q_at(turn(pl_), e))))

    loop(0, 2, greet_turn)
    same = jnp.where(jnp.logical_and(p == q, ql == 0), 1, 0)

    slot = [member(mem, k) // 8 for k in range(STEPS)]
    fetches[0].wait()
    for e, (k, m) in enumerate(PAIRS):
        scand[e] = hess[slot[k], pl.ds(slot[m], BS, stride=8), :]

    @pl.when(f == 0)
    def _():
        for k in range(2):
            for v in range(8):
                ccand[v, k] = hess[v, pl.ds(slot[k], BS, stride=8), :]

    @pl.when(f == 1)
    def _():
        for k in range(2):
            for v in range(8):
                ccand[v, k] = hess[slot[2 + k], pl.ds(v, BS, stride=8), :]

    pl.semaphore_wait(barrier, 19 - 2 * same)

    def rows_of(slice_id):
        return pl.ds(pl.multiple_of(8 * slice_id, 8), 8)

    def s1_copy(h, peer, at):
        lo, n = CHUNKS[h]
        return copy(
            scand.at[pl.ds(lo, n), rows_of(peer + 8 * f), :], s1r[h].at[at],
            snd_s1.at[h, peer], rcv_s1.at[h, at], place(p, peer),
        )

    def s2_copy(h, peer, at):
        lo, n = CHUNKS[h]
        return copy(
            s1.at[pl.ds(lo, n)], s2r[h].at[at],
            snd_s2.at[h, peer], rcv_s2.at[h, at], place(peer, q),
        )

    def s3_copy(h, peer, at):
        lo, n = CHUNKS[h]
        part = s_all.at[pl.ds(lo, n), rows_of(at + 8 * f), :]
        return copy(part, part, snd_s3.at[h, peer], rcv_s3.at[h, at], place(p, peer))

    def sx_copy(h, at, core):
        lo, n = CHUNKS[h]
        part = s_all.at[pl.ds(lo, n), rows_of(at + 8 * core), :]
        return copy(part, part, snd_sx.at[h, at], rcv_sx.at[h, at], sibling)

    def g1_copy(peer, at):
        return copy(pg.at[rows_of(peer)], g1r.at[at], snd_g1.at[peer], rcv_g1.at[at], (f, r, peer))

    def g2_copy(peer, at):
        return copy(g1, g2r.at[at], snd_g2.at[peer], rcv_g2.at[at], (f, peer, c))

    def g4_copy(peer, at):
        return copy(g_out.at[at], g_out.at[at], snd_g4.at[peer], rcv_g4.at[at], (f, r, peer))

    def a_copy(k, e, line, at):
        return copy(
            ccand.at[q_at(line, e), k], par[k].at[at, e],
            snd_a.at[2 * k + e, line], rcv_a.at[2 * k + e, at], place(p, q_at(line, qh)),
        )

    def b_copy(k):
        return copy(
            picked.at[k, 1 - qh], both[k].at[qh], snd_b.at[k], rcv_b.at[k], place(p, q_at(ql, 1 - qh))
        )

    def r1_copy(k, at):
        return copy(
            mine.at[k], raw.at[f, f, at, k], snd_r1.at[k], rcv_r.at[k, at], place(p, q_at(ql, 1 - qh))
        )

    def r2_copy(k, e, line, at):
        part = raw.at[f, f, at, k]
        return copy(part, part, snd_r2.at[2 * k + e, line], rcv_r.at[k, at], place(p, q_at(line, qh)))

    def t1_copy(k, e, at):
        return copy(
            mine.at[k], raw.at[1 - f, f, at, k], snd_t1.at[k, e], rcv_t.at[k, at], place(p_at(hub, e), p)
        )

    def t2_copy(k, e, line, at):
        part = raw.at[1 - f, f, at, k]
        return copy(part, part, snd_t2.at[2 * k + e, line], rcv_t.at[k, at], place(p_at(line, ph), q))

    def x_copy(which, at, core):
        part = raw.at[which, core, at]
        return copy(part, part, snd_x.at[which, at], rcv_x.at[which, at], sibling)

    def owner(k):
        return q_parts(lax.rem(mem[f, k], 8))

    def pick(k):
        for e in range(2):
            loop(1, 4, lambda d: a_copy(k, e, q_line(d), q_line(d)).wait())
        for e in range(2):
            picked[k, e] = par[k][owner(k)[0], e]
        b_copy(k).start()

    def spread_mine(k):
        both[k][qh] = picked[k, qh]
        b_copy(k).wait()

        @pl.when(f == 0)
        def _():
            mine[k] = both[k][lax.rem(mem[0, k], 2)]

        @pl.when(f == 1)
        def _():
            mine[k] = both[k][lax.rem(mem[1, k], 8) // 4].T

        r1_copy(k, q).start()
        for e in range(2):
            away(p_at(hub, e), p, lambda: t1_copy(k, e, q).start())
        raw[f, f, q, k] = mine[k]

        @pl.when(jnp.logical_and(p == q, ql == 0))
        def _():
            raw[1 - f, f, q, k] = mine[k]

    def spread_on(k):
        r1_copy(k, q_at(ql, 1 - qh)).wait_recv()
        for e in range(2):
            loop(1, 4, lambda d: r2_copy(k, e, q_line(d), q_at(ql, e)).start())
        for e in range(2):
            at = q_at(turn(pl_), e)
            away(q, at, lambda: t1_copy(k, e, at).wait_recv())
            loop(1, 4, lambda d: t2_copy(k, e, p_line(d), at).start())
        if k:
            for e in range(2):
                x_copy(f, q_at(ql, e), f).start()
                x_copy(1 - f, q_at(turn(pl_), e), f).start()

    for h in range(2):
        loop(1, 8, lambda d: s1_copy(h, q_peer(d), q).start())
    for k in range(2):
        for e in range(2):
            loop(1, 4, lambda d: a_copy(k, e, q_line(d), ql).start())
    for h, (lo, n) in enumerate(CHUNKS):
        s1r[h][q] = scand[lo : lo + n, rows_of(q + 8 * f), :]
    for e in range(2):
        for k in range(2):
            par[k][ql, e] = ccand[q_at(ql, e), k]
    for fetch in fetches[1:]:
        fetch.wait()
    moment = moments(poses, codebook, offsets, conf, codes, kinds)
    for half in range(2):
        pg[pl.ds(half, CODES, stride=2), :] = moment[:, BS * half : BS * half + BS]
    loop(1, 8, lambda d: g1_copy(c_peer(d), c).start())
    g1r[c] = pg[rows_of(c), :]

    for h in range(2):
        lo, n = CHUNKS[h]
        loop(1, 8, lambda d: s1_copy(h, q_peer(d), q_peer(d)).wait())
        for e in range(lo, lo + n):
            own_k = lax.rem(member(mem, PAIRS[e][0]), 8)
            own_m = lax.rem(member(mem, PAIRS[e][1]), 8)
            s1[e] = s1r[h][own_m + f * (own_k - own_m), e - lo]
        loop(1, 8, lambda d: s2_copy(h, p_peer(d), p).start())
        s2r[h][p] = s1[lo : lo + n]

    loop(1, 8, lambda d: g1_copy(c_peer(d), c_peer(d)).wait())
    g1[...] = jnp.sum(g1r[...], axis=0)
    loop(1, 8, lambda d: g2_copy(r_peer(d), r).start())
    g2r[r] = g1[...]


    for h in range(2):
        lo, n = CHUNKS[h]
        loop(1, 8, lambda d: s2_copy(h, p_peer(d), p_peer(d)).wait())
        for e in range(lo, lo + n):
            own_k = lax.rem(member(mem, PAIRS[e][0]), 8)
            own_m = lax.rem(member(mem, PAIRS[e][1]), 8)
            s_all[e, rows_of(q + 8 * f), :] = s2r[h][own_k + f * (own_m - own_k), e - lo]
        loop(1, 8, lambda d: s3_copy(h, q_peer(d), q).start())
        sx_copy(h, q, f).start()


    loop(1, 8, lambda d: g2_copy(r_peer(d), r_peer(d)).wait())
    g2[...] = jnp.sum(g2r[...], axis=0)
    g3 = copy(g2, g3r, snd_g3, rcv_g3, sibling)
    g3.start()

    def pass_on(h):
        def one(d):
            s3_copy(h, q_peer(d), q_peer(d)).wait_recv()
            sx_copy(h, q_peer(d), f).start()

        loop(1, 8, one)

    def sx_ready(h):
        loop(0, 8, lambda at: sx_copy(h, at, 1 - f).wait_recv())

    rr = lax.broadcasted_iota(jnp.int32, (BS, BS), 0)
    cc = lax.broadcasted_iota(jnp.int32, (BS, BS), 1)
    low[...] = jnp.zeros_like(low)
    inv[...] = jnp.zeros_like(inv)

    def before(k):
        if k == 0:
            sx_ready(0)
        if k == 2:
            sx_ready(1)
        if k:
            row = jnp.concatenate(
                [
                    s_all[PAIRS.index((k, m))] * pat[member(mem, k), member(mem, m)].astype(f32)
                    for m in range(k)
                ],
                axis=1,
            )
            low[k, :, 0 : BS * k] = dot_nt(row, inv[0 : BS * k, 0 : BS * k])
        value = s_all[PAIRS.index((k, k))] * pat[member(mem, k), member(mem, k)].astype(f32)
        value = value + jnp.where(rr == cc, SHIFT, 0.0)
        if k:
            lows = low[k, :, 0 : BS * k]
            value = value - dot_nt(lows, lows)
        fac_u[...] = value
        fac_i[...] = jnp.where(rr == cc, 1.0, 0.0)

    def after(k):
        at = slice(BS * k, BS * k + BS)
        inv[at, at] = fac_i[...]
        if k:
            inv[at, 0 : BS * k] = -dot_nn(fac_i[...], dot_nn(low[k, :, 0 : BS * k], inv[0 : BS * k, 0 : BS * k]))
        lower = fac_u[...].T
        low[k, :, at] = lower
        diag[k] = lower
        if k == 0:
            pass_on(1)
        if k == 1:
            spread_on(1)
        if k == 2:
            g3.wait()
            g_out[c] = g2[...] + g3r[...]
            loop(1, 8, lambda d: g4_copy(c_peer(d), c).start())

    def step(k):
        for kk in range(STEPS):
            @pl.when(k == kk)
            def _():
                before(kk)

        eliminate(fac_u, fac_i, 0, 8)

        @pl.when(k == 0)
        def _():
            spread_mine(0)
            spread_mine(1)

        @pl.when(k == 1)
        def _():
            spread_on(0)

        eliminate(fac_u, fac_i, 8, 16)
        pivots = jnp.sum(jnp.where(rr == cc, fac_u[...], 0.0), axis=1, keepdims=True)
        scale = 1.0 / jnp.sqrt(pivots)
        fac_u[...] = jnp.where(cc >= rr, fac_u[...] * scale, 0.0)
        fac_i[...] = fac_i[...] * scale
        for kk in range(STEPS):
            @pl.when(k == kk)
            def _():
                after(kk)

    pick(0)
    pick(1)
    pass_on(0)
    loop(0, STEPS, step)

    def arrives(d):
        for e in range(2):
            at = q_at(q_line(d), e)
            for k in range(2):
                r2_copy(k, e, q_line(d), at).wait_recv()
            x_copy(f, at, f).start()
            at = q_at(turn(p_line(d)), e)
            for k in range(2):
                t2_copy(k, e, p_line(d), at).wait_recv()
            x_copy(1 - f, at, f).start()

    loop(1, 4, arrives)

    h, l = split(inv[...])
    wh[...] = h
    wl[...] = l
    half = 2 * BS
    w11 = (wh[0:half, 0:half], wl[0:half, 0:half])
    w21 = (wh[half:, 0:half], wl[half:, 0:half])
    w22 = (wh[half:, half:], wl[half:, half:])

    loop(1, 8, lambda d: g4_copy(c_peer(d), c_peer(d)).wait_recv())
    gp = jnp.concatenate(
        [g_out[member(mem, k) // 8, pl.ds(lax.rem(member(mem, k), 8), 1), :] for k in range(STEPS)], axis=1
    )
    gp = jnp.broadcast_to(gp, (16, WIDE))
    y_out[...] = dot3(split(gp), (wh[...], wl[...]))[0:8]

    def store(which, rows, at, x):
        hi, rest = split(x)
        for target, parts in ((x_row, (hi, rest, hi)), (x_col, (hi, hi, rest))):
            @pl.when(which == (1 if target is x_col else 0))
            def _():
                for n, part in enumerate(parts):
                    target[rows, WIDE * n + at : WIDE * n + at + half] = part

    def panel(which, t):
        base = r + which * (c - r)
        ones, twos, keeps = [], [], []
        for e in range(2):
            a = 2 * t + e
            x_copy(which, a, 1 - f).wait_recv()
        for e in range(2):
            a = 2 * t + e
            i = 8 * a + base
            pivot = i == member(mem, 0)
            for k in range(1, STEPS):
                pivot = jnp.logical_or(pivot, i == member(mem, k))
            z = jnp.where(pivot, 0.0, 1.0).astype(f32)
            m1 = z * pat[i, member(mem, 0)].astype(f32)
            m2 = z * pat[i, member(mem, 2)].astype(f32)
            ones.append(jnp.concatenate([raw[which, 0, a, 0], raw[which, 0, a, 1]], axis=1) * m1)
            twos.append(jnp.concatenate([raw[which, 1, a, 0], raw[which, 1, a, 1]], axis=1))
            keeps.append(m2)
        one = split(jnp.concatenate(ones, axis=0))
        two = split(jnp.concatenate(twos, axis=0))
        second = dot3(one, w21) + dot3(two, w22)
        rows = pl.ds(pl.multiple_of(half * t, half), half)
        store(which, rows, 0, dot3(one, w11))
        second = jnp.concatenate([second[0:BS] * keeps[0], second[BS:half] * keeps[1]], axis=0)
        store(which, rows, half, second)

    loop(0, 8, lambda t: panel(t // 4, lax.rem(t, 4)))

    def tail(d):
        for h in range(2):
            s3_copy(h, q_peer(d), q).wait_send()
        g4_copy(c_peer(d), c).wait_send()

    loop(1, 8, tail)
    for k in range(2):
        r1_copy(k, q).wait_send()
        for e in range(2):
            away(p_at(hub, e), p, lambda: t1_copy(k, e, q).wait_send())

    def tail_line(d):
        for k in range(2):
            for e in range(2):
                r2_copy(k, e, q_line(d), q_at(ql, e)).wait_send()
                t2_copy(k, e, p_line(d), q_at(turn(pl_), e)).wait_send()

    loop(1, 4, tail_line)

    def tail_pair(d):
        for h in range(2):
            sx_copy(h, d, f).wait_send()
        for which in range(2):
            x_copy(which, d, f).wait_send()

    loop(0, 8, tail_pair)


def exchange(mem, pat, *operands):
    vmem = pltpu.VMEM
    sem = pltpu.SemaphoreType.DMA
    return pl.pallas_call(
        exchange_kernel,
        out_shape=(
            jax.ShapeDtypeStruct((1024, 3 * WIDE), bf16),
            jax.ShapeDtypeStruct((1024, 3 * WIDE), bf16),
            jax.ShapeDtypeStruct((STEPS, BS, BS), f32),
            jax.ShapeDtypeStruct((8, WIDE), f32),
            jax.ShapeDtypeStruct((8, 8, BS), f32),
        ),
        in_specs=[SM, SM] + [HBM] * 7,
        out_specs=(VM,) * 5,
        scratch_shapes=[vmem(x.shape, x.dtype) for x in operands]
        + [
            vmem((NQ, BS, BS), f32),
            vmem((8, 2, BS, BS), f32),
            vmem((64, BS), f32),
            vmem((NQ, BS, BS), f32),
            vmem((STEPS, BS, WIDE), f32),
            vmem((WIDE, WIDE), f32),
            vmem((BS, BS), f32),
            vmem((BS, BS), f32),
            vmem((2, 2, 8, 2, BS, BS), f32),
            vmem((WIDE, WIDE), bf16),
            vmem((WIDE, WIDE), bf16),
            vmem((8, CHUNKS[0][1], 8, BS), f32),
            vmem((8, CHUNKS[1][1], 8, BS), f32),
            vmem((NQ, 8, BS), f32),
            vmem((8, CHUNKS[0][1], 8, BS), f32),
            vmem((8, CHUNKS[1][1], 8, BS), f32),
            vmem((4, 2, BS, BS), f32),
            vmem((4, 2, BS, BS), f32),
            vmem((2, 2, BS, BS), f32),
            vmem((2, BS, BS), f32),
            vmem((2, BS, BS), f32),
            vmem((2, BS, BS), f32),
            vmem((8, 8, BS), f32),
            vmem((8, BS), f32),
            vmem((8, 8, BS), f32),
            vmem((8, BS), f32),
            vmem((8, BS), f32),
        ]
        + [sem((2, 8))] * 10
        + [sem((4, 4))] * 4
        + [sem((2, 2))]
        + [sem((2, 8))] * 2
        + [sem((8,))] * 6
        + [sem] * 2
        + [sem((2,))] * 3
        + [sem((7,))],
        compiler_params=pltpu.CompilerParams(
            collective_id=0, has_side_effects=True, vmem_limit_bytes=40 << 20
        ),
        name="exchange",
    )(mem, pat, *(pltpu.with_memory_space_constraint(x, pltpu.HBM) for x in operands))


def update_kernel(mem, pat, diag, x_row, x_col, y, g, hess, out, grad_out, rows, in_sem, out_sem):
    r = lax.axis_index("prow")
    c = lax.axis_index("pcol")

    def load(a):
        return pltpu.make_async_copy(hess.at[a], rows.at[a], in_sem.at[a])

    def save(a):
        return pltpu.make_async_copy(rows.at[a], out.at[a], out_sem.at[a])

    for a in range(8):
        load(a).start()

    def is_pivot(i):
        pivot = i == member(mem, 0)
        for k in range(1, STEPS):
            pivot = jnp.logical_or(pivot, i == member(mem, k))
        return pivot

    dec = dot3(split(jnp.concatenate([y[...], y[...]], axis=0)), (x_row[:, 0:WIDE], x_row[:, WIDE : 2 * WIDE]))
    for a in range(8):
        i = 8 * a + r
        val = g[a, pl.ds(r, 1), :] - dec[0:1, BS * a : BS * a + BS]
        for k in range(STEPS):
            val = jnp.where(i == member(mem, k), y[0:1, BS * k : BS * k + BS], val)
        grad_out[a : a + 1, :] = val

    rr = lax.broadcasted_iota(jnp.int32, (BS, BS), 0)
    cc = lax.broadcasted_iota(jnp.int32, (BS, BS), 1)
    shift = jnp.where(rr == cc, SHIFT, 0.0)

    def two_rows(t):
        at = pl.ds(pl.multiple_of(2 * BS * t, 2 * BS), 2 * BS)
        upd = lax.dot_general(x_row[at, :], x_col[...], NT, preferred_element_type=f32)
        for e in range(2):
            a = 2 * t + e
            i = 8 * a + r
            live = jnp.where(is_pivot(i), 0.0, 1.0).astype(f32)
            load(a).wait()
            for b in range(8):
                j = 8 * b + c
                keep = live * pat[i, j].astype(f32)
                on = jnp.where(i == j, 1.0, 0.0).astype(f32) * live
                sub = upd[BS * e : BS * e + BS, BS * b : BS * b + BS]
                there = pl.ds(b, BS, stride=8)
                rows[a, there, :] = keep * (rows[a, there, :] - sub) + on * shift
            for k in range(STEPS):
                pk = member(mem, k)

                @pl.when(lax.rem(pk, 8) == c)
                def _():
                    there = pl.ds(pk // 8, BS, stride=8)
                    mine = pl.ds(pl.multiple_of(BS * a, BS), BS)
                    part = slice(BS * k, BS * k + BS)
                    rest = slice(WIDE + BS * k, WIDE + BS * k + BS)

                    @pl.when(i != pk)
                    def _():
                        rows[a, there, :] = x_row[mine, part].astype(f32) + x_row[mine, rest].astype(f32)

                    @pl.when(i == pk)
                    def _():
                        rows[a, there, :] = diag[k]
            save(a).start()

    loop(0, 4, two_rows)
    for a in range(8):
        save(a).wait()


def update(mem, pat, diag, x_row, x_col, y, g, hess):
    return pl.pallas_call(
        update_kernel,
        out_shape=(
            jax.ShapeDtypeStruct(hess.shape, f32),
            jax.ShapeDtypeStruct((8, BS), f32),
        ),
        in_specs=[SM, SM, VM, VM, VM, VM, VM, ANY],
        out_specs=(ANY, VM),
        scratch_shapes=[
            pltpu.VMEM((8, 1024, BS), f32),
            pltpu.SemaphoreType.DMA((8,)),
            pltpu.SemaphoreType.DMA((8,)),
        ],
        compiler_params=pltpu.CompilerParams(vmem_limit_bytes=32 << 20),
        name="update",
    )(mem, pat, diag, x_row, x_col, y, g, hess)


def shards(
    poses, codebook, offsets, confidence, code_ids, creature_ids, hess_raw, pattern, membership
):
    hess = hess_raw.reshape(8, 1024, BS)
    x_row, x_col, diag, y, g = exchange(
        membership, pattern, hess, poses, codebook, offsets,
        confidence.reshape(16, BS), code_ids.reshape(16, BS), creature_ids.reshape(16, BS),
    )
    state, grad = update(membership, pattern, diag, x_row, x_col, y, g, hess)
    return state.reshape(hess_raw.shape), grad.reshape(8, 1, BS)


def solution(mesh):
    return jax.shard_map(
        shards,
        mesh=mesh,
        in_specs=(
            P(("frames", "prow", "pcol"), None),
            P(),
            P(),
            P(("frames", "prow", "pcol")),
            P(("frames", "prow", "pcol")),
            P(("frames", "prow", "pcol")),
            P(None, "prow", None, None, "pcol", None),
            P(),
            P(),
        ),
        out_specs=(P(None, "prow", None, None, "pcol", None), P(None, "prow", None)),
        check_vma=False,
    )
```

```python
import math

import jax
import jax.numpy as jnp
from jax import lax
from jax.experimental import pallas as pl
from jax.experimental.pallas import tpu as pltpu
from jax.sharding import PartitionSpec as P

NPAN = 8192
BS = 128
STEPS = 4
FRAMES = 262144
CODES = 32
SHIFT = 2.5 * math.sqrt(NPAN)
PAIRS = [(k, m) for k in range(STEPS) for m in range(k + 1)]
NQ = len(PAIRS)
CHUNKS = ((0, 3), (3, 7))
WIDE = STEPS * BS
MESH = pl.DeviceIdType.MESH
precise = lax.Precision.HIGHEST
f32 = jnp.float32
bf16 = jnp.bfloat16
NT = (((1,), (1,)), ((), ()))
NN = (((1,), (0,)), ((), ()))


def loop(lo, hi, fn):
    def body(d, carry):
        fn(d)
        return carry

    lax.fori_loop(lo, hi, body, 0)


def split(x):
    hi = x.astype(bf16)
    return hi, (x - hi.astype(f32)).astype(bf16)


def dot3(a, b):
    (ah, al), (bh, bl) = a, b
    d = lambda x, y: lax.dot_general(x, y, NT, preferred_element_type=f32)
    return d(ah, bh) + (d(ah, bl) + d(al, bh))


def member(mem, k):
    return mem[k // 2, k % 2]


VM = pl.BlockSpec(memory_space=pltpu.VMEM)
SM = pl.BlockSpec(memory_space=pltpu.SMEM)
ANY = pl.BlockSpec(memory_space=pl.ANY)
HBM = pl.BlockSpec(memory_space=pltpu.HBM)


def moments(poses, codebook, offsets, conf, codes, kinds):
    ids = lax.broadcasted_iota(jnp.int32, (CODES, BS), 0)
    weights, marks = [], []
    for s in range(16):
        weights.append(jnp.where(codes[s : s + 1, :] == ids, conf[s : s + 1, :], 0.0))
        marks.append(jnp.where(kinds[s : s + 1, :] == ids, 1.0, 0.0).astype(bf16))
    weight = jnp.concatenate(weights, axis=1)
    mark = jnp.concatenate(marks, axis=1)
    parts = []
    for _ in range(3):
        parts.append(weight.astype(bf16))
        weight = weight - parts[-1].astype(f32)
    stack = jnp.concatenate(parts, axis=0)

    def total(x):
        return x[0:CODES] + (x[CODES : 2 * CODES] + x[2 * CODES : 3 * CODES])

    moment = total(lax.dot_general(stack, poses[...], NN, preferred_element_type=f32))
    pair = total(lax.dot_general(stack, mark, NT, preferred_element_type=f32))
    count = jnp.sum(pair, axis=1, keepdims=True)
    moment = moment - count * codebook[...].astype(f32)
    moment = moment - lax.dot_general(
        pair, offsets[...].astype(f32), NN, precision=precise, preferred_element_type=f32
    )
    return moment / math.sqrt(FRAMES / CODES)


def spread(row):
    return jnp.broadcast_to(row, (8, BS))


def eliminate(upper_ref, inv_ref, first, last):
    groups = BS // 8
    row_ids = lax.broadcasted_iota(jnp.int32, (8, BS), 0)
    upper = {g: upper_ref[8 * g : 8 * g + 8, :] for g in range(first, groups)}
    inv = {g: inv_ref[8 * g : 8 * g + 8, :] for g in range(first, groups)}
    for g in range(first, last):
        k = 8 * g
        v, w = upper[g], inv[g]
        cols = [jnp.broadcast_to(v[:, k + j : k + j + 1], (8, BS)) for j in range(8)]
        rows_v, rows_w, coef = [], [], []
        for j in range(8):
            pivot = spread(cols[j][j : j + 1, :])
            recip = 1.0 / pivot
            rv = spread(v[j : j + 1, :]) * recip
            rw = spread(w[j : j + 1, :]) * recip
            rows_v.append(rv)
            rows_w.append(rw)
            below = jnp.where(row_ids > j, cols[j], 0.0)
            coef.append([None] * 8)
            for t in range(j + 1, 8):
                coef[j][t] = spread(cols[t][j : j + 1, :]) * recip
                cols[t] = cols[t] - below * coef[j][t]
            v = v - below * rv
            w = w - below * rw
        upper[g], inv[g] = v, w
        for h in range(g + 1, groups):
            v, w = upper[h], inv[h]
            cols = [jnp.broadcast_to(v[:, k + j : k + j + 1], (8, BS)) for j in range(8)]
            for j in range(8):
                for t in range(j + 1, 8):
                    cols[t] = cols[t] - cols[j] * coef[j][t]
                v = v - cols[j] * rows_v[j]
                w = w - cols[j] * rows_w[j]
            upper[h], inv[h] = v, w
    for g in range(first, groups):
        upper_ref[8 * g : 8 * g + 8, :] = upper[g]
        inv_ref[8 * g : 8 * g + 8, :] = inv[g]


def dot_nt(a, b):
    return lax.dot_general(a, b, NT, precision=precise, preferred_element_type=f32)


def dot_nn(a, b):
    return lax.dot_general(a, b, (((1,), (0,)), ((), ())), precision=precise, preferred_element_type=f32)


def exchange_kernel(
    mem, pat, hess_at, poses_at, codebook_at, offsets_at, conf_at, codes_at, kinds_at,
    x_row, x_col, diag, y_out, g_out,
    hess, poses, codebook, offsets, conf, codes, kinds, scand, ccand, pg, s_all, low, inv, fac_u, fac_i, raw, wh, wl,
    s1r_a, s1r_b, s1, s2r_a, s2r_b, par_a, par_b, picked, both_a, both_b, mine, g1r, g1, g2r, g2, g3r,
    snd_s1, rcv_s1, snd_s2, rcv_s2, snd_s3, rcv_s3, snd_sx, rcv_sx,
    snd_x, rcv_x, snd_a, rcv_a, snd_r2, snd_t2, snd_t1, rcv_r, rcv_t,
    snd_g1, rcv_g1, snd_g2, rcv_g2, snd_g4, rcv_g4, snd_g3, rcv_g3, snd_b, rcv_b, snd_r1, in_sem,
):
    fetches = [
        pltpu.make_async_copy(src, dst, in_sem.at[n])
        for n, (src, dst) in enumerate(
            [
                (hess_at, hess), (codes_at, codes), (conf_at, conf), (kinds_at, kinds),
                (poses_at, poses), (codebook_at, codebook), (offsets_at, offsets),
            ]
        )
    ]
    for fetch in fetches:
        fetch.start()
    s1r, s2r = (s1r_a, s1r_b), (s2r_a, s2r_b)
    par, both = (par_a, par_b), (both_a, both_b)
    f = lax.axis_index("frames")
    r = lax.axis_index("prow")
    c = lax.axis_index("pcol")
    p = r + f * (c - r)
    q = c + f * (r - c)

    def place(p_to, q_to):
        return (f, p_to + f * (q_to - p_to), q_to + f * (p_to - q_to))

    sibling = (1 - f, r, c)

    def q_at(line, pair):
        return 2 * line + pair + f * (3 * pair - line)

    def p_at(line, pair):
        return line + 4 * pair + f * (line - 3 * pair)

    def q_parts(v):
        return v // 2 + f * (lax.rem(v, 4) - v // 2), lax.rem(v, 2) + f * (v // 4 - lax.rem(v, 2))

    def p_parts(v):
        return lax.rem(v, 4) + f * (v // 2 - lax.rem(v, 4)), v // 4 + f * (lax.rem(v, 2) - v // 4)

    ql, qh = q_parts(q)
    pl_, ph = p_parts(p)

    hub = lax.rem(pl_ + ql, 4)

    def turn(v):
        return lax.rem(v - p_parts(q)[0] + 4, 4)

    def q_line(d):
        return lax.rem(ql + d, 4)

    def p_line(d):
        return lax.rem(pl_ + d, 4)

    def copy(src, dst, snd, rcv, to):
        return pltpu.make_async_remote_copy(
            src_ref=src, dst_ref=dst, send_sem=snd, recv_sem=rcv, device_id=to, device_id_type=MESH
        )

    def q_peer(d):
        return lax.rem(q + d, 8)

    def p_peer(d):
        return lax.rem(p + d, 8)

    def c_peer(d):
        return lax.rem(c + d, 8)

    def r_peer(d):
        return lax.rem(r + d, 8)

    barrier = pltpu.get_barrier_semaphore()

    def greet(to):
        pl.semaphore_signal(barrier, inc=1, device_id=to, device_id_type=MESH)

    greet(sibling)

    def greet_line(d):
        greet(place(p, q_peer(d)))
        greet(place(p_peer(d), q))

    loop(1, 8, greet_line)

    def at_home(p_to, q_to):
        return jnp.logical_and(p_to == p, q_to == q)

    def away(p_to, q_to, fn):
        @pl.when(jnp.logical_not(at_home(p_to, q_to)))
        def _():
            fn()

    def greet_turn(e):
        away(p_at(hub, e), p, lambda: greet(place(p_at(hub, e), p)))
        away(q, q_at(turn(pl_), e), lambda: greet(place(q, q_at(turn(pl_), e))))

    loop(0, 2, greet_turn)
    same = jnp.where(jnp.logical_and(p == q, ql == 0), 1, 0)

    slot = [member(mem, k) // 8 for k in range(STEPS)]
    fetches[0].wait()
    for e, (k, m) in enumerate(PAIRS):
        scand[e] = hess[slot[k], pl.ds(slot[m], BS, stride=8), :]

    @pl.when(f == 0)
    def _():
        for k in range(2):
            for v in range(8):
                ccand[v, k] = hess[v, pl.ds(slot[k], BS, stride=8), :]

    @pl.when(f == 1)
    def _():
        for k in range(2):
            for v in range(8):
                ccand[v, k] = hess[slot[2 + k], pl.ds(v, BS, stride=8), :]

    pl.semaphore_wait(barrier, 19 - 2 * same)

    def rows_of(slice_id):
        return pl.ds(pl.multiple_of(8 * slice_id, 8), 8)

    def s1_copy(h, peer, at):
        lo, n = CHUNKS[h]
        return copy(
            scand.at[pl.ds(lo, n), rows_of(peer + 8 * f), :], s1r[h].at[at],
            snd_s1.at[h, peer], rcv_s1.at[h, at], place(p, peer),
        )

    def s2_copy(h, peer, at):
        lo, n = CHUNKS[h]
        return copy(
            s1.at[pl.ds(lo, n)], s2r[h].at[at],
            snd_s2.at[h, peer], rcv_s2.at[h, at], place(peer, q),
        )

    def s3_copy(h, peer, at):
        lo, n = CHUNKS[h]
        part = s_all.at[pl.ds(lo, n), rows_of(at + 8 * f), :]
        return copy(part, part, snd_s3.at[h, peer], rcv_s3.at[h, at], place(p, peer))

    def sx_copy(h, at, core):
        lo, n = CHUNKS[h]
        part = s_all.at[pl.ds(lo, n), rows_of(at + 8 * core), :]
        return copy(part, part, snd_sx.at[h, at], rcv_sx.at[h, at], sibling)

    def g1_copy(peer, at):
        return copy(pg.at[rows_of(peer)], g1r.at[at], snd_g1.at[peer], rcv_g1.at[at], (f, r, peer))

    def g2_copy(peer, at):
        return copy(g1, g2r.at[at], snd_g2.at[peer], rcv_g2.at[at], (f, peer, c))

    def g4_copy(peer, at):
        return copy(g_out.at[at], g_out.at[at], snd_g4.at[peer], rcv_g4.at[at], (f, r, peer))

    def a_copy(k, e, line, at):
        return copy(
            ccand.at[q_at(line, e), k], par[k].at[at, e],
            snd_a.at[2 * k + e, line], rcv_a.at[2 * k + e, at], place(p, q_at(line, qh)),
        )

    def b_copy(k):
        return copy(
            picked.at[k, 1 - qh], both[k].at[qh], snd_b.at[k], rcv_b.at[k], place(p, q_at(ql, 1 - qh))
        )

    def r1_copy(k, at):
        return copy(
            mine.at[k], raw.at[f, f, at, k], snd_r1.at[k], rcv_r.at[k, at], place(p, q_at(ql, 1 - qh))
        )

    def r2_copy(k, e, line, at):
        part = raw.at[f, f, at, k]
        return copy(part, part, snd_r2.at[2 * k + e, line], rcv_r.at[k, at], place(p, q_at(line, qh)))

    def t1_copy(k, e, at):
        return copy(
            mine.at[k], raw.at[1 - f, f, at, k], snd_t1.at[k, e], rcv_t.at[k, at], place(p_at(hub, e), p)
        )

    def t2_copy(k, e, line, at):
        part = raw.at[1 - f, f, at, k]
        return copy(part, part, snd_t2.at[2 * k + e, line], rcv_t.at[k, at], place(p_at(line, ph), q))

    def x_copy(which, at, core):
        part = raw.at[which, core, at]
        return copy(part, part, snd_x.at[which, at], rcv_x.at[which, at], sibling)

    def owner(k):
        return q_parts(lax.rem(mem[f, k], 8))

    def pick(k):
        for e in range(2):
            loop(1, 4, lambda d: a_copy(k, e, q_line(d), q_line(d)).wait())
        for e in range(2):
            picked[k, e] = par[k][owner(k)[0], e]
        b_copy(k).start()

    def spread_mine(k):
        both[k][qh] = picked[k, qh]
        b_copy(k).wait()

        @pl.when(f == 0)
        def _():
            mine[k] = both[k][lax.rem(mem[0, k], 2)]

        @pl.when(f == 1)
        def _():
            mine[k] = both[k][lax.rem(mem[1, k], 8) // 4].T

        r1_copy(k, q).start()
        for e in range(2):
            away(p_at(hub, e), p, lambda: t1_copy(k, e, q).start())
        raw[f, f, q, k] = mine[k]

        @pl.when(jnp.logical_and(p == q, ql == 0))
        def _():
            raw[1 - f, f, q, k] = mine[k]

    def spread_on(k):
        r1_copy(k, q_at(ql, 1 - qh)).wait_recv()
        for e in range(2):
            loop(1, 4, lambda d: r2_copy(k, e, q_line(d), q_at(ql, e)).start())
        for e in range(2):
            at = q_at(turn(pl_), e)
            away(q, at, lambda: t1_copy(k, e, at).wait_recv())
            loop(1, 4, lambda d: t2_copy(k, e, p_line(d), at).start())
        if k:
            for e in range(2):
                x_copy(f, q_at(ql, e), f).start()
                x_copy(1 - f, q_at(turn(pl_), e), f).start()

    for h in range(2):
        loop(1, 8, lambda d: s1_copy(h, q_peer(d), q).start())
    for k in range(2):
        for e in range(2):
            loop(1, 4, lambda d: a_copy(k, e, q_line(d), ql).start())
    for h, (lo, n) in enumerate(CHUNKS):
        s1r[h][q] = scand[lo : lo + n, rows_of(q + 8 * f), :]
    for e in range(2):
        for k in range(2):
            par[k][ql, e] = ccand[q_at(ql, e), k]
    for fetch in fetches[1:]:
        fetch.wait()
    moment = moments(poses, codebook, offsets, conf, codes, kinds)
    for half in range(2):
        pg[pl.ds(half, CODES, stride=2), :] = moment[:, BS * half : BS * half + BS]
    loop(1, 8, lambda d: g1_copy(c_peer(d), c).start())
    g1r[c] = pg[rows_of(c), :]

    for h in range(2):
        lo, n = CHUNKS[h]
        loop(1, 8, lambda d: s1_copy(h, q_peer(d), q_peer(d)).wait())
        for e in range(lo, lo + n):
            own_k = lax.rem(member(mem, PAIRS[e][0]), 8)
            own_m = lax.rem(member(mem, PAIRS[e][1]), 8)
            s1[e] = s1r[h][own_m + f * (own_k - own_m), e - lo]
        loop(1, 8, lambda d: s2_copy(h, p_peer(d), p).start())
        s2r[h][p] = s1[lo : lo + n]

    loop(1, 8, lambda d: g1_copy(c_peer(d), c_peer(d)).wait())
    g1[...] = jnp.sum(g1r[...], axis=0)
    loop(1, 8, lambda d: g2_copy(r_peer(d), r).start())
    g2r[r] = g1[...]


    for h in range(2):
        lo, n = CHUNKS[h]
        loop(1, 8, lambda d: s2_copy(h, p_peer(d), p_peer(d)).wait())
        for e in range(lo, lo + n):
            own_k = lax.rem(member(mem, PAIRS[e][0]), 8)
            own_m = lax.rem(member(mem, PAIRS[e][1]), 8)
            s_all[e, rows_of(q + 8 * f), :] = s2r[h][own_k + f * (own_m - own_k), e - lo]
        loop(1, 8, lambda d: s3_copy(h, q_peer(d), q).start())
        sx_copy(h, q, f).start()


    loop(1, 8, lambda d: g2_copy(r_peer(d), r_peer(d)).wait())
    g2[...] = jnp.sum(g2r[...], axis=0)
    g3 = copy(g2, g3r, snd_g3, rcv_g3, sibling)
    g3.start()

    def pass_on(h):
        def one(d):
            s3_copy(h, q_peer(d), q_peer(d)).wait_recv()
            sx_copy(h, q_peer(d), f).start()

        loop(1, 8, one)

    def sx_ready(h):
        loop(0, 8, lambda at: sx_copy(h, at, 1 - f).wait_recv())

    rr = lax.broadcasted_iota(jnp.int32, (BS, BS), 0)
    cc = lax.broadcasted_iota(jnp.int32, (BS, BS), 1)
    low[...] = jnp.zeros_like(low)
    inv[...] = jnp.zeros_like(inv)

    def before(k):
        if k == 0:
            sx_ready(0)
        if k == 2:
            sx_ready(1)
        if k:
            row = jnp.concatenate(
                [
                    s_all[PAIRS.index((k, m))] * pat[member(mem, k), member(mem, m)].astype(f32)
                    for m in range(k)
                ],
                axis=1,
            )
            low[k, :, 0 : BS * k] = dot_nt(row, inv[0 : BS * k, 0 : BS * k])
        value = s_all[PAIRS.index((k, k))] * pat[member(mem, k), member(mem, k)].astype(f32)
        value = value + jnp.where(rr == cc, SHIFT, 0.0)
        if k:
            lows = low[k, :, 0 : BS * k]
            value = value - dot_nt(lows, lows)
        fac_u[...] = value
        fac_i[...] = jnp.where(rr == cc, 1.0, 0.0)

    def after(k):
        at = slice(BS * k, BS * k + BS)
        inv[at, at] = fac_i[...]
        if k:
            inv[at, 0 : BS * k] = -dot_nn(fac_i[...], dot_nn(low[k, :, 0 : BS * k], inv[0 : BS * k, 0 : BS * k]))
        lower = fac_u[...].T
        low[k, :, at] = lower
        diag[k] = lower
        if k == 0:
            pass_on(1)
        if k == 1:
            spread_on(1)
        if k == 2:
            g3.wait()
            g_out[c] = g2[...] + g3r[...]
            loop(1, 8, lambda d: g4_copy(c_peer(d), c).start())

    def step(k):
        for kk in range(STEPS):
            @pl.when(k == kk)
            def _():
                before(kk)

        eliminate(fac_u, fac_i, 0, 8)

        @pl.when(k == 0)
        def _():
            spread_mine(0)
            spread_mine(1)

        @pl.when(k == 1)
        def _():
            spread_on(0)

        eliminate(fac_u, fac_i, 8, 16)
        pivots = jnp.sum(jnp.where(rr == cc, fac_u[...], 0.0), axis=1, keepdims=True)
        scale = 1.0 / jnp.sqrt(pivots)
        fac_u[...] = jnp.where(cc >= rr, fac_u[...] * scale, 0.0)
        fac_i[...] = fac_i[...] * scale
        for kk in range(STEPS):
            @pl.when(k == kk)
            def _():
                after(kk)

    pick(0)
    pick(1)
    pass_on(0)
    loop(0, STEPS, step)

    def arrives(d):
        for e in range(2):
            at = q_at(q_line(d), e)
            for k in range(2):
                r2_copy(k, e, q_line(d), at).wait_recv()
            x_copy(f, at, f).start()
            at = q_at(turn(p_line(d)), e)
            for k in range(2):
                t2_copy(k, e, p_line(d), at).wait_recv()
            x_copy(1 - f, at, f).start()

    loop(1, 4, arrives)

    h, l = split(inv[...])
    wh[...] = h
    wl[...] = l
    half = 2 * BS
    w11 = (wh[0:half, 0:half], wl[0:half, 0:half])
    w21 = (wh[half:, 0:half], wl[half:, 0:half])
    w22 = (wh[half:, half:], wl[half:, half:])

    loop(1, 8, lambda d: g4_copy(c_peer(d), c_peer(d)).wait_recv())
    gp = jnp.concatenate(
        [g_out[member(mem, k) // 8, pl.ds(lax.rem(member(mem, k), 8), 1), :] for k in range(STEPS)], axis=1
    )
    gp = jnp.broadcast_to(gp, (16, WIDE))
    y_out[...] = dot3(split(gp), (wh[...], wl[...]))[0:8]

    def store(which, rows, at, x):
        hi, rest = split(x)
        for target, parts in ((x_row, (hi, rest, hi)), (x_col, (hi, hi, rest))):
            @pl.when(which == (1 if target is x_col else 0))
            def _():
                for n, part in enumerate(parts):
                    target[rows, WIDE * n + at : WIDE * n + at + half] = part

    def panel(which, t):
        base = r + which * (c - r)
        ones, twos, keeps = [], [], []
        for e in range(2):
            a = 2 * t + e
            x_copy(which, a, 1 - f).wait_recv()
        for e in range(2):
            a = 2 * t + e
            i = 8 * a + base
            pivot = i == member(mem, 0)
            for k in range(1, STEPS):
                pivot = jnp.logical_or(pivot, i == member(mem, k))
            z = jnp.where(pivot, 0.0, 1.0).astype(f32)
            m1 = z * pat[i, member(mem, 0)].astype(f32)
            m2 = z * pat[i, member(mem, 2)].astype(f32)
            ones.append(jnp.concatenate([raw[which, 0, a, 0], raw[which, 0, a, 1]], axis=1) * m1)
            twos.append(jnp.concatenate([raw[which, 1, a, 0], raw[which, 1, a, 1]], axis=1))
            keeps.append(m2)
        one = split(jnp.concatenate(ones, axis=0))
        two = split(jnp.concatenate(twos, axis=0))
        second = dot3(one, w21) + dot3(two, w22)
        rows = pl.ds(pl.multiple_of(half * t, half), half)
        store(which, rows, 0, dot3(one, w11))
        second = jnp.concatenate([second[0:BS] * keeps[0], second[BS:half] * keeps[1]], axis=0)
        store(which, rows, half, second)

    loop(0, 8, lambda t: panel(t // 4, lax.rem(t, 4)))

    def tail(d):
        for h in range(2):
            s3_copy(h, q_peer(d), q).wait_send()
        g4_copy(c_peer(d), c).wait_send()

    loop(1, 8, tail)
    for k in range(2):
        r1_copy(k, q).wait_send()
        for e in range(2):
            away(p_at(hub, e), p, lambda: t1_copy(k, e, q).wait_send())

    def tail_line(d):
        for k in range(2):
            for e in range(2):
                r2_copy(k, e, q_line(d), q_at(ql, e)).wait_send()
                t2_copy(k, e, p_line(d), q_at(turn(pl_), e)).wait_send()

    loop(1, 4, tail_line)

    def tail_pair(d):
        for h in range(2):
            sx_copy(h, d, f).wait_send()
        for which in range(2):
            x_copy(which, d, f).wait_send()

    loop(0, 8, tail_pair)


def exchange(mem, pat, *operands):
    vmem = pltpu.VMEM
    sem = pltpu.SemaphoreType.DMA
    return pl.pallas_call(
        exchange_kernel,
        out_shape=(
            jax.ShapeDtypeStruct((1024, 3 * WIDE), bf16),
            jax.ShapeDtypeStruct((1024, 3 * WIDE), bf16),
            jax.ShapeDtypeStruct((STEPS, BS, BS), f32),
            jax.ShapeDtypeStruct((8, WIDE), f32),
            jax.ShapeDtypeStruct((8, 8, BS), f32),
        ),
        in_specs=[SM, SM] + [HBM] * 7,
        out_specs=(VM,) * 5,
        scratch_shapes=[vmem(x.shape, x.dtype) for x in operands]
        + [
            vmem((NQ, BS, BS), f32),
            vmem((8, 2, BS, BS), f32),
            vmem((64, BS), f32),
            vmem((NQ, BS, BS), f32),
            vmem((STEPS, BS, WIDE), f32),
            vmem((WIDE, WIDE), f32),
            vmem((BS, BS), f32),
            vmem((BS, BS), f32),
            vmem((2, 2, 8, 2, BS, BS), f32),
            vmem((WIDE, WIDE), bf16),
            vmem((WIDE, WIDE), bf16),
            vmem((8, CHUNKS[0][1], 8, BS), f32),
            vmem((8, CHUNKS[1][1], 8, BS), f32),
            vmem((NQ, 8, BS), f32),
            vmem((8, CHUNKS[0][1], 8, BS), f32),
            vmem((8, CHUNKS[1][1], 8, BS), f32),
            vmem((4, 2, BS, BS), f32),
            vmem((4, 2, BS, BS), f32),
            vmem((2, 2, BS, BS), f32),
            vmem((2, BS, BS), f32),
            vmem((2, BS, BS), f32),
            vmem((2, BS, BS), f32),
            vmem((8, 8, BS), f32),
            vmem((8, BS), f32),
            vmem((8, 8, BS), f32),
            vmem((8, BS), f32),
            vmem((8, BS), f32),
        ]
        + [sem((2, 8))] * 10
        + [sem((4, 4))] * 4
        + [sem((2, 2))]
        + [sem((2, 8))] * 2
        + [sem((8,))] * 6
        + [sem] * 2
        + [sem((2,))] * 3
        + [sem((7,))],
        compiler_params=pltpu.CompilerParams(
            collective_id=0, has_side_effects=True, vmem_limit_bytes=40 << 20
        ),
        name="exchange",
    )(mem, pat, *(pltpu.with_memory_space_constraint(x, pltpu.HBM) for x in operands))


def update_kernel(mem, pat, diag, x_row, x_col, y, g, hess, out, grad_out, rows, out_sem):
    r = lax.axis_index("prow")
    c = lax.axis_index("pcol")

    def save(a):
        return pltpu.make_async_copy(rows.at[a], out.at[a], out_sem.at[a])

    def is_pivot(i):
        pivot = i == member(mem, 0)
        for k in range(1, STEPS):
            pivot = jnp.logical_or(pivot, i == member(mem, k))
        return pivot

    def gradient(a, i):
        mine = pl.ds(pl.multiple_of(BS * a, BS), BS)
        part = jnp.zeros((BS, BS), f32)
        for k in range(STEPS):
            hi = x_row[mine, BS * k : BS * k + BS].astype(f32)
            rest = x_row[mine, WIDE + BS * k : WIDE + BS * k + BS].astype(f32)
            part = part + (hi + rest) * y[0:1, BS * k : BS * k + BS]
        val = g[a, pl.ds(r, 1), :] - jnp.sum(part.T, axis=0, keepdims=True)
        for k in range(STEPS):
            val = jnp.where(i == member(mem, k), y[0:1, BS * k : BS * k + BS], val)
        grad_out[pl.ds(a, 1), :] = val

    rr = lax.broadcasted_iota(jnp.int32, (BS, BS), 0)
    cc = lax.broadcasted_iota(jnp.int32, (BS, BS), 1)
    shift = jnp.where(rr == cc, SHIFT, 0.0)

    def two_rows(t):
        at = pl.ds(pl.multiple_of(2 * BS * t, 2 * BS), 2 * BS)
        upd = lax.dot_general(x_row[at, :], x_col[...], NT, preferred_element_type=f32)
        for e in range(2):
            a = 2 * t + e
            i = 8 * a + r
            gradient(a, i)
            live = jnp.where(is_pivot(i), 0.0, 1.0).astype(f32)
            for b in range(8):
                j = 8 * b + c
                keep = live * pat[i, j].astype(f32)
                on = jnp.where(i == j, 1.0, 0.0).astype(f32) * live
                sub = upd[BS * e : BS * e + BS, BS * b : BS * b + BS]
                there = pl.ds(b, BS, stride=8)
                rows[a, there, :] = keep * (hess[a, there, :] - sub) + on * shift
            for k in range(STEPS):
                pk = member(mem, k)

                @pl.when(lax.rem(pk, 8) == c)
                def _():
                    there = pl.ds(pk // 8, BS, stride=8)
                    mine = pl.ds(pl.multiple_of(BS * a, BS), BS)
                    part = slice(BS * k, BS * k + BS)
                    rest = slice(WIDE + BS * k, WIDE + BS * k + BS)

                    @pl.when(i != pk)
                    def _():
                        rows[a, there, :] = x_row[mine, part].astype(f32) + x_row[mine, rest].astype(f32)

                    @pl.when(i == pk)
                    def _():
                        rows[a, there, :] = diag[k]
            save(a).start()

    loop(0, 4, two_rows)
    for a in range(8):
        save(a).wait()


def update(mem, pat, diag, x_row, x_col, y, g, hess):
    return pl.pallas_call(
        update_kernel,
        out_shape=(
            jax.ShapeDtypeStruct(hess.shape, f32),
            jax.ShapeDtypeStruct((8, BS), f32),
        ),
        in_specs=[SM, SM, VM, VM, VM, VM, VM, VM],
        out_specs=(ANY, VM),
        scratch_shapes=[
            pltpu.VMEM((8, 1024, BS), f32),
            pltpu.SemaphoreType.DMA((8,)),
        ],
        compiler_params=pltpu.CompilerParams(vmem_limit_bytes=32 << 20),
        name="update",
    )(mem, pat, diag, x_row, x_col, y, g, hess)


def shards(
    poses, codebook, offsets, confidence, code_ids, creature_ids, hess_raw, pattern, membership
):
    hess = hess_raw.reshape(8, 1024, BS)
    x_row, x_col, diag, y, g = exchange(
        membership, pattern, hess, poses, codebook, offsets,
        confidence.reshape(16, BS), code_ids.reshape(16, BS), creature_ids.reshape(16, BS),
    )
    state, grad = update(membership, pattern, diag, x_row, x_col, y, g, hess)
    return state.reshape(hess_raw.shape), grad.reshape(8, 1, BS)


def solution(mesh):
    return jax.shard_map(
        shards,
        mesh=mesh,
        in_specs=(
            P(("frames", "prow", "pcol"), None),
            P(),
            P(),
            P(("frames", "prow", "pcol")),
            P(("frames", "prow", "pcol")),
            P(("frames", "prow", "pcol")),
            P(None, "prow", None, None, "pcol", None),
            P(),
            P(),
        ),
        out_specs=(P(None, "prow", None, None, "pcol", None), P(None, "prow", None)),
        check_vma=False,
    )
```

```python
import math

import jax
import jax.numpy as jnp
from jax import lax
from jax.experimental import pallas as pl
from jax.experimental.pallas import tpu as pltpu
from jax.sharding import PartitionSpec as P

NPAN = 8192
BS = 128
STEPS = 4
FRAMES = 262144
CODES = 32
SHIFT = 2.5 * math.sqrt(NPAN)
PAIRS = [(k, m) for k in range(STEPS) for m in range(k + 1)]
NQ = len(PAIRS)
CHUNKS = ((0, 3), (3, 7))
WIDE = STEPS * BS
MESH = pl.DeviceIdType.MESH
precise = lax.Precision.HIGHEST
f32 = jnp.float32
bf16 = jnp.bfloat16
NT = (((1,), (1,)), ((), ()))
NN = (((1,), (0,)), ((), ()))


def loop(lo, hi, fn):
    def body(d, carry):
        fn(d)
        return carry

    lax.fori_loop(lo, hi, body, 0)


def split(x):
    hi = x.astype(bf16)
    return hi, (x - hi.astype(f32)).astype(bf16)


def dot3(a, b):
    (ah, al), (bh, bl) = a, b
    d = lambda x, y: lax.dot_general(x, y, NT, preferred_element_type=f32)
    return d(ah, bh) + (d(ah, bl) + d(al, bh))


def member(mem, k):
    return mem[k // 2, k % 2]


VM = pl.BlockSpec(memory_space=pltpu.VMEM)
SM = pl.BlockSpec(memory_space=pltpu.SMEM)
ANY = pl.BlockSpec(memory_space=pl.ANY)
HBM = pl.BlockSpec(memory_space=pltpu.HBM)


def moments(poses, codebook, offsets, conf, codes, kinds):
    ids = lax.broadcasted_iota(jnp.int32, (CODES, BS), 0)
    weights, marks = [], []
    for s in range(16):
        weights.append(jnp.where(codes[s : s + 1, :] == ids, conf[s : s + 1, :], 0.0))
        marks.append(jnp.where(kinds[s : s + 1, :] == ids, 1.0, 0.0).astype(bf16))
    weight = jnp.concatenate(weights, axis=1)
    mark = jnp.concatenate(marks, axis=1)
    parts = []
    for _ in range(3):
        parts.append(weight.astype(bf16))
        weight = weight - parts[-1].astype(f32)
    stack = jnp.concatenate(parts, axis=0)

    def total(x):
        return x[0:CODES] + (x[CODES : 2 * CODES] + x[2 * CODES : 3 * CODES])

    moment = total(lax.dot_general(stack, poses[...], NN, preferred_element_type=f32))
    pair = total(lax.dot_general(stack, mark, NT, preferred_element_type=f32))
    count = jnp.sum(pair, axis=1, keepdims=True)
    moment = moment - count * codebook[...].astype(f32)
    moment = moment - lax.dot_general(
        pair, offsets[...].astype(f32), NN, precision=precise, preferred_element_type=f32
    )
    return moment / math.sqrt(FRAMES / CODES)


def spread(row):
    return jnp.broadcast_to(row, (8, BS))


def eliminate(upper_ref, inv_ref, first, last):
    groups = BS // 8
    row_ids = lax.broadcasted_iota(jnp.int32, (8, BS), 0)
    upper = {g: upper_ref[8 * g : 8 * g + 8, :] for g in range(first, groups)}
    inv = {g: inv_ref[8 * g : 8 * g + 8, :] for g in range(first, groups)}
    for g in range(first, last):
        k = 8 * g
        v, w = upper[g], inv[g]
        cols = [jnp.broadcast_to(v[:, k + j : k + j + 1], (8, BS)) for j in range(8)]
        rows_v, rows_w, coef = [], [], []
        for j in range(8):
            pivot = spread(cols[j][j : j + 1, :])
            recip = 1.0 / pivot
            rv = spread(v[j : j + 1, :]) * recip
            rw = spread(w[j : j + 1, :]) * recip
            rows_v.append(rv)
            rows_w.append(rw)
            below = jnp.where(row_ids > j, cols[j], 0.0)
            coef.append([None] * 8)
            for t in range(j + 1, 8):
                coef[j][t] = spread(cols[t][j : j + 1, :]) * recip
                cols[t] = cols[t] - below * coef[j][t]
            v = v - below * rv
            w = w - below * rw
        upper[g], inv[g] = v, w
        for h in range(g + 1, groups):
            v, w = upper[h], inv[h]
            cols = [jnp.broadcast_to(v[:, k + j : k + j + 1], (8, BS)) for j in range(8)]
            for j in range(8):
                for t in range(j + 1, 8):
                    cols[t] = cols[t] - cols[j] * coef[j][t]
                v = v - cols[j] * rows_v[j]
                w = w - cols[j] * rows_w[j]
            upper[h], inv[h] = v, w
    for g in range(first, groups):
        upper_ref[8 * g : 8 * g + 8, :] = upper[g]
        inv_ref[8 * g : 8 * g + 8, :] = inv[g]


def dot_nt(a, b):
    return lax.dot_general(a, b, NT, precision=precise, preferred_element_type=f32)


def dot_nn(a, b):
    return lax.dot_general(a, b, (((1,), (0,)), ((), ())), precision=precise, preferred_element_type=f32)


def exchange_kernel(
    mem_at, pat_at, hess_at, poses_at, codebook_at, offsets_at, conf_at, codes_at, kinds_at,
    x_row, x_col, diag, y_out, g_out,
    hess, poses, codebook, offsets, conf, codes, kinds, scand, ccand, pg, s_all, low, inv, fac_u, fac_i, raw, wh, wl,
    s1r_a, s1r_b, s1, s2r_a, s2r_b, par_a, par_b, picked, both_a, both_b, mine, g1r, g1, g2r, g2, g3r,
    snd_s1, rcv_s1, snd_s2, rcv_s2, snd_s3, rcv_s3, snd_sx, rcv_sx,
    snd_x, rcv_x, snd_a, rcv_a, snd_r2, snd_t2, snd_t1, rcv_r, rcv_t,
    snd_g1, rcv_g1, snd_g2, rcv_g2, snd_g4, rcv_g4, snd_g3, rcv_g3, snd_b, rcv_b, snd_r1, in_sem, mem, pat,
):
    fetches = [
        pltpu.make_async_copy(src, dst, in_sem.at[n])
        for n, (src, dst) in enumerate(
            [
                (hess_at, hess), (codes_at, codes), (conf_at, conf), (kinds_at, kinds),
                (poses_at, poses), (codebook_at, codebook), (offsets_at, offsets),
                (mem_at, mem), (pat_at, pat),
            ]
        )
    ]
    for fetch in fetches[7:] + fetches[:7]:
        fetch.start()
    s1r, s2r = (s1r_a, s1r_b), (s2r_a, s2r_b)
    par, both = (par_a, par_b), (both_a, both_b)
    f = lax.axis_index("frames")
    r = lax.axis_index("prow")
    c = lax.axis_index("pcol")
    p = r + f * (c - r)
    q = c + f * (r - c)

    def place(p_to, q_to):
        return (f, p_to + f * (q_to - p_to), q_to + f * (p_to - q_to))

    sibling = (1 - f, r, c)

    def q_at(line, pair):
        return 2 * line + pair + f * (3 * pair - line)

    def p_at(line, pair):
        return line + 4 * pair + f * (line - 3 * pair)

    def q_parts(v):
        return v // 2 + f * (lax.rem(v, 4) - v // 2), lax.rem(v, 2) + f * (v // 4 - lax.rem(v, 2))

    def p_parts(v):
        return lax.rem(v, 4) + f * (v // 2 - lax.rem(v, 4)), v // 4 + f * (lax.rem(v, 2) - v // 4)

    ql, qh = q_parts(q)
    pl_, ph = p_parts(p)

    hub = lax.rem(pl_ + ql, 4)

    def turn(v):
        return lax.rem(v - p_parts(q)[0] + 4, 4)

    def q_line(d):
        return lax.rem(ql + d, 4)

    def p_line(d):
        return lax.rem(pl_ + d, 4)

    def copy(src, dst, snd, rcv, to):
        return pltpu.make_async_remote_copy(
            src_ref=src, dst_ref=dst, send_sem=snd, recv_sem=rcv, device_id=to, device_id_type=MESH
        )

    def q_peer(d):
        return lax.rem(q + d, 8)

    def p_peer(d):
        return lax.rem(p + d, 8)

    def c_peer(d):
        return lax.rem(c + d, 8)

    def r_peer(d):
        return lax.rem(r + d, 8)

    barrier = pltpu.get_barrier_semaphore()

    def greet(to):
        pl.semaphore_signal(barrier, inc=1, device_id=to, device_id_type=MESH)

    greet(sibling)

    def greet_line(d):
        greet(place(p, q_peer(d)))
        greet(place(p_peer(d), q))

    loop(1, 8, greet_line)

    def at_home(p_to, q_to):
        return jnp.logical_and(p_to == p, q_to == q)

    def away(p_to, q_to, fn):
        @pl.when(jnp.logical_not(at_home(p_to, q_to)))
        def _():
            fn()

    def greet_turn(e):
        away(p_at(hub, e), p, lambda: greet(place(p_at(hub, e), p)))
        away(q, q_at(turn(pl_), e), lambda: greet(place(q, q_at(turn(pl_), e))))

    loop(0, 2, greet_turn)
    same = jnp.where(jnp.logical_and(p == q, ql == 0), 1, 0)

    fetches[7].wait()
    fetches[0].wait()
    slot = [member(mem, k) // 8 for k in range(STEPS)]
    for e, (k, m) in enumerate(PAIRS):
        scand[e] = hess[slot[k], pl.ds(slot[m], BS, stride=8), :]

    @pl.when(f == 0)
    def _():
        for k in range(2):
            for v in range(8):
                ccand[v, k] = hess[v, pl.ds(slot[k], BS, stride=8), :]

    @pl.when(f == 1)
    def _():
        for k in range(2):
            for v in range(8):
                ccand[v, k] = hess[slot[2 + k], pl.ds(v, BS, stride=8), :]

    pl.semaphore_wait(barrier, 19 - 2 * same)

    def rows_of(slice_id):
        return pl.ds(pl.multiple_of(8 * slice_id, 8), 8)

    def s1_copy(h, peer, at):
        lo, n = CHUNKS[h]
        return copy(
            scand.at[pl.ds(lo, n), rows_of(peer + 8 * f), :], s1r[h].at[at],
            snd_s1.at[h, peer], rcv_s1.at[h, at], place(p, peer),
        )

    def s2_copy(h, peer, at):
        lo, n = CHUNKS[h]
        return copy(
            s1.at[pl.ds(lo, n)], s2r[h].at[at],
            snd_s2.at[h, peer], rcv_s2.at[h, at], place(peer, q),
        )

    def s3_copy(h, peer, at):
        lo, n = CHUNKS[h]
        part = s_all.at[pl.ds(lo, n), rows_of(at + 8 * f), :]
        return copy(part, part, snd_s3.at[h, peer], rcv_s3.at[h, at], place(p, peer))

    def sx_copy(h, at, core):
        lo, n = CHUNKS[h]
        part = s_all.at[pl.ds(lo, n), rows_of(at + 8 * core), :]
        return copy(part, part, snd_sx.at[h, at], rcv_sx.at[h, at], sibling)

    def g1_copy(peer, at):
        return copy(pg.at[rows_of(peer)], g1r.at[at], snd_g1.at[peer], rcv_g1.at[at], (f, r, peer))

    def g2_copy(peer, at):
        return copy(g1, g2r.at[at], snd_g2.at[peer], rcv_g2.at[at], (f, peer, c))

    def g4_copy(peer, at):
        return copy(g_out.at[at], g_out.at[at], snd_g4.at[peer], rcv_g4.at[at], (f, r, peer))

    def a_copy(k, e, line, at):
        return copy(
            ccand.at[q_at(line, e), k], par[k].at[at, e],
            snd_a.at[2 * k + e, line], rcv_a.at[2 * k + e, at], place(p, q_at(line, qh)),
        )

    def b_copy(k):
        return copy(
            picked.at[k, 1 - qh], both[k].at[qh], snd_b.at[k], rcv_b.at[k], place(p, q_at(ql, 1 - qh))
        )

    def r1_copy(k, at):
        return copy(
            mine.at[k], raw.at[f, f, at, k], snd_r1.at[k], rcv_r.at[k, at], place(p, q_at(ql, 1 - qh))
        )

    def r2_copy(k, e, line, at):
        part = raw.at[f, f, at, k]
        return copy(part, part, snd_r2.at[2 * k + e, line], rcv_r.at[k, at], place(p, q_at(line, qh)))

    def t1_copy(k, e, at):
        return copy(
            mine.at[k], raw.at[1 - f, f, at, k], snd_t1.at[k, e], rcv_t.at[k, at], place(p_at(hub, e), p)
        )

    def t2_copy(k, e, line, at):
        part = raw.at[1 - f, f, at, k]
        return copy(part, part, snd_t2.at[2 * k + e, line], rcv_t.at[k, at], place(p_at(line, ph), q))

    def x_copy(which, at, core):
        part = raw.at[which, core, at]
        return copy(part, part, snd_x.at[which, at], rcv_x.at[which, at], sibling)

    def owner(k):
        return q_parts(lax.rem(mem[f, k], 8))

    def pick(k):
        for e in range(2):
            loop(1, 4, lambda d: a_copy(k, e, q_line(d), q_line(d)).wait())
        for e in range(2):
            picked[k, e] = par[k][owner(k)[0], e]
        b_copy(k).start()

    def spread_mine(k):
        both[k][qh] = picked[k, qh]
        b_copy(k).wait()

        @pl.when(f == 0)
        def _():
            mine[k] = both[k][lax.rem(mem[0, k], 2)]

        @pl.when(f == 1)
        def _():
            mine[k] = both[k][lax.rem(mem[1, k], 8) // 4].T

        r1_copy(k, q).start()
        for e in range(2):
            away(p_at(hub, e), p, lambda: t1_copy(k, e, q).start())
        raw[f, f, q, k] = mine[k]

        @pl.when(jnp.logical_and(p == q, ql == 0))
        def _():
            raw[1 - f, f, q, k] = mine[k]

    def spread_on(k):
        r1_copy(k, q_at(ql, 1 - qh)).wait_recv()
        for e in range(2):
            loop(1, 4, lambda d: r2_copy(k, e, q_line(d), q_at(ql, e)).start())
        for e in range(2):
            at = q_at(turn(pl_), e)
            away(q, at, lambda: t1_copy(k, e, at).wait_recv())
            loop(1, 4, lambda d: t2_copy(k, e, p_line(d), at).start())
        if k:
            for e in range(2):
                x_copy(f, q_at(ql, e), f).start()
                x_copy(1 - f, q_at(turn(pl_), e), f).start()

    for h in range(2):
        loop(1, 8, lambda d: s1_copy(h, q_peer(d), q).start())
    for k in range(2):
        for e in range(2):
            loop(1, 4, lambda d: a_copy(k, e, q_line(d), ql).start())
    for h, (lo, n) in enumerate(CHUNKS):
        s1r[h][q] = scand[lo : lo + n, rows_of(q + 8 * f), :]
    for e in range(2):
        for k in range(2):
            par[k][ql, e] = ccand[q_at(ql, e), k]
    for fetch in fetches[1:7] + fetches[8:]:
        fetch.wait()
    moment = moments(poses, codebook, offsets, conf, codes, kinds)
    for half in range(2):
        pg[pl.ds(half, CODES, stride=2), :] = moment[:, BS * half : BS * half + BS]
    loop(1, 8, lambda d: g1_copy(c_peer(d), c).start())
    g1r[c] = pg[rows_of(c), :]

    for h in range(2):
        lo, n = CHUNKS[h]
        loop(1, 8, lambda d: s1_copy(h, q_peer(d), q_peer(d)).wait())
        for e in range(lo, lo + n):
            own_k = lax.rem(member(mem, PAIRS[e][0]), 8)
            own_m = lax.rem(member(mem, PAIRS[e][1]), 8)
            s1[e] = s1r[h][own_m + f * (own_k - own_m), e - lo]
        loop(1, 8, lambda d: s2_copy(h, p_peer(d), p).start())
        s2r[h][p] = s1[lo : lo + n]

    loop(1, 8, lambda d: g1_copy(c_peer(d), c_peer(d)).wait())
    g1[...] = jnp.sum(g1r[...], axis=0)
    loop(1, 8, lambda d: g2_copy(r_peer(d), r).start())
    g2r[r] = g1[...]


    for h in range(2):
        lo, n = CHUNKS[h]
        loop(1, 8, lambda d: s2_copy(h, p_peer(d), p_peer(d)).wait())
        for e in range(lo, lo + n):
            own_k = lax.rem(member(mem, PAIRS[e][0]), 8)
            own_m = lax.rem(member(mem, PAIRS[e][1]), 8)
            s_all[e, rows_of(q + 8 * f), :] = s2r[h][own_k + f * (own_m - own_k), e - lo]
        loop(1, 8, lambda d: s3_copy(h, q_peer(d), q).start())
        sx_copy(h, q, f).start()


    loop(1, 8, lambda d: g2_copy(r_peer(d), r_peer(d)).wait())
    g2[...] = jnp.sum(g2r[...], axis=0)
    g3 = copy(g2, g3r, snd_g3, rcv_g3, sibling)
    g3.start()

    def pass_on(h):
        def one(d):
            s3_copy(h, q_peer(d), q_peer(d)).wait_recv()
            sx_copy(h, q_peer(d), f).start()

        loop(1, 8, one)

    def sx_ready(h):
        loop(0, 8, lambda at: sx_copy(h, at, 1 - f).wait_recv())

    rr = lax.broadcasted_iota(jnp.int32, (BS, BS), 0)
    cc = lax.broadcasted_iota(jnp.int32, (BS, BS), 1)
    low[...] = jnp.zeros_like(low)
    inv[...] = jnp.zeros_like(inv)

    def before(k):
        if k == 0:
            sx_ready(0)
        if k == 2:
            sx_ready(1)
        if k:
            row = jnp.concatenate(
                [
                    s_all[PAIRS.index((k, m))] * pat[member(mem, k), member(mem, m)].astype(f32)
                    for m in range(k)
                ],
                axis=1,
            )
            low[k, :, 0 : BS * k] = dot_nt(row, inv[0 : BS * k, 0 : BS * k])
        value = s_all[PAIRS.index((k, k))] * pat[member(mem, k), member(mem, k)].astype(f32)
        value = value + jnp.where(rr == cc, SHIFT, 0.0)
        if k:
            lows = low[k, :, 0 : BS * k]
            value = value - dot_nt(lows, lows)
        fac_u[...] = value
        fac_i[...] = jnp.where(rr == cc, 1.0, 0.0)

    def after(k):
        at = slice(BS * k, BS * k + BS)
        inv[at, at] = fac_i[...]
        if k:
            inv[at, 0 : BS * k] = -dot_nn(fac_i[...], dot_nn(low[k, :, 0 : BS * k], inv[0 : BS * k, 0 : BS * k]))
        lower = fac_u[...].T
        low[k, :, at] = lower
        diag[k] = lower
        if k == 0:
            pass_on(1)
        if k == 1:
            spread_on(1)
        if k == 2:
            g3.wait()
            g_out[c] = g2[...] + g3r[...]
            loop(1, 8, lambda d: g4_copy(c_peer(d), c).start())

    def step(k):
        for kk in range(STEPS):
            @pl.when(k == kk)
            def _():
                before(kk)

        eliminate(fac_u, fac_i, 0, 8)

        @pl.when(k == 0)
        def _():
            spread_mine(0)
            spread_mine(1)

        @pl.when(k == 1)
        def _():
            spread_on(0)

        eliminate(fac_u, fac_i, 8, 16)
        pivots = jnp.sum(jnp.where(rr == cc, fac_u[...], 0.0), axis=1, keepdims=True)
        scale = 1.0 / jnp.sqrt(pivots)
        fac_u[...] = jnp.where(cc >= rr, fac_u[...] * scale, 0.0)
        fac_i[...] = fac_i[...] * scale
        for kk in range(STEPS):
            @pl.when(k == kk)
            def _():
                after(kk)

    pick(0)
    pick(1)
    pass_on(0)
    loop(0, STEPS, step)

    def arrives(d):
        for e in range(2):
            at = q_at(q_line(d), e)
            for k in range(2):
                r2_copy(k, e, q_line(d), at).wait_recv()
            x_copy(f, at, f).start()
            at = q_at(turn(p_line(d)), e)
            for k in range(2):
                t2_copy(k, e, p_line(d), at).wait_recv()
            x_copy(1 - f, at, f).start()

    loop(1, 4, arrives)

    h, l = split(inv[...])
    wh[...] = h
    wl[...] = l
    half = 2 * BS
    w11 = (wh[0:half, 0:half], wl[0:half, 0:half])
    w21 = (wh[half:, 0:half], wl[half:, 0:half])
    w22 = (wh[half:, half:], wl[half:, half:])

    loop(1, 8, lambda d: g4_copy(c_peer(d), c_peer(d)).wait_recv())
    gp = jnp.concatenate(
        [g_out[member(mem, k) // 8, pl.ds(lax.rem(member(mem, k), 8), 1), :] for k in range(STEPS)], axis=1
    )
    gp = jnp.broadcast_to(gp, (16, WIDE))
    y_out[...] = dot3(split(gp), (wh[...], wl[...]))[0:8]

    def store(which, rows, at, x):
        hi, rest = split(x)
        for target, parts in ((x_row, (hi, rest, hi)), (x_col, (hi, hi, rest))):
            @pl.when(which == (1 if target is x_col else 0))
            def _():
                for n, part in enumerate(parts):
                    target[rows, WIDE * n + at : WIDE * n + at + half] = part

    def panel(which, t):
        base = r + which * (c - r)
        ones, twos, keeps = [], [], []
        for e in range(2):
            a = 2 * t + e
            x_copy(which, a, 1 - f).wait_recv()
        for e in range(2):
            a = 2 * t + e
            i = 8 * a + base
            pivot = i == member(mem, 0)
            for k in range(1, STEPS):
                pivot = jnp.logical_or(pivot, i == member(mem, k))
            z = jnp.where(pivot, 0.0, 1.0).astype(f32)
            m1 = z * pat[i, member(mem, 0)].astype(f32)
            m2 = z * pat[i, member(mem, 2)].astype(f32)
            ones.append(jnp.concatenate([raw[which, 0, a, 0], raw[which, 0, a, 1]], axis=1) * m1)
            twos.append(jnp.concatenate([raw[which, 1, a, 0], raw[which, 1, a, 1]], axis=1))
            keeps.append(m2)
        one = split(jnp.concatenate(ones, axis=0))
        two = split(jnp.concatenate(twos, axis=0))
        second = dot3(one, w21) + dot3(two, w22)
        rows = pl.ds(pl.multiple_of(half * t, half), half)
        store(which, rows, 0, dot3(one, w11))
        second = jnp.concatenate([second[0:BS] * keeps[0], second[BS:half] * keeps[1]], axis=0)
        store(which, rows, half, second)

    loop(0, 8, lambda t: panel(t // 4, lax.rem(t, 4)))

    def tail(d):
        for h in range(2):
            s3_copy(h, q_peer(d), q).wait_send()
        g4_copy(c_peer(d), c).wait_send()

    loop(1, 8, tail)
    for k in range(2):
        r1_copy(k, q).wait_send()
        for e in range(2):
            away(p_at(hub, e), p, lambda: t1_copy(k, e, q).wait_send())

    def tail_line(d):
        for k in range(2):
            for e in range(2):
                r2_copy(k, e, q_line(d), q_at(ql, e)).wait_send()
                t2_copy(k, e, p_line(d), q_at(turn(pl_), e)).wait_send()

    loop(1, 4, tail_line)

    def tail_pair(d):
        for h in range(2):
            sx_copy(h, d, f).wait_send()
        for which in range(2):
            x_copy(which, d, f).wait_send()

    loop(0, 8, tail_pair)


def exchange(mem, pat, *operands):
    vmem = pltpu.VMEM
    sem = pltpu.SemaphoreType.DMA
    return pl.pallas_call(
        exchange_kernel,
        out_shape=(
            jax.ShapeDtypeStruct((1024, 3 * WIDE), bf16),
            jax.ShapeDtypeStruct((1024, 3 * WIDE), bf16),
            jax.ShapeDtypeStruct((STEPS, BS, BS), f32),
            jax.ShapeDtypeStruct((8, WIDE), f32),
            jax.ShapeDtypeStruct((8, 8, BS), f32),
        ),
        in_specs=[HBM] * 9,
        out_specs=(VM,) * 5,
        scratch_shapes=[vmem(x.shape, x.dtype) for x in operands]
        + [
            vmem((NQ, BS, BS), f32),
            vmem((8, 2, BS, BS), f32),
            vmem((64, BS), f32),
            vmem((NQ, BS, BS), f32),
            vmem((STEPS, BS, WIDE), f32),
            vmem((WIDE, WIDE), f32),
            vmem((BS, BS), f32),
            vmem((BS, BS), f32),
            vmem((2, 2, 8, 2, BS, BS), f32),
            vmem((WIDE, WIDE), bf16),
            vmem((WIDE, WIDE), bf16),
            vmem((8, CHUNKS[0][1], 8, BS), f32),
            vmem((8, CHUNKS[1][1], 8, BS), f32),
            vmem((NQ, 8, BS), f32),
            vmem((8, CHUNKS[0][1], 8, BS), f32),
            vmem((8, CHUNKS[1][1], 8, BS), f32),
            vmem((4, 2, BS, BS), f32),
            vmem((4, 2, BS, BS), f32),
            vmem((2, 2, BS, BS), f32),
            vmem((2, BS, BS), f32),
            vmem((2, BS, BS), f32),
            vmem((2, BS, BS), f32),
            vmem((8, 8, BS), f32),
            vmem((8, BS), f32),
            vmem((8, 8, BS), f32),
            vmem((8, BS), f32),
            vmem((8, BS), f32),
        ]
        + [sem((2, 8))] * 10
        + [sem((4, 4))] * 4
        + [sem((2, 2))]
        + [sem((2, 8))] * 2
        + [sem((8,))] * 6
        + [sem] * 2
        + [sem((2,))] * 3
        + [sem((9,)), pltpu.SMEM(mem.shape, jnp.int32), pltpu.SMEM(pat.shape, jnp.int32)],
        compiler_params=pltpu.CompilerParams(
            collective_id=0, has_side_effects=True, vmem_limit_bytes=40 << 20
        ),
        name="exchange",
    )(*(pltpu.with_memory_space_constraint(x, pltpu.HBM) for x in (mem, pat, *operands)))


def update_kernel(mem, pat, diag, x_row, x_col, y, g, hess, out, grad_out, rows, out_sem):
    r = lax.axis_index("prow")
    c = lax.axis_index("pcol")

    def save(a):
        return pltpu.make_async_copy(rows.at[a], out.at[a], out_sem.at[a])

    def is_pivot(i):
        pivot = i == member(mem, 0)
        for k in range(1, STEPS):
            pivot = jnp.logical_or(pivot, i == member(mem, k))
        return pivot

    def gradient(a, i):
        mine = pl.ds(pl.multiple_of(BS * a, BS), BS)
        part = jnp.zeros((BS, BS), f32)
        for k in range(STEPS):
            hi = x_row[mine, BS * k : BS * k + BS].astype(f32)
            rest = x_row[mine, WIDE + BS * k : WIDE + BS * k + BS].astype(f32)
            part = part + (hi + rest) * y[0:1, BS * k : BS * k + BS]
        val = g[a, pl.ds(r, 1), :] - jnp.sum(part.T, axis=0, keepdims=True)
        for k in range(STEPS):
            val = jnp.where(i == member(mem, k), y[0:1, BS * k : BS * k + BS], val)
        grad_out[pl.ds(a, 1), :] = val

    rr = lax.broadcasted_iota(jnp.int32, (BS, BS), 0)
    cc = lax.broadcasted_iota(jnp.int32, (BS, BS), 1)
    shift = jnp.where(rr == cc, SHIFT, 0.0)

    def two_rows(t):
        at = pl.ds(pl.multiple_of(2 * BS * t, 2 * BS), 2 * BS)
        upd = lax.dot_general(x_row[at, :], x_col[...], NT, preferred_element_type=f32)
        for e in range(2):
            a = 2 * t + e
            i = 8 * a + r
            gradient(a, i)
            live = jnp.where(is_pivot(i), 0.0, 1.0).astype(f32)
            for b in range(8):
                j = 8 * b + c
                keep = live * pat[i, j].astype(f32)
                on = jnp.where(i == j, 1.0, 0.0).astype(f32) * live
                sub = upd[BS * e : BS * e + BS, BS * b : BS * b + BS]
                there = pl.ds(b, BS, stride=8)
                rows[a, there, :] = keep * (hess[a, there, :] - sub) + on * shift
            for k in range(STEPS):
                pk = member(mem, k)

                @pl.when(lax.rem(pk, 8) == c)
                def _():
                    there = pl.ds(pk // 8, BS, stride=8)
                    mine = pl.ds(pl.multiple_of(BS * a, BS), BS)
                    part = slice(BS * k, BS * k + BS)
                    rest = slice(WIDE + BS * k, WIDE + BS * k + BS)

                    @pl.when(i != pk)
                    def _():
                        rows[a, there, :] = x_row[mine, part].astype(f32) + x_row[mine, rest].astype(f32)

                    @pl.when(i == pk)
                    def _():
                        rows[a, there, :] = diag[k]
            save(a).start()

    loop(0, 4, two_rows)
    for a in range(8):
        save(a).wait()


def update(mem, pat, diag, x_row, x_col, y, g, hess):
    return pl.pallas_call(
        update_kernel,
        out_shape=(
            jax.ShapeDtypeStruct(hess.shape, f32),
            jax.ShapeDtypeStruct((8, BS), f32),
        ),
        in_specs=[SM, SM, VM, VM, VM, VM, VM, VM],
        out_specs=(ANY, VM),
        scratch_shapes=[
            pltpu.VMEM((8, 1024, BS), f32),
            pltpu.SemaphoreType.DMA((8,)),
        ],
        compiler_params=pltpu.CompilerParams(vmem_limit_bytes=32 << 20),
        name="update",
    )(mem, pat, diag, x_row, x_col, y, g, hess)


def shards(
    poses, codebook, offsets, confidence, code_ids, creature_ids, hess_raw, pattern, membership
):
    hess = hess_raw.reshape(8, 1024, BS)
    x_row, x_col, diag, y, g = exchange(
        membership, pattern, hess, poses, codebook, offsets,
        confidence.reshape(16, BS), code_ids.reshape(16, BS), creature_ids.reshape(16, BS),
    )
    state, grad = update(membership, pattern, diag, x_row, x_col, y, g, hess)
    return state.reshape(hess_raw.shape), grad.reshape(8, 1, BS)


def solution(mesh):
    return jax.shard_map(
        shards,
        mesh=mesh,
        in_specs=(
            P(("frames", "prow", "pcol"), None),
            P(),
            P(),
            P(("frames", "prow", "pcol")),
            P(("frames", "prow", "pcol")),
            P(("frames", "prow", "pcol")),
            P(None, "prow", None, None, "pcol", None),
            P(),
            P(),
        ),
        out_specs=(P(None, "prow", None, None, "pcol", None), P(None, "prow", None)),
        check_vma=False,
    )
```

```python
import math

import jax
import jax.numpy as jnp
from jax import lax
from jax.experimental import pallas as pl
from jax.experimental.pallas import tpu as pltpu
from jax.sharding import PartitionSpec as P

NPAN = 8192
BS = 128
STEPS = 4
FRAMES = 262144
CODES = 32
SHIFT = 2.5 * math.sqrt(NPAN)
PAIRS = [(k, m) for k in range(STEPS) for m in range(k + 1)]
NQ = len(PAIRS)
CHUNKS = ((0, 3), (3, 7))
WIDE = STEPS * BS
MESH = pl.DeviceIdType.MESH
precise = lax.Precision.HIGHEST
f32 = jnp.float32
bf16 = jnp.bfloat16
NT = (((1,), (1,)), ((), ()))
NN = (((1,), (0,)), ((), ()))


def loop(lo, hi, fn):
    def body(d, carry):
        fn(d)
        return carry

    lax.fori_loop(lo, hi, body, 0)


def split(x):
    hi = x.astype(bf16)
    return hi, (x - hi.astype(f32)).astype(bf16)


def dot3(a, b):
    (ah, al), (bh, bl) = a, b
    d = lambda x, y: lax.dot_general(x, y, NT, preferred_element_type=f32)
    return d(ah, bh) + (d(ah, bl) + d(al, bh))


def member(mem, k):
    return mem[k // 2, k % 2]


VM = pl.BlockSpec(memory_space=pltpu.VMEM)
SM = pl.BlockSpec(memory_space=pltpu.SMEM)
ANY = pl.BlockSpec(memory_space=pl.ANY)
HBM = pl.BlockSpec(memory_space=pltpu.HBM)


def moments(poses, codebook, offsets, conf, codes, kinds):
    ids = lax.broadcasted_iota(jnp.int32, (CODES, BS), 0)
    weights, marks = [], []
    for s in range(16):
        weights.append(jnp.where(codes[s : s + 1, :] == ids, conf[s : s + 1, :], 0.0))
        marks.append(jnp.where(kinds[s : s + 1, :] == ids, 1.0, 0.0).astype(bf16))
    weight = jnp.concatenate(weights, axis=1)
    mark = jnp.concatenate(marks, axis=1)
    parts = []
    for _ in range(3):
        parts.append(weight.astype(bf16))
        weight = weight - parts[-1].astype(f32)
    stack = jnp.concatenate(parts, axis=0)

    def total(x):
        return x[0:CODES] + (x[CODES : 2 * CODES] + x[2 * CODES : 3 * CODES])

    moment = total(lax.dot_general(stack, poses[...], NN, preferred_element_type=f32))
    pair = total(lax.dot_general(stack, mark, NT, preferred_element_type=f32))
    count = jnp.sum(pair, axis=1, keepdims=True)
    moment = moment - count * codebook[...].astype(f32)
    moment = moment - lax.dot_general(
        pair, offsets[...].astype(f32), NN, precision=precise, preferred_element_type=f32
    )
    return moment / math.sqrt(FRAMES / CODES)


def spread(row):
    return jnp.broadcast_to(row, (8, BS))


def eliminate(upper_ref, inv_ref, first, last):
    groups = BS // 8
    row_ids = lax.broadcasted_iota(jnp.int32, (8, BS), 0)
    upper = {g: upper_ref[8 * g : 8 * g + 8, :] for g in range(first, groups)}
    inv = {g: inv_ref[8 * g : 8 * g + 8, :] for g in range(first, groups)}
    for g in range(first, last):
        k = 8 * g
        v, w = upper[g], inv[g]
        cols = [jnp.broadcast_to(v[:, k + j : k + j + 1], (8, BS)) for j in range(8)]
        rows_v, rows_w, coef = [], [], []
        for j in range(8):
            pivot = spread(cols[j][j : j + 1, :])
            recip = 1.0 / pivot
            rv = spread(v[j : j + 1, :]) * recip
            rw = spread(w[j : j + 1, :]) * recip
            rows_v.append(rv)
            rows_w.append(rw)
            below = jnp.where(row_ids > j, cols[j], 0.0)
            coef.append([None] * 8)
            for t in range(j + 1, 8):
                coef[j][t] = spread(cols[t][j : j + 1, :]) * recip
                cols[t] = cols[t] - below * coef[j][t]
            v = v - below * rv
            w = w - below * rw
        upper[g], inv[g] = v, w
        for h in range(g + 1, groups):
            v, w = upper[h], inv[h]
            cols = [jnp.broadcast_to(v[:, k + j : k + j + 1], (8, BS)) for j in range(8)]
            for j in range(8):
                for t in range(j + 1, 8):
                    cols[t] = cols[t] - cols[j] * coef[j][t]
                v = v - cols[j] * rows_v[j]
                w = w - cols[j] * rows_w[j]
            upper[h], inv[h] = v, w
    for g in range(first, groups):
        upper_ref[8 * g : 8 * g + 8, :] = upper[g]
        inv_ref[8 * g : 8 * g + 8, :] = inv[g]


def dot_nt(a, b):
    return lax.dot_general(a, b, NT, precision=precise, preferred_element_type=f32)


def dot_nn(a, b):
    return lax.dot_general(a, b, (((1,), (0,)), ((), ())), precision=precise, preferred_element_type=f32)


def exchange_kernel(
    mem_at, pat_at, hess_at, poses_at, codebook_at, offsets_at, conf_at, codes_at, kinds_at,
    x_row, x_col, diag, y_out, g_out,
    hess, poses, codebook, offsets, conf, codes, kinds, scand, ccand, pg, s_all, low, inv, fac_u, fac_i, raw, wh, wl,
    s1r_a, s1r_b, s1, s2r_a, s2r_b, par_a, par_b, picked, both_a, both_b, mine, g1r, g1, g2r, g2, g3r,
    snd_s1, rcv_s1, snd_s2, rcv_s2, snd_s3, rcv_s3, snd_sx, rcv_sx,
    snd_x, rcv_x, snd_a, rcv_a, snd_r2, snd_t2, snd_t1, rcv_r, rcv_t,
    snd_g1, rcv_g1, snd_g2, rcv_g2, snd_g4, rcv_g4, snd_g3, rcv_g3, snd_b, rcv_b, snd_r1, in_sem, mem, pat,
):
    fetches = [
        pltpu.make_async_copy(src, dst, in_sem.at[n])
        for n, (src, dst) in enumerate(
            [
                (hess_at, hess), (codes_at, codes), (conf_at, conf), (kinds_at, kinds),
                (poses_at, poses), (codebook_at, codebook), (offsets_at, offsets),
                (mem_at, mem), (pat_at, pat),
            ]
        )
    ]
    for fetch in fetches[7:] + fetches[:7]:
        fetch.start()
    s1r, s2r = (s1r_a, s1r_b), (s2r_a, s2r_b)
    par, both = (par_a, par_b), (both_a, both_b)
    f = lax.axis_index("frames")
    r = lax.axis_index("prow")
    c = lax.axis_index("pcol")
    p = r + f * (c - r)
    q = c + f * (r - c)

    def place(p_to, q_to):
        return (f, p_to + f * (q_to - p_to), q_to + f * (p_to - q_to))

    sibling = (1 - f, r, c)

    def q_at(line, pair):
        return 2 * line + pair + f * (3 * pair - line)

    def p_at(line, pair):
        return line + 4 * pair + f * (line - 3 * pair)

    def q_parts(v):
        return v // 2 + f * (lax.rem(v, 4) - v // 2), lax.rem(v, 2) + f * (v // 4 - lax.rem(v, 2))

    def p_parts(v):
        return lax.rem(v, 4) + f * (v // 2 - lax.rem(v, 4)), v // 4 + f * (lax.rem(v, 2) - v // 4)

    ql, qh = q_parts(q)
    pl_, ph = p_parts(p)

    hub = lax.rem(pl_ + ql, 4)

    def turn(v):
        return lax.rem(v - p_parts(q)[0] + 4, 4)

    def q_line(d):
        return lax.rem(ql + d, 4)

    def p_line(d):
        return lax.rem(pl_ + d, 4)

    def copy(src, dst, snd, rcv, to):
        return pltpu.make_async_remote_copy(
            src_ref=src, dst_ref=dst, send_sem=snd, recv_sem=rcv, device_id=to, device_id_type=MESH
        )

    def q_peer(d):
        return lax.rem(q + d, 8)

    def p_peer(d):
        return lax.rem(p + d, 8)

    def c_peer(d):
        return lax.rem(c + d, 8)

    def r_peer(d):
        return lax.rem(r + d, 8)

    barrier = pltpu.get_barrier_semaphore()

    def greet(to):
        pl.semaphore_signal(barrier, inc=1, device_id=to, device_id_type=MESH)

    greet(sibling)

    def greet_line(d):
        greet(place(p, q_peer(d)))
        greet(place(p_peer(d), q))

    loop(1, 8, greet_line)

    def at_home(p_to, q_to):
        return jnp.logical_and(p_to == p, q_to == q)

    def away(p_to, q_to, fn):
        @pl.when(jnp.logical_not(at_home(p_to, q_to)))
        def _():
            fn()

    def greet_turn(e):
        away(p_at(hub, e), p, lambda: greet(place(p_at(hub, e), p)))
        away(q, q_at(turn(pl_), e), lambda: greet(place(q, q_at(turn(pl_), e))))

    loop(0, 2, greet_turn)
    same = jnp.where(jnp.logical_and(p == q, ql == 0), 1, 0)

    fetches[7].wait()
    fetches[0].wait()
    slot = [member(mem, k) // 8 for k in range(STEPS)]
    for e, (k, m) in enumerate(PAIRS):
        scand[e] = hess[slot[k], pl.ds(slot[m], BS, stride=8), :]

    @pl.when(f == 0)
    def _():
        for k in range(2):
            for v in range(8):
                ccand[v, k] = hess[v, pl.ds(slot[k], BS, stride=8), :]

    @pl.when(f == 1)
    def _():
        for k in range(2):
            for v in range(8):
                ccand[v, k] = hess[slot[2 + k], pl.ds(v, BS, stride=8), :]

    pl.semaphore_wait(barrier, 19 - 2 * same)

    def rows_of(slice_id):
        return pl.ds(pl.multiple_of(8 * slice_id, 8), 8)

    def s1_copy(h, peer, at):
        lo, n = CHUNKS[h]
        return copy(
            scand.at[pl.ds(lo, n), rows_of(peer + 8 * f), :], s1r[h].at[at],
            snd_s1.at[h, peer], rcv_s1.at[h, at], place(p, peer),
        )

    def s2_copy(h, peer, at):
        lo, n = CHUNKS[h]
        return copy(
            s1.at[pl.ds(lo, n)], s2r[h].at[at],
            snd_s2.at[h, peer], rcv_s2.at[h, at], place(peer, q),
        )

    def s3_copy(h, peer, at):
        lo, n = CHUNKS[h]
        part = s_all.at[pl.ds(lo, n), rows_of(at + 8 * f), :]
        return copy(part, part, snd_s3.at[h, peer], rcv_s3.at[h, at], place(p, peer))

    def sx_copy(h, at, core):
        lo, n = CHUNKS[h]
        part = s_all.at[pl.ds(lo, n), rows_of(at + 8 * core), :]
        return copy(part, part, snd_sx.at[h, at], rcv_sx.at[h, at], sibling)

    def g1_copy(peer, at):
        return copy(pg.at[rows_of(peer)], g1r.at[at], snd_g1.at[peer], rcv_g1.at[at], (f, r, peer))

    def g2_copy(peer, at):
        return copy(g1, g2r.at[at], snd_g2.at[peer], rcv_g2.at[at], (f, peer, c))

    def g4_copy(peer, at):
        return copy(g_out.at[at], g_out.at[at], snd_g4.at[peer], rcv_g4.at[at], (f, r, peer))

    def a_copy(k, e, line, at):
        return copy(
            ccand.at[q_at(line, e), k], par[k].at[at, e],
            snd_a.at[2 * k + e, line], rcv_a.at[2 * k + e, at], place(p, q_at(line, qh)),
        )

    def b_copy(k):
        return copy(
            picked.at[k, 1 - qh], both[k].at[qh], snd_b.at[k], rcv_b.at[k], place(p, q_at(ql, 1 - qh))
        )

    def r1_copy(k, at):
        return copy(
            mine.at[k], raw.at[f, f, at, k], snd_r1.at[k], rcv_r.at[k, at], place(p, q_at(ql, 1 - qh))
        )

    def r2_copy(k, e, line, at):
        part = raw.at[f, f, at, k]
        return copy(part, part, snd_r2.at[2 * k + e, line], rcv_r.at[k, at], place(p, q_at(line, qh)))

    def t1_copy(k, e, at):
        return copy(
            mine.at[k], raw.at[1 - f, f, at, k], snd_t1.at[k, e], rcv_t.at[k, at], place(p_at(hub, e), p)
        )

    def t2_copy(k, e, line, at):
        part = raw.at[1 - f, f, at, k]
        return copy(part, part, snd_t2.at[2 * k + e, line], rcv_t.at[k, at], place(p_at(line, ph), q))

    def x_copy(which, at, core):
        part = raw.at[which, core, at]
        return copy(part, part, snd_x.at[which, at], rcv_x.at[which, at], sibling)

    def owner(k):
        return q_parts(lax.rem(mem[f, k], 8))

    def pick(k):
        for e in range(2):
            loop(1, 4, lambda d: a_copy(k, e, q_line(d), q_line(d)).wait())
        for e in range(2):
            picked[k, e] = par[k][owner(k)[0], e]
        b_copy(k).start()

    def spread_mine(k):
        both[k][qh] = picked[k, qh]
        b_copy(k).wait()

        @pl.when(f == 0)
        def _():
            mine[k] = both[k][lax.rem(mem[0, k], 2)]

        @pl.when(f == 1)
        def _():
            mine[k] = both[k][lax.rem(mem[1, k], 8) // 4].T

        for e in range(2):
            away(p_at(hub, e), p, lambda: t1_copy(k, e, q).start())
        r1_copy(k, q).start()
        raw[f, f, q, k] = mine[k]

        @pl.when(jnp.logical_and(p == q, ql == 0))
        def _():
            raw[1 - f, f, q, k] = mine[k]

    def spread_on(k):
        r1_copy(k, q_at(ql, 1 - qh)).wait_recv()
        for e in range(2):
            loop(1, 4, lambda d: r2_copy(k, e, q_line(d), q_at(ql, e)).start())
        for e in range(2):
            at = q_at(turn(pl_), e)
            away(q, at, lambda: t1_copy(k, e, at).wait_recv())
            loop(1, 4, lambda d: t2_copy(k, e, p_line(d), at).start())
        if k:
            for e in range(2):
                x_copy(f, q_at(ql, e), f).start()
                x_copy(1 - f, q_at(turn(pl_), e), f).start()

    for h in range(2):
        loop(1, 8, lambda d: s1_copy(h, q_peer(d), q).start())
    for k in range(2):
        for e in range(2):
            loop(1, 4, lambda d: a_copy(k, e, q_line(d), ql).start())
    for h, (lo, n) in enumerate(CHUNKS):
        s1r[h][q] = scand[lo : lo + n, rows_of(q + 8 * f), :]
    for e in range(2):
        for k in range(2):
            par[k][ql, e] = ccand[q_at(ql, e), k]
    for fetch in fetches[1:7] + fetches[8:]:
        fetch.wait()
    moment = moments(poses, codebook, offsets, conf, codes, kinds)
    for half in range(2):
        pg[pl.ds(half, CODES, stride=2), :] = moment[:, BS * half : BS * half + BS]
    loop(1, 8, lambda d: g1_copy(c_peer(d), c).start())
    g1r[c] = pg[rows_of(c), :]

    for h in range(2):
        lo, n = CHUNKS[h]
        loop(1, 8, lambda d: s1_copy(h, q_peer(d), q_peer(d)).wait())
        for e in range(lo, lo + n):
            own_k = lax.rem(member(mem, PAIRS[e][0]), 8)
            own_m = lax.rem(member(mem, PAIRS[e][1]), 8)
            s1[e] = s1r[h][own_m + f * (own_k - own_m), e - lo]
        loop(1, 8, lambda d: s2_copy(h, p_peer(d), p).start())
        s2r[h][p] = s1[lo : lo + n]

    loop(1, 8, lambda d: g1_copy(c_peer(d), c_peer(d)).wait())
    g1[...] = jnp.sum(g1r[...], axis=0)
    loop(1, 8, lambda d: g2_copy(r_peer(d), r).start())
    g2r[r] = g1[...]


    for h in range(2):
        lo, n = CHUNKS[h]
        loop(1, 8, lambda d: s2_copy(h, p_peer(d), p_peer(d)).wait())
        for e in range(lo, lo + n):
            own_k = lax.rem(member(mem, PAIRS[e][0]), 8)
            own_m = lax.rem(member(mem, PAIRS[e][1]), 8)
            s_all[e, rows_of(q + 8 * f), :] = s2r[h][own_k + f * (own_m - own_k), e - lo]
        loop(1, 8, lambda d: s3_copy(h, q_peer(d), q).start())
        sx_copy(h, q, f).start()


    loop(1, 8, lambda d: g2_copy(r_peer(d), r_peer(d)).wait())
    g2[...] = jnp.sum(g2r[...], axis=0)
    g3 = copy(g2, g3r, snd_g3, rcv_g3, sibling)
    g3.start()

    def pass_on(h):
        def one(d):
            s3_copy(h, q_peer(d), q_peer(d)).wait_recv()
            sx_copy(h, q_peer(d), f).start()

        loop(1, 8, one)

    def sx_ready(h):
        loop(0, 8, lambda at: sx_copy(h, at, 1 - f).wait_recv())

    rr = lax.broadcasted_iota(jnp.int32, (BS, BS), 0)
    cc = lax.broadcasted_iota(jnp.int32, (BS, BS), 1)
    low[...] = jnp.zeros_like(low)
    inv[...] = jnp.zeros_like(inv)

    def before(k):
        if k == 0:
            sx_ready(0)
        if k == 2:
            sx_ready(1)
        if k:
            row = jnp.concatenate(
                [
                    s_all[PAIRS.index((k, m))] * pat[member(mem, k), member(mem, m)].astype(f32)
                    for m in range(k)
                ],
                axis=1,
            )
            low[k, :, 0 : BS * k] = dot_nt(row, inv[0 : BS * k, 0 : BS * k])
        value = s_all[PAIRS.index((k, k))] * pat[member(mem, k), member(mem, k)].astype(f32)
        value = value + jnp.where(rr == cc, SHIFT, 0.0)
        if k:
            lows = low[k, :, 0 : BS * k]
            value = value - dot_nt(lows, lows)
        fac_u[...] = value
        fac_i[...] = jnp.where(rr == cc, 1.0, 0.0)

    def after(k):
        at = slice(BS * k, BS * k + BS)
        inv[at, at] = fac_i[...]
        if k:
            inv[at, 0 : BS * k] = -dot_nn(fac_i[...], dot_nn(low[k, :, 0 : BS * k], inv[0 : BS * k, 0 : BS * k]))
        lower = fac_u[...].T
        low[k, :, at] = lower
        diag[k] = lower
        if k == 0:
            pass_on(1)
        if k == 1:
            spread_on(1)
        if k == 2:
            g3.wait()
            g_out[c] = g2[...] + g3r[...]
            loop(1, 8, lambda d: g4_copy(c_peer(d), c).start())

    def step(k):
        for kk in range(STEPS):
            @pl.when(k == kk)
            def _():
                before(kk)

        eliminate(fac_u, fac_i, 0, 8)

        @pl.when(k == 0)
        def _():
            spread_mine(0)
            spread_mine(1)

        @pl.when(k == 1)
        def _():
            spread_on(0)

        eliminate(fac_u, fac_i, 8, 16)
        pivots = jnp.sum(jnp.where(rr == cc, fac_u[...], 0.0), axis=1, keepdims=True)
        scale = 1.0 / jnp.sqrt(pivots)
        fac_u[...] = jnp.where(cc >= rr, fac_u[...] * scale, 0.0)
        fac_i[...] = fac_i[...] * scale
        for kk in range(STEPS):
            @pl.when(k == kk)
            def _():
                after(kk)

    pick(0)
    pick(1)
    pass_on(0)
    loop(0, STEPS, step)

    def arrives(d):
        for e in range(2):
            at = q_at(q_line(d), e)
            for k in range(2):
                r2_copy(k, e, q_line(d), at).wait_recv()
            x_copy(f, at, f).start()
            at = q_at(turn(p_line(d)), e)
            for k in range(2):
                t2_copy(k, e, p_line(d), at).wait_recv()
            x_copy(1 - f, at, f).start()

    loop(1, 4, arrives)

    h, l = split(inv[...])
    wh[...] = h
    wl[...] = l
    half = 2 * BS
    w11 = (wh[0:half, 0:half], wl[0:half, 0:half])
    w21 = (wh[half:, 0:half], wl[half:, 0:half])
    w22 = (wh[half:, half:], wl[half:, half:])

    loop(1, 8, lambda d: g4_copy(c_peer(d), c_peer(d)).wait_recv())
    gp = jnp.concatenate(
        [g_out[member(mem, k) // 8, pl.ds(lax.rem(member(mem, k), 8), 1), :] for k in range(STEPS)], axis=1
    )
    gp = jnp.broadcast_to(gp, (16, WIDE))
    y_out[...] = dot3(split(gp), (wh[...], wl[...]))[0:8]

    def store(which, rows, at, x):
        hi, rest = split(x)
        for target, parts in ((x_row, (hi, rest, hi)), (x_col, (hi, hi, rest))):
            @pl.when(which == (1 if target is x_col else 0))
            def _():
                for n, part in enumerate(parts):
                    target[rows, WIDE * n + at : WIDE * n + at + half] = part

    def panel(which, t):
        base = r + which * (c - r)
        ones, twos, keeps = [], [], []
        for e in range(2):
            a = 2 * t + e
            x_copy(which, a, 1 - f).wait_recv()
        for e in range(2):
            a = 2 * t + e
            i = 8 * a + base
            pivot = i == member(mem, 0)
            for k in range(1, STEPS):
                pivot = jnp.logical_or(pivot, i == member(mem, k))
            z = jnp.where(pivot, 0.0, 1.0).astype(f32)
            m1 = z * pat[i, member(mem, 0)].astype(f32)
            m2 = z * pat[i, member(mem, 2)].astype(f32)
            ones.append(jnp.concatenate([raw[which, 0, a, 0], raw[which, 0, a, 1]], axis=1) * m1)
            twos.append(jnp.concatenate([raw[which, 1, a, 0], raw[which, 1, a, 1]], axis=1))
            keeps.append(m2)
        one = split(jnp.concatenate(ones, axis=0))
        two = split(jnp.concatenate(twos, axis=0))
        second = dot3(one, w21) + dot3(two, w22)
        rows = pl.ds(pl.multiple_of(half * t, half), half)
        store(which, rows, 0, dot3(one, w11))
        second = jnp.concatenate([second[0:BS] * keeps[0], second[BS:half] * keeps[1]], axis=0)
        store(which, rows, half, second)

    loop(0, 8, lambda t: panel(t // 4, lax.rem(t, 4)))

    def tail(d):
        for h in range(2):
            s3_copy(h, q_peer(d), q).wait_send()
        g4_copy(c_peer(d), c).wait_send()

    loop(1, 8, tail)
    for k in range(2):
        r1_copy(k, q).wait_send()
        for e in range(2):
            away(p_at(hub, e), p, lambda: t1_copy(k, e, q).wait_send())

    def tail_line(d):
        for k in range(2):
            for e in range(2):
                r2_copy(k, e, q_line(d), q_at(ql, e)).wait_send()
                t2_copy(k, e, p_line(d), q_at(turn(pl_), e)).wait_send()

    loop(1, 4, tail_line)

    def tail_pair(d):
        for h in range(2):
            sx_copy(h, d, f).wait_send()
        for which in range(2):
            x_copy(which, d, f).wait_send()

    loop(0, 8, tail_pair)


def exchange(mem, pat, *operands):
    vmem = pltpu.VMEM
    sem = pltpu.SemaphoreType.DMA
    return pl.pallas_call(
        exchange_kernel,
        out_shape=(
            jax.ShapeDtypeStruct((1024, 3 * WIDE), bf16),
            jax.ShapeDtypeStruct((1024, 3 * WIDE), bf16),
            jax.ShapeDtypeStruct((STEPS, BS, BS), f32),
            jax.ShapeDtypeStruct((8, WIDE), f32),
            jax.ShapeDtypeStruct((8, 8, BS), f32),
        ),
        in_specs=[HBM] * 9,
        out_specs=(VM,) * 5,
        scratch_shapes=[vmem(x.shape, x.dtype) for x in operands]
        + [
            vmem((NQ, BS, BS), f32),
            vmem((8, 2, BS, BS), f32),
            vmem((64, BS), f32),
            vmem((NQ, BS, BS), f32),
            vmem((STEPS, BS, WIDE), f32),
            vmem((WIDE, WIDE), f32),
            vmem((BS, BS), f32),
            vmem((BS, BS), f32),
            vmem((2, 2, 8, 2, BS, BS), f32),
            vmem((WIDE, WIDE), bf16),
            vmem((WIDE, WIDE), bf16),
            vmem((8, CHUNKS[0][1], 8, BS), f32),
            vmem((8, CHUNKS[1][1], 8, BS), f32),
            vmem((NQ, 8, BS), f32),
            vmem((8, CHUNKS[0][1], 8, BS), f32),
            vmem((8, CHUNKS[1][1], 8, BS), f32),
            vmem((4, 2, BS, BS), f32),
            vmem((4, 2, BS, BS), f32),
            vmem((2, 2, BS, BS), f32),
            vmem((2, BS, BS), f32),
            vmem((2, BS, BS), f32),
            vmem((2, BS, BS), f32),
            vmem((8, 8, BS), f32),
            vmem((8, BS), f32),
            vmem((8, 8, BS), f32),
            vmem((8, BS), f32),
            vmem((8, BS), f32),
        ]
        + [sem((2, 8))] * 10
        + [sem((4, 4))] * 4
        + [sem((2, 2))]
        + [sem((2, 8))] * 2
        + [sem((8,))] * 6
        + [sem] * 2
        + [sem((2,))] * 3
        + [sem((9,)), pltpu.SMEM(mem.shape, jnp.int32), pltpu.SMEM(pat.shape, jnp.int32)],
        compiler_params=pltpu.CompilerParams(
            collective_id=0, has_side_effects=True, vmem_limit_bytes=40 << 20
        ),
        name="exchange",
    )(*(pltpu.with_memory_space_constraint(x, pltpu.HBM) for x in (mem, pat, *operands)))


def update_kernel(mem, pat, diag, x_row, x_col, y, g, hess, out, grad_out, rows, out_sem):
    r = lax.axis_index("prow")
    c = lax.axis_index("pcol")

    def save(a):
        return pltpu.make_async_copy(rows.at[a], out.at[a], out_sem.at[a])

    def is_pivot(i):
        pivot = i == member(mem, 0)
        for k in range(1, STEPS):
            pivot = jnp.logical_or(pivot, i == member(mem, k))
        return pivot

    def gradient(a, i):
        mine = pl.ds(pl.multiple_of(BS * a, BS), BS)
        part = jnp.zeros((BS, BS), f32)
        for k in range(STEPS):
            hi = x_row[mine, BS * k : BS * k + BS].astype(f32)
            rest = x_row[mine, WIDE + BS * k : WIDE + BS * k + BS].astype(f32)
            part = part + (hi + rest) * y[0:1, BS * k : BS * k + BS]
        val = g[a, pl.ds(r, 1), :] - jnp.sum(part.T, axis=0, keepdims=True)
        for k in range(STEPS):
            val = jnp.where(i == member(mem, k), y[0:1, BS * k : BS * k + BS], val)
        grad_out[pl.ds(a, 1), :] = val

    rr = lax.broadcasted_iota(jnp.int32, (BS, BS), 0)
    cc = lax.broadcasted_iota(jnp.int32, (BS, BS), 1)
    shift = jnp.where(rr == cc, SHIFT, 0.0)

    def two_rows(t):
        at = pl.ds(pl.multiple_of(2 * BS * t, 2 * BS), 2 * BS)
        upd = lax.dot_general(x_row[at, :], x_col[...], NT, preferred_element_type=f32)
        for e in range(2):
            a = 2 * t + e
            i = 8 * a + r
            gradient(a, i)
            live = jnp.where(is_pivot(i), 0.0, 1.0).astype(f32)
            for b in range(8):
                j = 8 * b + c
                keep = live * pat[i, j].astype(f32)
                on = jnp.where(i == j, 1.0, 0.0).astype(f32) * live
                sub = upd[BS * e : BS * e + BS, BS * b : BS * b + BS]
                there = pl.ds(b, BS, stride=8)
                rows[a, there, :] = keep * (hess[a, there, :] - sub) + on * shift
            for k in range(STEPS):
                pk = member(mem, k)

                @pl.when(lax.rem(pk, 8) == c)
                def _():
                    there = pl.ds(pk // 8, BS, stride=8)
                    mine = pl.ds(pl.multiple_of(BS * a, BS), BS)
                    part = slice(BS * k, BS * k + BS)
                    rest = slice(WIDE + BS * k, WIDE + BS * k + BS)

                    @pl.when(i != pk)
                    def _():
                        rows[a, there, :] = x_row[mine, part].astype(f32) + x_row[mine, rest].astype(f32)

                    @pl.when(i == pk)
                    def _():
                        rows[a, there, :] = diag[k]
            save(a).start()

    loop(0, 4, two_rows)
    for a in range(8):
        save(a).wait()


def update(mem, pat, diag, x_row, x_col, y, g, hess):
    return pl.pallas_call(
        update_kernel,
        out_shape=(
            jax.ShapeDtypeStruct(hess.shape, f32),
            jax.ShapeDtypeStruct((8, BS), f32),
        ),
        in_specs=[SM, SM, VM, VM, VM, VM, VM, VM],
        out_specs=(ANY, VM),
        scratch_shapes=[
            pltpu.VMEM((8, 1024, BS), f32),
            pltpu.SemaphoreType.DMA((8,)),
        ],
        compiler_params=pltpu.CompilerParams(vmem_limit_bytes=32 << 20),
        name="update",
    )(mem, pat, diag, x_row, x_col, y, g, hess)


def shards(
    poses, codebook, offsets, confidence, code_ids, creature_ids, hess_raw, pattern, membership
):
    hess = hess_raw.reshape(8, 1024, BS)
    x_row, x_col, diag, y, g = exchange(
        membership, pattern, hess, poses, codebook, offsets,
        confidence.reshape(16, BS), code_ids.reshape(16, BS), creature_ids.reshape(16, BS),
    )
    state, grad = update(membership, pattern, diag, x_row, x_col, y, g, hess)
    return state.reshape(hess_raw.shape), grad.reshape(8, 1, BS)


def solution(mesh):
    return jax.shard_map(
        shards,
        mesh=mesh,
        in_specs=(
            P(("frames", "prow", "pcol"), None),
            P(),
            P(),
            P(("frames", "prow", "pcol")),
            P(("frames", "prow", "pcol")),
            P(("frames", "prow", "pcol")),
            P(None, "prow", None, None, "pcol", None),
            P(),
            P(),
        ),
        out_specs=(P(None, "prow", None, None, "pcol", None), P(None, "prow", None)),
        check_vma=False,
    )
```
